128 devices in a mesh: gx: 16 (over x, z), gy: 8 (over y, core).
Axes of the slice: x: 4, y: 4, z: 4, core: 2. Of those that a mesh axis runs over, the one named last changes fastest.
Arguments:
- guess: float32 [256, 256, 256], P('gx', 'gy'), may hold values from -6 to 6
- right_side: float32 [256, 256, 256], P('gx', 'gy'), may hold values from -6 to 6
- coefficient: float32 [256, 256, 256], P('gx', 'gy'), may hold values from 0.3 to 3
Outputs:
- solution: float32 [256, 256, 256], P('gx', 'gy')
The draws below stay inside these ranges and needn't reach their ends.
All inputs are finite; a program needn't handle non-finite values.
Results may differ from the reference program's by a relative error of at most 0.0001.
Values sent between devices are 32-bit elements; how exact they have to be, the bound alone decides.
A program may use at most 128 MiB of HBM per device.

```python
import math
import jax
import jax.numpy as jnp

LEVELS = 4
SWEEPS = 3
CHEB = 8
NX = 256
NY = 256
NZ = 256


def draw_right_side(key, part):
    result = jnp.clip(jax.random.normal(key, (NX, NY, NZ), jnp.float32), -6.0, 6.0)
    return result


def levels(rng, dims, pieces, smallest, top_value):
    factor_of, own = 1.0, jax.random.fold_in(rng, 6)
    for axis_at, parts in pieces:
        steps = jnp.exp(jax.random.uniform(jax.random.fold_in(own, axis_at), (parts,), jnp.float32, smallest / len(pieces), top_value / len(pieces)))
        factor_of = factor_of * jnp.repeat(steps, dims[axis_at] // parts).reshape([-1 if axis == axis_at else 1 for axis in range(len(dims))])
    return factor_of


def noise(stream_key, shape, width, reach, cuts=(), held_as=jnp.bfloat16):
    gain = levels(stream_key, shape, cuts, -0.22, 0.18) if cuts else 1.0
    drawn = jax.random.normal(stream_key, shape, jnp.float32) * width * gain
    return jnp.minimum(jnp.maximum(drawn, -reach), reach).astype(held_as)


def setup_inputs(seed: int = 0) -> dict:
    arg_keys = jax.random.split(jax.random.key(seed), 4)
    return {
        "guess": noise(arg_keys[0], (NX, NY, NZ), 1.0, 6.0, ((0, 16), (1, 8)), jnp.float32),
        "right_side": draw_right_side(jax.random.fold_in(arg_keys[3], 71), 0),
        "coefficient": jnp.clip(jnp.exp(math.log(3.0) - 2.3025851 * jax.random.uniform(arg_keys[2], (NX, NY, NZ), jnp.float32) ** levels(arg_keys[2], (NX, NY, NZ), ((0, 16), (1, 8)), -0.2, 0.2)), 0.3, 3.0),
    }


RELAX_WEIGHT = 0.7
CHEBY_LOWER = 0.08
CHEBY_UPPER = 2.0


def offset_view(array, direction, offset):
    selector = [slice(1, -1), slice(1, -1), slice(1, -1)]
    selector[direction] = slice(1 + offset, array.shape[direction] - 1 + offset)
    return array[tuple(selector)]


def apply_operator(padded_field, padded_coef, factor):
    center_coef = padded_coef[1:-1, 1:-1, 1:-1]
    center_value = padded_field[1:-1, 1:-1, 1:-1]
    summed = jnp.zeros(center_value.shape, jnp.float32)
    for direction in range(3):
        for offset in (-1, 1):
            near_coef = offset_view(padded_coef, direction, offset)
            near_value = offset_view(padded_field, direction, offset)
            summed = summed + 0.5 * (center_coef + near_coef) * (center_value - near_value)
    return factor * summed


def diagonal_of(padded_coef, factor):
    center_coef = padded_coef[1:-1, 1:-1, 1:-1]
    summed = jnp.zeros(center_coef.shape, jnp.float32)
    for direction in range(3):
        for offset in (-1, 1):
            summed = summed + 0.5 * (center_coef + offset_view(padded_coef, direction, offset))
    return factor * summed


def zero_pad(array):
    return jnp.pad(array, 1)


def smooth(iterate, source, padded_coef, diagonal, factor, pad_field, zero_start):
    for sweep_index in range(SWEEPS):
        if sweep_index == 0 and zero_start:
            iterate = RELAX_WEIGHT * source / diagonal
        else:
            image = apply_operator(pad_field(iterate), padded_coef, factor)
            iterate = iterate + RELAX_WEIGHT * (source - image) / diagonal
    return iterate


def restrict(array):
    extent = array.shape
    blocks = array.reshape(extent[0] // 2, 2, extent[1] // 2, 2, extent[2] // 2, 2)
    return blocks.mean(axis=(1, 3, 5))


def prolong(array):
    return jnp.repeat(jnp.repeat(jnp.repeat(array, 2, 0), 2, 1), 2, 2)


def chebyshev(source, padded_coef, diagonal, factor):
    center_value = (CHEBY_UPPER + CHEBY_LOWER) / 2.0
    half_width = (CHEBY_UPPER - CHEBY_LOWER) / 2.0
    ratio_sigma = center_value / half_width
    weight_old = 1.0 / ratio_sigma
    iterate = jnp.zeros(source.shape, jnp.float32)
    residual = source
    direction_field = residual / diagonal / center_value
    for step_index in range(CHEB):
        iterate = iterate + direction_field
        residual = residual - apply_operator(zero_pad(direction_field), padded_coef, factor)
        weight_new = 1.0 / (2.0 * ratio_sigma - weight_old)
        direction_field = weight_new * weight_old * direction_field + (2.0 * weight_new / half_width) * (residual / diagonal)
        weight_old = weight_new
    return iterate


def reference(guess, right_side, coefficient):
    padded_coef = zero_pad(coefficient)
    diagonal = diagonal_of(padded_coef, 1.0)
    iterate = smooth(guess, right_side, padded_coef, diagonal, 1.0, zero_pad, False)
    entries = [(iterate, right_side, padded_coef, diagonal, 1.0)]
    residual = right_side - apply_operator(zero_pad(iterate), padded_coef, 1.0)
    coarse_coef = coefficient
    for level_index in range(1, LEVELS):
        factor = 0.25 ** level_index
        source = restrict(residual)
        coarse_coef = restrict(coarse_coef)
        padded_coef = zero_pad(coarse_coef)
        diagonal = diagonal_of(padded_coef, factor)
        iterate = smooth(jnp.zeros_like(source), source, padded_coef, diagonal, factor, zero_pad, True)
        residual = source - apply_operator(zero_pad(iterate), padded_coef, factor)
        entries.append((iterate, source, padded_coef, diagonal, factor))
    factor = 0.25 ** LEVELS
    source = restrict(residual)
    coarse_coef = restrict(coarse_coef)
    padded_coef = zero_pad(coarse_coef)
    diagonal = diagonal_of(padded_coef, factor)
    correction = chebyshev(source, padded_coef, diagonal, factor)
    for entry in reversed(entries):
        iterate, source, padded_coef, diagonal, factor = entry
        iterate = iterate + prolong(correction)
        correction = smooth(iterate, source, padded_coef, diagonal, factor, zero_pad, False)
    return correction
```

```python
import functools

import jax
import jax.numpy as jnp
from jax import lax
from jax.experimental import pallas as pl
from jax.experimental.pallas import tpu as pltpu
from jax.sharding import PartitionSpec as P

MESH = pl.DeviceIdType.MESH
F32 = jnp.float32
RELAX = 0.7
CHEB = 8
THETA = 1.04
DELTA = 0.96
LANES = 128


def iota(shape, dim):
    return lax.broadcasted_iota(jnp.int32, shape, dim)


class Level:
    def __init__(self, nh, nz, halo, bx, by, rows, total_x, total_y):
        self.nh, self.nz, self.halo, self.bx, self.by = nh, nz, halo, bx, by
        self.rows, self.total_x, self.total_y = rows, total_x, total_y
        self.width = bx + 2 * halo

    def ext(self):
        return pltpu.VMEM((self.width, self.nh, self.rows, LANES), F32)

    def own(self):
        return pltpu.VMEM((self.bx, self.nh, self.by, LANES), F32)


def z_sum(level, v):
    lane = iota(v[0].shape, 2)
    up = [pltpu.roll(a, 1, 2) for a in v]
    down = [pltpu.roll(a, LANES - 1, 2) for a in v]
    if level.nh == 2:
        low = [jnp.where(lane == 0, 0.0, up[0]), jnp.where(lane == 0, up[0], up[1])]
        high = [
            jnp.where(lane == LANES - 1, down[1], down[0]),
            jnp.where(lane == LANES - 1, 0.0, down[1]),
        ]
    elif level.nz == LANES:
        low = [jnp.where(lane == 0, 0.0, up[0])]
        high = [jnp.where(lane == LANES - 1, 0.0, down[0])]
    else:
        low, high = up, down
    return [a + b for a, b in zip(low, high)]


def block(ref, half, x0, cx, r0, n):
    return ref[pl.ds(x0, cx), half, pl.ds(r0, n), :]


def couple(level, v_ref, c_ref, x0, cx, r0, n):
    halves = range(level.nh)
    v = [block(v_ref, h, x0, cx, r0, n) for h in halves]
    c = [block(c_ref, h, x0, cx, r0, n) for h in halves]
    vz = z_sum(level, v)
    uz = z_sum(level, [a * b for a, b in zip(c, v)])
    out = []
    for h in halves:
        sv, su = vz[h], uz[h]
        for dx, dr in ((-1, 0), (1, 0), (0, -1), (0, 1)):
            near = block(v_ref, h, x0 + dx, cx, r0 + dr, n)
            sv = sv + near
            su = su + near * block(c_ref, h, x0 + dx, cx, r0 + dr, n)
        out.append(c[h] * sv + su)
    return v, out


def loop(count, chunk, body):
    steps = count // chunk
    assert steps * chunk == count
    if steps == 1:
        body(0)
    else:
        lax.fori_loop(0, steps, lambda k, _: (body(k * chunk), 0)[1], 0)


def sweep(level, src, dst, c, g, b, rim, r0, n, chunk, dst_x=0, dst_r=0):
    start = level.halo - rim

    def body(k):
        x0 = start + k
        v, t = couple(level, src, c, x0, chunk, r0, n)
        for h in range(level.nh):
            new = (1.0 - RELAX) * v[h] + block(g, h, x0, chunk, r0, n) * (
                t[h] + block(b, h, x0, chunk, r0, n)
            )
            dst[pl.ds(x0 - dst_x, chunk), h, pl.ds(r0 - dst_r, n), :] = new

    loop(level.bx + 2 * rim, chunk, body)


def first_sweep(level, dst, g, b, rim, r0, n, chunk):
    start = level.halo - rim

    def body(k):
        x0 = start + k
        for h in range(level.nh):
            dst[pl.ds(x0, chunk), h, pl.ds(r0, n), :] = block(g, h, x0, chunk, r0, n) * block(
                b, h, x0, chunk, r0, n
            )

    loop(level.bx + 2 * rim, chunk, body)


def setup(level, c, g, d, rim, r0, n, chunk, base_x, base_y, scale=RELAX):
    start = level.halo - rim

    def body(k):
        x0 = start + k
        halves = range(level.nh)
        mid = [block(c, h, x0, chunk, r0, n) for h in halves]
        cz = z_sum(level, mid)
        shape = mid[0].shape
        px = iota(shape, 0) + (base_x + x0 - level.halo)
        py = iota(shape, 1) + (base_y + r0 - 8)
        mask = (px >= 0) & (px < level.total_x) & (py >= 0) & (py < level.total_y)
        if level.nz < LANES:
            mask = mask & (iota(shape, 2) < level.nz)
        for h in halves:
            total = 6.0 * mid[h] + cz[h]
            for dx, dr in ((-1, 0), (1, 0), (0, -1), (0, 1)):
                total = total + block(c, h, x0 + dx, chunk, r0 + dr, n)
            g[pl.ds(x0, chunk), h, pl.ds(r0, n), :] = jnp.where(
                mask, scale / jnp.where(mask, total, 1.0), 0.0
            )

    loop(level.bx + 2 * rim, chunk, body)

    def diagonal(k):
        halves = range(level.nh)
        x0 = level.halo + k
        mid = [block(c, h, x0, chunk, 8, level.by) for h in halves]
        cz = z_sum(level, mid)
        for h in halves:
            total = 6.0 * mid[h] + cz[h]
            for dx, dr in ((-1, 0), (1, 0), (0, -1), (0, 1)):
                total = total + block(c, h, x0 + dx, chunk, 8 + dr, level.by)
            d[pl.ds(k, chunk), h, :, :] = total

    loop(level.bx, chunk, diagonal)


def residual_pairs(level, v_ref, c, b, d, s, keep, twice=False):
    def body(k):
        x0 = level.halo + 2 * k
        v, t = couple(level, v_ref, c, x0, 2, 8, level.by)
        for h in range(level.nh):
            r = block(b, h, x0, 2, 8, level.by) + t[h] - d[pl.ds(2 * k, 2), h, :, :] * v[h]
            s[pl.ds(k, 1), h, pl.ds(0, level.by), :] = r[0:1] + r[1:2]
            if twice:
                s[pl.ds(k, 1), h, pl.ds(level.by, level.by), :] = r[0:1] + r[1:2]
            if keep is not None:
                keep[pl.ds(x0, 2), h, pl.ds(8, level.by), :] = v[h]

    loop(level.bx // 2, 1, body)


def field_pairs(level, ref, s, twice=False):
    def body(k):
        x0 = level.halo + 2 * k
        for h in range(level.nh):
            r = block(ref, h, x0, 1, 8, level.by) + block(ref, h, x0 + 1, 1, 8, level.by)
            s[pl.ds(k, 1), h, pl.ds(0, level.by), :] = r
            if twice:
                s[pl.ds(k, 1), h, pl.ds(level.by, level.by), :] = r

    loop(level.bx // 2, 1, body)


def dot(a, m):
    return jnp.dot(a, m, precision=lax.Precision.HIGHEST, preferred_element_type=F32)


def halve(level, s, weight, rows=None, lane_base=0):
    rows = level.by // 2 if rows is None else rows
    count = level.bx // 2
    row, col = iota((LANES, LANES), 0), iota((LANES, LANES), 1)
    total = None
    for h in range(level.nh):
        pick = (lax.shift_right_logical(row, 1) + (lane_base + h * 64) == col) & (row < level.nz)
        m = jnp.where(pick, weight, 0.0).astype(F32)
        a = s[:, h, pl.ds(0, rows, stride=2), :] + s[:, h, pl.ds(1, rows, stride=2), :]
        part = dot(a.reshape(count * rows, LANES), m)
        total = part if total is None else total + part
    return total.reshape(count, rows, LANES)


def prolong(level, e, ex, er, count, ne, pe, base, dst, x0):
    row, col = iota((LANES, LANES), 0), iota((LANES, LANES), 1)
    coarse = e[pl.ds(ex, count), 0, pl.ds(er, ne), :].reshape(count * ne, LANES)
    for h in range(level.nh):
        m = jnp.where(row == lax.shift_right_logical(col, 1) + h * 64, 1.0, 0.0).astype(F32)
        pe[:, h, :, :] = dot(coarse, m).reshape(count, ne, LANES)


def add_prolonged(level, pe, base, dst, x0, r0, count, ne):
    def body(k):
        for h in range(level.nh):
            fine = pe[k, h, :, :]
            for dx in range(2):
                for dr in range(2):
                    at = (x0 + 2 * k + dx, h, pl.ds(r0 + dr, ne, stride=2), slice(None))
                    dst[at] = base[at] + fine

    loop(count, 1, body)


class Copy:
    def __init__(self, src, dst, target, sends, receives, sems):
        send_sem, recv_sem, index = sems
        self.copy = pltpu.make_async_remote_copy(
            src_ref=src,
            dst_ref=dst,
            send_sem=send_sem.at[index],
            recv_sem=recv_sem.at[index],
            device_id=target,
            device_id_type=MESH,
        )
        self.sends, self.receives = sends, receives

    def start(self):
        pl.when(self.sends)(lambda: self.copy.start())

    def arrive(self):
        pl.when(self.receives)(lambda: self.copy.wait_recv())

    def leave(self):
        pl.when(self.sends)(lambda: self.copy.wait_send())


def kernel(nx, ny, levels, guess, rhs, coef, out, *scratch):
    l0, l1, l2, l3, l4 = levels
    names = iter(scratch)
    take = lambda k: [next(names) for _ in range(k)]
    va0, vb0, vc0, c0, b0, g0, d0, s0, o0, pe0 = take(10)
    va1, vb1, vc1, c1, b1, g1, d1, s1, pe1 = take(9)
    va2, vb2, vc2, c2, b2, g2, d2, s2, pe2 = take(9)
    va3, vb3, c3, b3, g3, d3, s3, pe3 = take(8)
    va4, vb4, c4, q4, d4, res4, e4 = take(7)
    pc, pb, fc, fb = take(4)
    send_sem, recv_sem, gather_send, gather_recv, local_sem = take(5)

    gx, gy = lax.axis_index("gx"), lax.axis_index("gy")
    counter = iter(range(1000))

    def sems():
        return send_sem, recv_sem, next(counter)

    loads = []
    for i, (src, dst) in enumerate(((coef, c0), (guess, va0), (rhs, b0))):
        for h in range(2):
            loads.append(
                pltpu.make_async_copy(
                    src.at[:, :, h * LANES : (h + 1) * LANES],
                    dst.at[l0.halo : l0.halo + l0.bx, h, 8 : 8 + l0.by, :],
                    local_sem.at[2 * i + h],
                )
            )
    for copy in loads:
        copy.start()

    barrier = pltpu.get_barrier_semaphore()
    for k in range(1, nx):
        pl.semaphore_signal(
            barrier, inc=1, device_id=(lax.rem(gx + k, nx), gy), device_id_type=MESH
        )
    for k in range(1, ny):
        pl.semaphore_signal(
            barrier, inc=1, device_id=(gx, lax.rem(gy + k, ny)), device_id_type=MESH
        )

    everything = []

    class Exchange:
        def __init__(self, level, ref, wide, reach=1, faces=True):
            lo, bx, by = level.halo, level.bx, level.by
            if reach == 1:
                up = ((lo + bx - wide, lo - wide), (lo, lo + bx))
            else:
                up = ((lo + 2 * bx - lo, 0), (lo, lo + 2 * bx))
            self.x, self.y, self.corners = [], [], []
            own = pl.ds(8, by)
            for sign, (src, dst) in zip((1, -1), up):
                there, back = gx + sign * reach, gx - sign * reach
                ok = lambda p: (p >= 0) & (p < nx)
                self.x.append(
                    Copy(
                        ref.at[pl.ds(src, wide), :, own, :],
                        ref.at[pl.ds(dst, wide), :, own, :],
                        (there, gy),
                        ok(there),
                        ok(back),
                        sems(),
                    )
                )
            sides = ((1, by, 0), (-1, 8, 8 + by))
            for sign, src, dst in sides:
                there, back = gy + sign, gy - sign
                ok_y = lambda p: (p >= 0) & (p < ny)
                spans = [(lo, bx, None)] if faces else []
                spans += [(up[0][1], wide, gx - reach >= 0), (up[1][1], wide, gx + reach < nx)]
                for start, count, also in spans:
                    sends, receives = ok_y(there), ok_y(back)
                    if also is not None:
                        sends, receives = sends & also, receives & also
                    (self.y if also is None else self.corners).append(
                        Copy(
                            ref.at[pl.ds(start, count), :, pl.ds(src, 8), :],
                            ref.at[pl.ds(start, count), :, pl.ds(dst, 8), :],
                            (gx, there),
                            sends,
                            receives,
                            sems(),
                        )
                    )
            everything.append(self)

        def send(self):
            for copy in self.x + self.y:
                copy.start()

        def forward(self):
            for copy in self.x:
                copy.arrive()
            for copy in self.corners:
                copy.start()

        def finish(self):
            for copy in self.y + self.corners:
                copy.arrive()

        def leave(self):
            everything.remove(self)
            for copy in self.x + self.y + self.corners:
                copy.leave()

    class Gather:
        def __init__(self, rows, full, index):
            self.rows, self.full = rows, full
            self.first, self.second = [], []
            for k in range(1, ny):
                self.first.append(
                    pltpu.make_async_remote_copy(
                        src_ref=rows.at[gy],
                        dst_ref=rows.at[gy],
                        send_sem=gather_send.at[index, k],
                        recv_sem=gather_recv.at[index, k],
                        device_id=(gx, lax.rem(gy + k, ny)),
                        device_id_type=MESH,
                    )
                )
            mine = full.at[pl.ds(2 * gx, 2)]
            for k in range(1, nx):
                self.second.append(
                    pltpu.make_async_remote_copy(
                        src_ref=mine,
                        dst_ref=mine,
                        send_sem=gather_send.at[index, ny + k],
                        recv_sem=gather_recv.at[index, ny + k],
                        device_id=(lax.rem(gx + k, nx), gy),
                        device_id_type=MESH,
                    )
                )

        def send(self, tile):
            self.rows[gy] = tile
            for copy in self.first:
                copy.start()

        def forward(self):
            for copy in self.first:
                copy.wait_recv()
            total = self.rows[0]
            for k in range(1, ny):
                total = total + self.rows[k]
            self.full[pl.ds(2 * gx, 2)] = total
            for copy in self.second:
                copy.start()

        def finish(self):
            for copy in self.second:
                copy.wait_recv()

        def leave(self):
            for copy in self.first + self.second:
                copy.wait_send()

    x_v0, x_c0, x_b0 = Exchange(l0, va0, 4), Exchange(l0, c0, 4), Exchange(l0, b0, 3)
    x_k0 = Exchange(l0, vc0, 3)
    x_c1, x_b1, x_k1 = Exchange(l1, c1, 5), Exchange(l1, b1, 4), Exchange(l1, vc1, 5)
    x_c2, x_b2, x_k2 = (Exchange(l2, ref, 4) for ref in (c2, b2, vc2))
    f_c2, f_b2, f_k2 = (Exchange(l2, ref, 2, 2, False) for ref in (c2, b2, vc2))
    g_c3, g_b3 = Gather(pc, fc, 0), Gather(pb, fb, 1)

    for copy in loads:
        copy.wait()
    pl.semaphore_wait(barrier, nx + ny - 2)

    x_c0.send()
    x_v0.send()

    def double(k):
        for h in range(2):
            own = (pl.ds(l0.halo + k, 1), h, pl.ds(8, l0.by), slice(None))
            b0[own] = 2.0 * b0[own]

    loop(l0.bx, 1, double)
    x_b0.send()

    def clear(level, refs, far):
        lo, bx, by = level.halo, level.bx, level.by

        def layers(start, count):
            for ref in refs:
                ref[pl.ds(start, count)] = jnp.zeros((count,) + ref.shape[1:], F32)

        near = min(lo, bx)
        pl.when(gx == 0)(lambda: layers(lo - near, near))
        pl.when(gx == nx - 1)(lambda: layers(lo + bx, near))
        if far:
            pl.when(gx < 2)(lambda: layers(0, lo - bx))
            pl.when(gx >= nx - 2)(lambda: layers(lo + 2 * bx, lo - bx))

        def rows(start, count):
            for ref in refs:
                for h in range(level.nh):
                    ref[:, h, pl.ds(start, count), :] = jnp.zeros((level.width, count, LANES), F32)

        pl.when(gy == 0)(lambda: rows(0, 8))
        pl.when(gy == ny - 1)(lambda: rows(8 + by, 8))

    clear(l0, (va0, c0, b0, vc0), False)
    clear(l1, (c1, b1, vc1), False)
    clear(l2, (c2, b2, vc2), True)
    for ref in (vb0, va1, vb1, va2, vb2, va3, vb3, c3, va4, vb4, c4):
        for h in range(ref.shape[1]):
            for r in range(0, ref.shape[2], 8):
                ref[:, h, pl.ds(r, 8), :] = jnp.zeros((ref.shape[0], 8, LANES), F32)

    lane_base = 32 * lax.shift_right_logical(gy, 1)
    odd_rows = iota((2, 8, LANES), 1) >= 4
    mine = odd_rows == ((gy & 1) == 1)

    def tile_of(value):
        return jnp.where(mine, value, 0.0)

    field_pairs(l0, c0, s0)
    c1[l1.halo : l1.halo + l1.bx, 0, 8 : 8 + l1.by, :] = halve(l0, s0, 0.125)
    x_c1.send()
    field_pairs(l1, c1, s1)
    c2[l2.halo : l2.halo + l2.bx, 0, 8 : 8 + l2.by, :] = halve(l1, s1, 0.125)
    x_c2.send()
    f_c2.send()
    field_pairs(l2, c2, s2, True)
    g_c3.send(tile_of(halve(l2, s2, 0.125, 8, lane_base)))

    for exchange in (x_c0, x_v0, x_b0):
        exchange.forward()
    for exchange in (x_c0, x_v0, x_b0):
        exchange.finish()
    bx0, by0 = gx * l0.bx, gy * l0.by

    setup(l0, c0, g0, d0, 3, 4, 40, 1, bx0, by0)
    sweep(l0, va0, vb0, c0, g0, b0, 3, 4, 40, 1)
    x_v0.leave()
    sweep(l0, vb0, va0, c0, g0, b0, 2, 4, 40, 1)
    sweep(l0, va0, vb0, c0, g0, b0, 1, 4, 40, 1)
    residual_pairs(l0, vb0, c0, b0, d0, s0, vc0)
    b1[l1.halo : l1.halo + l1.bx, 0, 8 : 8 + l1.by, :] = halve(l0, s0, 0.5)
    x_b1.send()
    x_k0.send()
    for exchange in (x_c1, x_c2, f_c2):
        exchange.forward()
    g_c3.forward()
    for exchange in (x_c1, x_c2, f_c2):
        exchange.finish()
    setup(l1, c1, g1, d1, 4, 4, 24, 2, gx * l1.bx, gy * l1.by)
    setup(l2, c2, g2, d2, 5, 2, 24, 2, gx * l2.bx, gy * l2.by)
    x_b1.forward()
    x_b1.finish()
    first_sweep(l1, va1, g1, b1, 3, 4, 24, 2)
    sweep(l1, va1, vb1, c1, g1, b1, 2, 4, 24, 2)
    sweep(l1, vb1, va1, c1, g1, b1, 1, 4, 24, 2)
    residual_pairs(l1, va1, c1, b1, d1, s1, vc1)
    b2[l2.halo : l2.halo + l2.bx, 0, 8 : 8 + l2.by, :] = halve(l1, s1, 0.5)
    x_b2.send()
    f_b2.send()
    x_k1.send()

    def unpack(packed, dst):
        def body(k):
            t = packed[pl.ds(k, 4)]
            lane = iota(t.shape, 2)
            for q in range(l3.total_y // 8):
                part = t if q == 0 else pltpu.roll(t, LANES - 32 * q, 2)
                dst[pl.ds(l3.halo + k, 4), 0, pl.ds(8 + 8 * q, 8), :] = jnp.where(
                    lane < 32, part, 0.0
                )

        loop(l3.bx, 4, body)

    g_c3.finish()
    unpack(fc, c3)
    setup(l3, c3, g3, d3, 0, 8, l3.by, 2, 0, 0)
    field_pairs(l3, c3, s3)
    c4[l4.halo : l4.halo + l4.bx, 0, 8 : 8 + l4.by, :] = halve(l3, s3, 0.125)
    setup(l4, c4, q4, d4, 0, 8, l4.by, 2, 0, 0, 1.0)

    x_b2.forward()
    x_b2.finish()
    first_sweep(l2, va2, g2, b2, 3, 2, 24, 2)
    sweep(l2, va2, vb2, c2, g2, b2, 2, 2, 24, 2)
    sweep(l2, vb2, va2, c2, g2, b2, 1, 2, 24, 2)
    residual_pairs(l2, va2, c2, b2, d2, s2, vc2, True)
    g_b3.send(tile_of(halve(l2, s2, 0.5, 8, lane_base)))
    x_k2.send()
    f_k2.send()
    x_k0.forward()
    x_k1.forward()
    f_b2.forward()
    g_b3.forward()
    x_k2.forward()
    f_k2.forward()
    g_b3.finish()
    unpack(fb, b3)

    first_sweep(l3, va3, g3, b3, 0, 8, l3.by, 2)
    sweep(l3, va3, vb3, c3, g3, b3, 0, 8, l3.by, 2)
    sweep(l3, vb3, va3, c3, g3, b3, 0, 8, l3.by, 2)
    residual_pairs(l3, va3, c3, b3, d3, s3, None)

    res4[:, 0, :, :] = halve(l3, s3, 0.5)
    sigma = THETA / DELTA
    rho = 1.0 / sigma
    inner = (pl.ds(l4.halo, l4.bx), 0, pl.ds(8, l4.by), slice(None))
    q = q4[inner]
    direction = res4[:, 0, :, :] * q * (1.0 / THETA)
    e4[:, 0, :, :] = direction
    va4[inner] = direction
    src, dst = va4, vb4
    for step in range(CHEB - 1):
        v, t = couple(l4, src, c4, l4.halo, l4.bx, 8, l4.by)
        r = res4[:, 0, :, :] - (d4[:, 0, :, :] * v[0] - t[0])
        rho_new = 1.0 / (2.0 * sigma - rho)
        direction = (rho_new * rho) * v[0] + (2.0 * rho_new / DELTA) * (r * q4[inner])
        rho = rho_new
        res4[:, 0, :, :] = r
        e4[:, 0, :, :] = e4[:, 0, :, :] + direction
        dst[inner] = direction
        src, dst = dst, src

    prolong(l3, e4, 0, 0, l4.bx, l4.by, pe3, None, None, 0)
    add_prolonged(l3, pe3, va3, vb3, l3.halo, 8, l4.bx, l4.by)
    sweep(l3, vb3, va3, c3, g3, b3, 0, 8, l3.by, 2)
    sweep(l3, va3, vb3, c3, g3, b3, 0, 8, l3.by, 2)
    sweep(l3, vb3, va3, c3, g3, b3, 0, 8, l3.by, 2)

    f_b2.finish()
    x_k2.finish()
    f_k2.finish()
    prolong(l2, va3, 2 * gx + 1, 4 * gy + 4, 8, 16, pe2, None, None, 0)
    add_prolonged(l2, pe2, vc2, va2, 0, 0, 8, 16)
    sweep(l2, va2, vb2, c2, g2, b2, 5, 2, 24, 2)
    sweep(l2, vb2, va2, c2, g2, b2, 4, 2, 24, 2)
    sweep(l2, va2, vb2, c2, g2, b2, 3, 2, 24, 2)

    x_k1.finish()
    prolong(l1, vb2, 3, 4, 10, 16, pe1, None, None, 0)
    add_prolonged(l1, pe1, vc1, va1, 0, 0, 10, 16)
    sweep(l1, va1, vb1, c1, g1, b1, 4, 4, 24, 2)
    sweep(l1, vb1, va1, c1, g1, b1, 3, 4, 24, 2)
    sweep(l1, va1, vb1, c1, g1, b1, 2, 4, 24, 2)

    x_k0.finish()
    prolong(l0, vb1, 4, 4, 12, 24, pe0, None, None, 0)
    add_prolonged(l0, pe0, vc0, va0, 0, 0, 12, 24)
    sweep(l0, va0, vb0, c0, g0, b0, 2, 4, 40, 1)
    sweep(l0, vb0, va0, c0, g0, b0, 1, 4, 40, 1)
    sweep(l0, va0, o0, c0, g0, b0, 0, 8, 32, 1, l0.halo, 8)
    stores = []
    for h in range(2):
        stores.append(
            pltpu.make_async_copy(
                o0.at[:, h], out.at[:, :, h * LANES : (h + 1) * LANES], local_sem.at[6 + h]
            )
        )
    for copy in stores:
        copy.start()
    for copy in stores:
        copy.wait()
    for exchange in list(everything):
        exchange.leave()
    g_c3.leave()
    g_b3.leave()


def solution(mesh):
    nx, ny = mesh.shape["gx"], mesh.shape["gy"]
    l0 = Level(2, 256, 4, 16, 32, 48, 16 * nx, 32 * ny)
    l1 = Level(1, 128, 6, 8, 16, 32, 8 * nx, 16 * ny)
    l2 = Level(1, 64, 6, 4, 8, 32, 4 * nx, 8 * ny)
    l3 = Level(1, 32, 4, 2 * nx, 4 * ny, 16 + 4 * ny, 2 * nx, 4 * ny)
    l4 = Level(1, 16, 1, nx, 2 * ny, 16 + 2 * ny, nx, 2 * ny)

    def vmem(*shape):
        return pltpu.VMEM(shape, F32)

    e, o = (lambda l: l.ext()), (lambda l: l.own())
    scratch = [e(l0)] * 6 + [o(l0), vmem(8, 2, 32, LANES), o(l0), vmem(12, 2, 24, LANES)]
    scratch += [e(l1)] * 6 + [o(l1), vmem(4, 1, 16, LANES), vmem(10, 1, 16, LANES)]
    scratch += [e(l2)] * 6 + [o(l2), vmem(2, 1, 16, LANES), vmem(8, 1, 16, LANES)]
    scratch += [e(l3)] * 5 + [o(l3), vmem(nx, 1, 4 * ny, LANES), vmem(nx, 1, 2 * ny, LANES)]
    scratch += [e(l4)] * 4 + [o(l4)] * 3
    scratch += [vmem(ny, 2, 8, LANES)] * 2 + [vmem(2 * nx, 8, LANES)] * 2
    copies = 10 * 8 + 3 * 6
    scratch += [
        pltpu.SemaphoreType.DMA((copies,)),
        pltpu.SemaphoreType.DMA((copies,)),
        pltpu.SemaphoreType.DMA((2, nx + ny)),
        pltpu.SemaphoreType.DMA((2, nx + ny)),
        pltpu.SemaphoreType.DMA((8,)),
    ]

    def step(guess, right_side, coefficient):
        return pl.pallas_call(
            functools.partial(kernel, nx, ny, (l0, l1, l2, l3, l4)),
            out_shape=jax.ShapeDtypeStruct(guess.shape, F32),
            in_specs=[pl.BlockSpec(memory_space=pl.ANY)] * 3,
            out_specs=pl.BlockSpec(memory_space=pl.ANY),
            scratch_shapes=scratch,
            compiler_params=pltpu.CompilerParams(collective_id=0, has_side_effects=True),
        )(guess, right_side, coefficient)

    spec = P("gx", "gy", None)
    return jax.shard_map(
        step, mesh=mesh, in_specs=(spec, spec, spec), out_specs=spec, check_vma=False
    )
```

```python
import functools

import jax
import jax.numpy as jnp
from jax import lax
from jax.experimental import pallas as pl
from jax.experimental.pallas import tpu as pltpu
from jax.sharding import PartitionSpec as P

MESH = pl.DeviceIdType.MESH
F32 = jnp.float32
RELAX = 0.7
CHEB = 8
THETA = 1.04
DELTA = 0.96
LANES = 128


def iota(shape, dim):
    return lax.broadcasted_iota(jnp.int32, shape, dim)


class Level:
    def __init__(self, nh, nz, halo, bx, by, rows, total_x, total_y):
        self.nh, self.nz, self.halo, self.bx, self.by = nh, nz, halo, bx, by
        self.rows, self.total_x, self.total_y = rows, total_x, total_y
        self.width = bx + 2 * halo

    def ext(self):
        return pltpu.VMEM((self.width, self.nh, self.rows, LANES), F32)

    def own(self):
        return pltpu.VMEM((self.bx, self.nh, self.by, LANES), F32)


def z_sum(level, v):
    lane = iota(v[0].shape, 2)
    up = [pltpu.roll(a, 1, 2) for a in v]
    down = [pltpu.roll(a, LANES - 1, 2) for a in v]
    if level.nh == 2:
        low = [jnp.where(lane == 0, 0.0, up[0]), jnp.where(lane == 0, up[0], up[1])]
        high = [
            jnp.where(lane == LANES - 1, down[1], down[0]),
            jnp.where(lane == LANES - 1, 0.0, down[1]),
        ]
    elif level.nz == LANES:
        low = [jnp.where(lane == 0, 0.0, up[0])]
        high = [jnp.where(lane == LANES - 1, 0.0, down[0])]
    else:
        low, high = up, down
    return [a + b for a, b in zip(low, high)]


def block(ref, half, x0, cx, r0, n):
    return ref[pl.ds(x0, cx), half, pl.ds(r0, n), :]


def couple(level, v_ref, c_ref, x0, cx, r0, n):
    halves = range(level.nh)
    v = [block(v_ref, h, x0, cx, r0, n) for h in halves]
    c = [block(c_ref, h, x0, cx, r0, n) for h in halves]
    vz = z_sum(level, v)
    uz = z_sum(level, [a * b for a, b in zip(c, v)])
    out = []
    for h in halves:
        sv, su = vz[h], uz[h]
        for dx, dr in ((-1, 0), (1, 0), (0, -1), (0, 1)):
            near = block(v_ref, h, x0 + dx, cx, r0 + dr, n)
            sv = sv + near
            su = su + near * block(c_ref, h, x0 + dx, cx, r0 + dr, n)
        out.append(c[h] * sv + su)
    return v, out


def pieces(x0, count, r0, n):
    return [(x0 + i, r0 + r) for i in range(count) for r in range(0, n, 8)]


def loop(count, chunk, body):
    steps = count // chunk
    assert steps * chunk == count
    if steps == 1:
        body(0)
    else:
        lax.fori_loop(0, steps, lambda k, _: (body(k * chunk), 0)[1], 0)


def sweep(level, src, dst, c, g, b, rim, r0, n, chunk, dst_x=0, dst_r=0):
    start = level.halo - rim
    chunk = chunk or (level.bx + 2 * rim) // 2

    def body(k):
        for x0, r in pieces(start + k, chunk, r0, n):
            v, t = couple(level, src, c, x0, 1, r, 8)
            for h in range(level.nh):
                new = (1.0 - RELAX) * v[h] + block(g, h, x0, 1, r, 8) * (
                    t[h] + block(b, h, x0, 1, r, 8)
                )
                dst[pl.ds(x0 - dst_x, 1), h, pl.ds(r - dst_r, 8), :] = new

    loop(level.bx + 2 * rim, chunk, body)


def first_sweep(level, dst, g, b, rim, r0, n, chunk):
    start = level.halo - rim
    chunk = chunk or (level.bx + 2 * rim) // 2

    def body(k):
        x0 = start + k
        for h in range(level.nh):
            dst[pl.ds(x0, chunk), h, pl.ds(r0, n), :] = block(g, h, x0, chunk, r0, n) * block(
                b, h, x0, chunk, r0, n
            )

    loop(level.bx + 2 * rim, chunk, body)


def setup(level, c, g, d, rim, r0, n, chunk, base_x, base_y, scale=RELAX):
    start = level.halo - rim

    def body(k):
        halves = range(level.nh)
        for x0, r in pieces(start + k, chunk, r0, n):
            mid = [block(c, h, x0, 1, r, 8) for h in halves]
            cz = z_sum(level, mid)
            shape = mid[0].shape
            px = base_x + x0 - level.halo
            py = iota(shape, 1) + jnp.where((px >= 0) & (px < level.total_x), base_y + r - 8, -1000)
            mask = (py >= 0) & (py < level.total_y)
            if level.nz < LANES:
                mask = mask & (iota(shape, 2) < level.nz)
            for h in halves:
                total = 6.0 * mid[h] + cz[h]
                for dx, dr in ((-1, 0), (1, 0), (0, -1), (0, 1)):
                    total = total + block(c, h, x0 + dx, 1, r + dr, 8)
                g[pl.ds(x0, 1), h, pl.ds(r, 8), :] = jnp.where(
                    mask, scale / jnp.where(mask, total, 1.0), 0.0
                )

    loop(level.bx + 2 * rim, chunk, body)

    def diagonal(k):
        halves = range(level.nh)
        for x0, r in pieces(level.halo + k, chunk, 8, level.by):
            mid = [block(c, h, x0, 1, r, 8) for h in halves]
            cz = z_sum(level, mid)
            for h in halves:
                total = 6.0 * mid[h] + cz[h]
                for dx, dr in ((-1, 0), (1, 0), (0, -1), (0, 1)):
                    total = total + block(c, h, x0 + dx, 1, r + dr, 8)
                d[pl.ds(x0 - level.halo, 1), h, pl.ds(r - 8, 8), :] = total

    loop(level.bx, chunk, diagonal)


def residual_pairs(level, v_ref, c, b, d, s, keep):
    def body(k):
        for r in range(0, level.by, 8):
            parts = []
            for dx in range(2):
                x0 = level.halo + 2 * k + dx
                v, t = couple(level, v_ref, c, x0, 1, 8 + r, 8)
                for h in range(level.nh):
                    own = d[pl.ds(2 * k + dx, 1), h, pl.ds(r, 8), :]
                    parts.append(block(b, h, x0, 1, 8 + r, 8) + t[h] - own * v[h])
                    if keep is not None:
                        keep[pl.ds(x0, 1), h, pl.ds(8 + r, 8), :] = v[h]
            for h in range(level.nh):
                total = parts[h] + parts[level.nh + h]
                s[pl.ds(k, 1), h, pl.ds(r, 8), :] = total

    loop(level.bx // 2, 1, body)


def field_pairs(level, ref, s):
    def body(k):
        x0 = level.halo + 2 * k
        for h in range(level.nh):
            r = block(ref, h, x0, 1, 8, level.by) + block(ref, h, x0 + 1, 1, 8, level.by)
            s[pl.ds(k, 1), h, pl.ds(0, level.by), :] = r

    loop(level.bx // 2, 1, body)


def dot(a, m):
    return jnp.dot(a, m, precision=lax.Precision.HIGHEST, preferred_element_type=F32)


def halve(level, s, weight):
    rows = level.by // 2
    count = level.bx // 2
    row, col = iota((LANES, LANES), 0), iota((LANES, LANES), 1)
    total = None
    for h in range(level.nh):
        pick = (lax.shift_right_logical(row, 1) + h * 64 == col) & (row < level.nz)
        m = jnp.where(pick, weight, 0.0).astype(F32)
        a = s[:, h, pl.ds(0, rows, stride=2), :] + s[:, h, pl.ds(1, rows, stride=2), :]
        part = dot(a.reshape(count * rows, LANES), m)
        total = part if total is None else total + part
    return total.reshape(count, rows, LANES)


def prolong(level, e, ex, er, count, ne, pe, base, dst, x0):
    row, col = iota((LANES, LANES), 0), iota((LANES, LANES), 1)
    coarse = e[pl.ds(ex, count), 0, pl.ds(er, ne), :].reshape(count * ne, LANES)
    for h in range(level.nh):
        m = jnp.where(row == lax.shift_right_logical(col, 1) + h * 64, 1.0, 0.0).astype(F32)
        pe[:, h, :, :] = dot(coarse, m).reshape(count, ne, LANES)


def add_prolonged(level, pe, base, dst, x0, r0, count, ne, er=0):
    def body(k):
        for h in range(level.nh):
            fine = pe[k, h, pl.ds(er, ne), :]
            for dx in range(2):
                for dr in range(2):
                    at = (x0 + 2 * k + dx, h, pl.ds(r0 + dr, ne, stride=2), slice(None))
                    dst[at] = base[at] + fine

    loop(count, 1, body)


class Packed:
    def __init__(self, count, pad, rows, width, groups):
        self.count, self.pad, self.rows, self.width, self.groups = count, pad, rows, width, groups

    def ext(self):
        return pltpu.VMEM((self.count + 2 * self.pad, 8, LANES), F32)

    def own(self, more=0):
        return pltpu.VMEM((self.count + more, 8, LANES), F32)


def packed_near(p, v):
    row = iota(v.shape, 1) & (p.rows - 1)
    after, before = pltpu.roll(v, 7, 1), pltpu.roll(v, 1, 1)
    return (
        jnp.where(row == p.rows - 1, pltpu.roll(after, LANES - p.width, 2), after),
        jnp.where(row == 0, pltpu.roll(before, p.width, 2), before),
        pltpu.roll(v, LANES - 1, 2),
        pltpu.roll(v, 1, 2),
    )


def packed_setup(p, c, w, wx, g, d, scale):
    def body(k):
        at = pl.ds(p.pad + k, 1)
        mid = c[at]
        lane, row = iota(mid.shape, 2), iota(mid.shape, 1) & (p.rows - 1)
        valid = lane < p.width * p.groups
        z = lane & (p.width - 1)
        inside = (
            (row < p.rows - 1) | (lane < p.width * (p.groups - 1)),
            (row > 0) | (lane >= p.width),
            z < p.width - 1,
            z > 0,
        )
        below = c[pl.ds(p.pad + k - 1, 1)]
        total = 6.0 * mid + below + c[pl.ds(p.pad + k + 1, 1)]
        wx[pl.ds(k, 1)] = mid + below
        for ref, near, ok in zip(w, packed_near(p, mid), inside):
            near = jnp.where(valid & ok, near, 0.0)
            ref[pl.ds(k, 1)] = jnp.where(valid & ok, mid + near, 0.0)
            total = total + near
        g[pl.ds(k, 1)] = jnp.where(valid, scale / jnp.where(valid, total, 1.0), 0.0)
        d[pl.ds(k, 1)] = total

    loop_pieces(p.count, 4, body)
    wx[pl.ds(p.count, 1)] = c[pl.ds(p.pad + p.count - 1, 1)]


def packed_couple(p, v_ref, w, wx, k):
    v = v_ref[pl.ds(p.pad + k, 1)]
    t = wx[pl.ds(k, 1)] * v_ref[pl.ds(p.pad + k - 1, 1)]
    t = t + wx[pl.ds(k + 1, 1)] * v_ref[pl.ds(p.pad + k + 1, 1)]
    parts = [ref[pl.ds(k, 1)] * near for ref, near in zip(w, packed_near(p, v))]
    return v, t + ((parts[0] + parts[1]) + (parts[2] + parts[3]))


def loop_pieces(count, chunk, body):
    def several(k):
        for i in range(chunk):
            body(k + i)

    loop(count, chunk, several)


def packed_sweep(p, src, dst, w, wx, g, b, b_pad):
    def body(k):
        v, t = packed_couple(p, src, w, wx, k)
        new = (1.0 - RELAX) * v + g[pl.ds(k, 1)] * (t + b[pl.ds(b_pad + k, 1)])
        dst[pl.ds(p.pad + k, 1)] = new

    loop_pieces(p.count, 16, body)


def packed_halve(s, weight):
    row, col = iota((LANES, LANES), 0), iota((LANES, LANES), 1)
    m = jnp.where(lax.shift_right_logical(row, 1) == col, weight, 0.0).astype(F32)
    a = s[:, pl.ds(0, 8, stride=2), :] + s[:, pl.ds(1, 8, stride=2), :]
    return dot(a.reshape(s.shape[0] * 8, LANES), m).reshape(s.shape[0], 8, LANES)


class Copy:
    def __init__(self, src, dst, target, sends, receives, sems):
        send_sem, recv_sem, index = sems
        self.copy = pltpu.make_async_remote_copy(
            src_ref=src,
            dst_ref=dst,
            send_sem=send_sem.at[index],
            recv_sem=recv_sem.at[index],
            device_id=target,
            device_id_type=MESH,
        )
        self.sends, self.receives = sends, receives

    def start(self):
        pl.when(self.sends)(lambda: self.copy.start())

    def arrive(self):
        pl.when(self.receives)(lambda: self.copy.wait_recv())

    def leave(self):
        pl.when(self.sends)(lambda: self.copy.wait_send())


def kernel(nx, ny, levels, guess, rhs, coef, out, *scratch):
    l0, l1, l2, l3, l4 = levels
    names = iter(scratch)
    take = lambda k: [next(names) for _ in range(k)]
    va0, vb0, vc0, c0, b0, g0, d0, s0, o0, pe0 = take(10)
    va1, vb1, vc1, c1, b1, g1, d1, s1, pe1 = take(9)
    va2, vb2, vc2, c2, b2, g2, d2, s2, pe2 = take(9)
    va3, vb3, c3, b3, wx3, g3, d3, s3, t3 = take(9)
    w3 = take(4)
    va4, vb4, c4, wx4, q4, d4, res4, e4 = take(8)
    w4 = take(4)
    pc, pb = take(2)
    send_sem, recv_sem, gather_send, gather_recv, local_sem = take(5)

    gx, gy = lax.axis_index("gx"), lax.axis_index("gy")
    counter = iter(range(1000))

    def sems():
        return send_sem, recv_sem, next(counter)

    loads = []
    for i, (src, dst) in enumerate(((coef, c0), (guess, va0), (rhs, b0))):
        for h in range(2):
            loads.append(
                pltpu.make_async_copy(
                    src.at[:, :, h * LANES : (h + 1) * LANES],
                    dst.at[l0.halo : l0.halo + l0.bx, h, 8 : 8 + l0.by, :],
                    local_sem.at[2 * i + h],
                )
            )
    for copy in loads:
        copy.start()

    barrier = pltpu.get_barrier_semaphore()
    for k in range(1, nx):
        pl.semaphore_signal(
            barrier, inc=1, device_id=(lax.rem(gx + k, nx), gy), device_id_type=MESH
        )
    for k in range(1, ny):
        pl.semaphore_signal(
            barrier, inc=1, device_id=(gx, lax.rem(gy + k, ny)), device_id_type=MESH
        )

    everything = []

    class Exchange:
        def __init__(self, level, ref, wide, reach=1, faces=True):
            lo, bx, by = level.halo, level.bx, level.by
            if reach == 1:
                up = ((lo + bx - wide, lo - wide), (lo, lo + bx))
            else:
                up = ((lo + 2 * bx - lo, 0), (lo, lo + 2 * bx))
            self.x, self.y, self.corners = [], [], []
            own = pl.ds(8, by)
            for sign, (src, dst) in zip((1, -1), up):
                there, back = gx + sign * reach, gx - sign * reach
                ok = lambda p: (p >= 0) & (p < nx)
                self.x.append(
                    Copy(
                        ref.at[pl.ds(src, wide), :, own, :],
                        ref.at[pl.ds(dst, wide), :, own, :],
                        (there, gy),
                        ok(there),
                        ok(back),
                        sems(),
                    )
                )
            rows = 4 if level.nh == 2 else 8
            sides = ((1, 8 + by - rows, 8 - rows), (-1, 8, 8 + by))
            for sign, src, dst in sides:
                there, back = gy + sign, gy - sign
                ok_y = lambda p: (p >= 0) & (p < ny)
                spans = [(lo, bx, None)] if faces else []
                spans += [(up[0][1], wide, gx - reach >= 0), (up[1][1], wide, gx + reach < nx)]
                for start, count, also in spans:
                    sends, receives = ok_y(there), ok_y(back)
                    if also is not None:
                        sends, receives = sends & also, receives & also
                    (self.y if also is None else self.corners).append(
                        Copy(
                            ref.at[pl.ds(start, count), :, pl.ds(src, rows), :],
                            ref.at[pl.ds(start, count), :, pl.ds(dst, rows), :],
                            (gx, there),
                            sends,
                            receives,
                            sems(),
                        )
                    )
            everything.append(self)

        def send(self):
            for copy in self.x + self.y:
                copy.start()

        def forward(self):
            for copy in self.x:
                copy.arrive()
            for copy in self.corners:
                copy.start()

        def finish(self):
            for copy in self.y + self.corners:
                copy.arrive()

        def leave(self):
            everything.remove(self)
            for copy in self.x + self.y + self.corners:
                copy.leave()

    class Gather:
        def __init__(self, rows, full, pad, index):
            self.rows, self.full, self.at = rows, full, pl.ds(pad + 2 * gx, 2)
            self.first = [
                self.copy(rows.at[gy], index, (gx, lax.rem(gy + k, ny))) for k in range(1, ny)
            ]
            mine = full.at[self.at]
            self.second = [
                self.copy(mine, index + 1, (lax.rem(gx + k, nx), gy)) for k in range(1, nx)
            ]
            self.first_all = self.copy(rows.at[pl.ds(0, ny - 1)], index, (gx, gy))
            self.second_all = self.copy(full.at[pl.ds(0, 2 * nx - 2)], index + 1, (gx, gy))

        def copy(self, ref, index, target):
            return pltpu.make_async_remote_copy(
                src_ref=ref,
                dst_ref=ref,
                send_sem=gather_send.at[index],
                recv_sem=gather_recv.at[index],
                device_id=target,
                device_id_type=MESH,
            )

        def send(self, tile):
            self.rows[gy] = tile
            for copy in self.first:
                copy.start()

        def forward(self):
            self.first_all.wait_recv()
            even, odd = self.rows[0], self.rows[1]
            for k in range(2, ny, 2):
                even, odd = even + self.rows[k], odd + self.rows[k + 1]
            low = iota(even.shape, 0) < 4
            layers = (
                jnp.where(low, even, pltpu.roll(odd, 4, 0)),
                jnp.where(low, pltpu.roll(even, 4, 0), odd),
            )
            for i in range(2):
                self.full[self.at.start + i] = layers[i]
            for copy in self.second:
                copy.start()

        def finish(self):
            self.second_all.wait_recv()

        def leave(self):
            self.first_all.wait_send()
            self.second_all.wait_send()

    x_v0, x_c0, x_b0 = Exchange(l0, va0, 4), Exchange(l0, c0, 4), Exchange(l0, b0, 3)
    x_k0 = Exchange(l0, vc0, 3)
    x_c1, x_b1, x_k1 = Exchange(l1, c1, 5), Exchange(l1, b1, 4), Exchange(l1, vc1, 5)
    x_c2, x_b2, x_k2 = (Exchange(l2, ref, 4) for ref in (c2, b2, vc2))
    f_c2, f_b2, f_k2 = (Exchange(l2, ref, 2, 2, False) for ref in (c2, b2, vc2))
    g_c3, g_b3 = Gather(pc, c3, l3.pad, 0), Gather(pb, b3, l3.pad, 2)

    for copy in loads:
        copy.wait()
    pl.semaphore_wait(barrier, nx + ny - 2)

    x_c0.send()
    x_v0.send()

    def double(k):
        for h in range(2):
            own = (pl.ds(l0.halo + k, 1), h, pl.ds(8, l0.by), slice(None))
            b0[own] = 2.0 * b0[own]

    loop(l0.bx, 1, double)
    x_b0.send()

    def clear(level, refs, far):
        lo, bx, by = level.halo, level.bx, level.by

        def layers(start, count):
            for ref in refs:
                ref[pl.ds(start, count)] = jnp.zeros((count,) + ref.shape[1:], F32)

        near = min(lo, bx)
        pl.when(gx == 0)(lambda: layers(lo - near, near))
        pl.when(gx == nx - 1)(lambda: layers(lo + bx, near))
        if far:
            pl.when(gx < 2)(lambda: layers(0, lo - bx))
            pl.when(gx >= nx - 2)(lambda: layers(lo + 2 * bx, lo - bx))

        def rows(start, count):
            for ref in refs:
                for h in range(level.nh):
                    ref[:, h, pl.ds(start, count), :] = jnp.zeros((level.width, count, LANES), F32)

        pl.when(gy == 0)(lambda: rows(0, 8))
        pl.when(gy == ny - 1)(lambda: rows(8 + by, 8))

    clear(l0, (va0, c0, b0, vc0), False)
    clear(l1, (c1, b1, vc1), False)
    clear(l2, (c2, b2, vc2), True)
    for ref in (va3, vb3, c3, va4, vb4, c4):
        pad = 1 if ref.shape[0] == nx + 2 else l3.pad
        for start in (0, ref.shape[0] - pad):
            ref[pl.ds(start, pad)] = jnp.zeros((pad, 8, LANES), F32)
    for ref in (vb0, va1, vb1, va2, vb2):
        for h in range(ref.shape[1]):
            for r in range(0, ref.shape[2], 8):
                ref[:, h, pl.ds(r, 8), :] = jnp.zeros((ref.shape[0], 8, LANES), F32)

    lane_base = 32 * lax.shift_right_logical(gy, 1)

    def tile_of(s, weight):
        row, col = iota((LANES, LANES), 0), iota((LANES, LANES), 1)
        pick = (lax.shift_right_logical(row, 1) + lane_base == col) & (row < l2.nz)
        m = jnp.where(pick, weight, 0.0).astype(F32)
        a = s[pl.ds(0, 8, stride=2), :] + s[pl.ds(1, 8, stride=2), :]
        return dot(a, m)

    field_pairs(l0, c0, s0)
    c1[l1.halo : l1.halo + l1.bx, 0, 8 : 8 + l1.by, :] = halve(l0, s0, 0.125)
    x_c1.send()
    field_pairs(l1, c1, s1)
    c2[l2.halo : l2.halo + l2.bx, 0, 8 : 8 + l2.by, :] = halve(l1, s1, 0.125)
    x_c2.send()
    f_c2.send()
    for k in range(2):
        s2[pl.ds(8 * k, 8), :] = (
            c2[l2.halo + 2 * k, 0, pl.ds(8, 8), :] + c2[l2.halo + 2 * k + 1, 0, pl.ds(8, 8), :]
        )
    g_c3.send(tile_of(s2, 0.125))

    for exchange in (x_c0, x_v0, x_b0):
        exchange.forward()
    for exchange in (x_c0, x_v0, x_b0):
        exchange.finish()
    g_c3.forward()
    for exchange in (x_c1, x_c2, f_c2):
        exchange.forward()
    bx0, by0 = gx * l0.bx, gy * l0.by

    setup(l0, c0, g0, d0, 3, 4, 40, 2, bx0, by0)
    sweep(l0, va0, vb0, c0, g0, b0, 3, 4, 40, 2)
    x_v0.leave()
    sweep(l0, vb0, va0, c0, g0, b0, 2, 4, 40, 2)
    sweep(l0, va0, vb0, c0, g0, b0, 1, 4, 40, 2)
    residual_pairs(l0, vb0, c0, b0, d0, s0, vc0)
    b1[l1.halo : l1.halo + l1.bx, 0, 8 : 8 + l1.by, :] = halve(l0, s0, 0.5)
    x_b1.send()
    x_k0.send()
    for exchange in (x_c1, x_c2, f_c2):
        exchange.finish()
    setup(l1, c1, g1, d1, 4, 4, 24, 2, gx * l1.bx, gy * l1.by)
    setup(l2, c2, g2, d2, 5, 2, 24, 2, gx * l2.bx, gy * l2.by)
    x_b1.forward()
    x_b1.finish()
    first_sweep(l1, va1, g1, b1, 3, 4, 24, 0)
    sweep(l1, va1, vb1, c1, g1, b1, 2, 4, 24, 0)
    sweep(l1, vb1, va1, c1, g1, b1, 1, 4, 24, 0)
    residual_pairs(l1, va1, c1, b1, d1, s1, vc1)
    b2[l2.halo : l2.halo + l2.bx, 0, 8 : 8 + l2.by, :] = halve(l1, s1, 0.5)
    x_b2.send()
    f_b2.send()
    x_k1.send()

    def pairs_of(ref):
        for k in range(nx):
            total = ref[l3.pad + 2 * k] + ref[l3.pad + 2 * k + 1]
            s3[k, pl.ds(0, 8), :] = total
            s3[k, pl.ds(8, 8), :] = total

    g_c3.finish()
    packed_setup(l3, c3, w3, wx3, g3, d3, RELAX)
    pairs_of(c3)
    c4[pl.ds(l4.pad, nx)] = packed_halve(s3, 0.125)
    packed_setup(l4, c4, w4, wx4, q4, d4, 1.0)

    x_b2.forward()
    x_b2.finish()
    first_sweep(l2, va2, g2, b2, 3, 2, 24, 0)
    sweep(l2, va2, vb2, c2, g2, b2, 2, 2, 24, 0)
    sweep(l2, vb2, va2, c2, g2, b2, 1, 2, 24, 0)
    for k in range(2):
        total = None
        for x0 in (l2.halo + 2 * k, l2.halo + 2 * k + 1):
            v, t = couple(l2, va2, c2, x0, 1, 8, 8)
            r = block(b2, 0, x0, 1, 8, 8) + t[0] - d2[pl.ds(x0 - l2.halo, 1), 0, :, :] * v[0]
            vc2[pl.ds(x0, 1), 0, pl.ds(8, 8), :] = v[0]
            total = r if total is None else total + r
        s2[pl.ds(8 * k, 8), :] = total[0]
    g_b3.send(tile_of(s2, 0.5))
    x_k2.send()
    f_k2.send()
    x_k0.forward()
    x_k1.forward()
    f_b2.forward()
    g_b3.forward()
    x_k2.forward()
    f_k2.forward()
    g_b3.finish()
    for k in range(l3.count):
        va3[l3.pad + k] = g3[k] * b3[l3.pad + k]
    packed_sweep(l3, va3, vb3, w3, wx3, g3, b3, l3.pad)
    packed_sweep(l3, vb3, va3, w3, wx3, g3, b3, l3.pad)

    def residual3(k):
        total = None
        for i in (2 * k, 2 * k + 1):
            v, t = packed_couple(l3, va3, w3, wx3, i)
            r = b3[pl.ds(l3.pad + i, 1)] + t - d3[pl.ds(i, 1)] * v
            total = r if total is None else total + r
        s3[pl.ds(k, 1), pl.ds(0, 8), :] = total
        s3[pl.ds(k, 1), pl.ds(8, 8), :] = total

    loop_pieces(nx, 2, residual3)
    res4[...] = packed_halve(s3, 0.5)

    sigma = THETA / DELTA
    rho = 1.0 / sigma
    for k in range(nx):
        direction = res4[k] * q4[k] * (1.0 / THETA)
        e4[k] = direction
        va4[l4.pad + k] = direction
    src, dst = va4, vb4
    for step in range(CHEB - 1):
        rho_new = 1.0 / (2.0 * sigma - rho)
        for k in range(nx):
            at = pl.ds(k, 1)
            v, t = packed_couple(l4, src, w4, wx4, k)
            r = res4[at] - (d4[at] * v - t)
            direction = (rho_new * rho) * v + (2.0 * rho_new / DELTA) * (r * q4[at])
            res4[at] = r
            e4[at] = e4[at] + direction
            dst[pl.ds(l4.pad + k, 1)] = direction
        rho = rho_new
        src, dst = dst, src

    row, col = iota((LANES, LANES), 0), iota((LANES, LANES), 1)
    spread = jnp.where(row == lax.shift_right_logical(col, 1), 1.0, 0.0).astype(F32)
    fine = dot(e4[...].reshape(nx * 8, LANES), spread).reshape(nx, 8, LANES)
    for dr in range(2):
        t3[:, pl.ds(dr, 4, stride=2), :] = fine[:, 0:4, :]
    for k in range(l3.count):
        vb3[l3.pad + k] = va3[l3.pad + k] + t3[k // 2]
    packed_sweep(l3, vb3, va3, w3, wx3, g3, b3, l3.pad)
    packed_sweep(l3, va3, vb3, w3, wx3, g3, b3, l3.pad)
    packed_sweep(l3, vb3, va3, w3, wx3, g3, b3, l3.pad)

    f_b2.finish()
    x_k2.finish()
    f_k2.finish()
    group = lax.shift_right_logical(gy, 1) - 1
    e3 = va3[pl.ds(l3.pad - 3 + 2 * gx, 8)].reshape(64, LANES)
    for q in range(3):
        pick = (row == lax.shift_right_logical(col, 1) + 32 * (group + q)) & (col < l2.nz)
        part = dot(e3, jnp.where(pick, 1.0, 0.0).astype(F32))
        pe2[:, 0, pl.ds(8 * q, 8), :] = part.reshape(8, 8, LANES)
    add_prolonged(l2, pe2, vc2, va2, 0, 0, 8, 16, 4 * (gy & 1) + 4)
    sweep(l2, va2, vb2, c2, g2, b2, 5, 2, 24, 0)
    sweep(l2, vb2, va2, c2, g2, b2, 4, 2, 24, 0)
    sweep(l2, va2, vb2, c2, g2, b2, 3, 2, 24, 0)

    x_k1.finish()
    prolong(l1, vb2, 3, 4, 10, 16, pe1, None, None, 0)
    add_prolonged(l1, pe1, vc1, va1, 0, 0, 10, 16)
    sweep(l1, va1, vb1, c1, g1, b1, 4, 4, 24, 0)
    sweep(l1, vb1, va1, c1, g1, b1, 3, 4, 24, 0)
    sweep(l1, va1, vb1, c1, g1, b1, 2, 4, 24, 0)

    x_k0.finish()
    prolong(l0, vb1, 4, 4, 12, 24, pe0, None, None, 0)
    add_prolonged(l0, pe0, vc0, va0, 0, 0, 12, 24)
    sweep(l0, va0, vb0, c0, g0, b0, 2, 4, 40, 2)
    sweep(l0, vb0, va0, c0, g0, b0, 1, 4, 40, 2)
    sweep(l0, va0, o0, c0, g0, b0, 0, 8, 32, 2, l0.halo, 8)
    stores = []
    for h in range(2):
        stores.append(
            pltpu.make_async_copy(
                o0.at[:, h], out.at[:, :, h * LANES : (h + 1) * LANES], local_sem.at[6 + h]
            )
        )
    for copy in stores:
        copy.start()
    for copy in stores:
        copy.wait()
    for exchange in list(everything):
        exchange.leave()
    g_c3.leave()
    g_b3.leave()


def solution(mesh):
    nx, ny = mesh.shape["gx"], mesh.shape["gy"]
    l0 = Level(2, 256, 4, 16, 32, 48, 16 * nx, 32 * ny)
    l1 = Level(1, 128, 6, 8, 16, 32, 8 * nx, 16 * ny)
    l2 = Level(1, 64, 6, 4, 8, 32, 4 * nx, 8 * ny)
    l3 = Packed(2 * nx, 4, 8, 32, ny // 2)
    l4 = Packed(nx, 1, 4, 16, ny // 2)

    def vmem(*shape):
        return pltpu.VMEM(shape, F32)

    e, o = (lambda l: l.ext()), (lambda l: l.own())
    scratch = [e(l0)] * 6 + [o(l0), vmem(8, 2, 32, LANES), o(l0), vmem(12, 2, 24, LANES)]
    scratch += [e(l1)] * 6 + [o(l1), vmem(4, 1, 16, LANES), vmem(10, 1, 16, LANES)]
    scratch += [e(l2)] * 6 + [o(l2), vmem(16, LANES), vmem(8, 1, 24, LANES)]
    scratch += [e(l3)] * 4 + [l3.own(1), o(l3), o(l3), vmem(nx, 16, LANES), vmem(nx, 8, LANES)]
    scratch += [o(l3)] * 4
    scratch += [e(l4)] * 3 + [l4.own(1)] + [o(l4)] * 8
    scratch += [vmem(ny, 8, LANES)] * 2
    copies = 10 * 8 + 3 * 6
    scratch += [
        pltpu.SemaphoreType.DMA((copies,)),
        pltpu.SemaphoreType.DMA((copies,)),
        pltpu.SemaphoreType.DMA((4,)),
        pltpu.SemaphoreType.DMA((4,)),
        pltpu.SemaphoreType.DMA((8,)),
    ]

    def step(guess, right_side, coefficient):
        return pl.pallas_call(
            functools.partial(kernel, nx, ny, (l0, l1, l2, l3, l4)),
            out_shape=jax.ShapeDtypeStruct(guess.shape, F32),
            in_specs=[pl.BlockSpec(memory_space=pl.ANY)] * 3,
            out_specs=pl.BlockSpec(memory_space=pl.ANY),
            scratch_shapes=scratch,
            compiler_params=pltpu.CompilerParams(collective_id=0, has_side_effects=True),
        )(guess, right_side, coefficient)

    spec = P("gx", "gy", None)
    return jax.shard_map(
        step, mesh=mesh, in_specs=(spec, spec, spec), out_specs=spec, check_vma=False
    )
```

```python
import functools

import jax
import jax.numpy as jnp
from jax import lax
from jax.experimental import pallas as pl
from jax.experimental.pallas import tpu as pltpu
from jax.sharding import PartitionSpec as P

MESH = pl.DeviceIdType.MESH
F32 = jnp.float32
RELAX = 0.7
CHEB = 8
THETA = 1.04
DELTA = 0.96
LANES = 128
PIECES = 24


def iota(shape, dim):
    return lax.broadcasted_iota(jnp.int32, shape, dim)


class Level:
    def __init__(self, nh, nz, halo, bx, by, rows, total_x, total_y):
        self.nh, self.nz, self.halo, self.bx, self.by = nh, nz, halo, bx, by
        self.rows, self.total_x, self.total_y = rows, total_x, total_y
        self.width = bx + 2 * halo

    def ext(self):
        return pltpu.VMEM((self.width, self.nh, self.rows, LANES), F32)

    def own(self):
        return pltpu.VMEM((self.bx, self.nh, self.by, LANES), F32)


def z_sum(level, v):
    lane = iota(v[0].shape, 2)
    up = [pltpu.roll(a, 1, 2) for a in v]
    down = [pltpu.roll(a, LANES - 1, 2) for a in v]
    if level.nh == 2:
        low = [jnp.where(lane == 0, 0.0, up[0]), jnp.where(lane == 0, up[0], up[1])]
        high = [
            jnp.where(lane == LANES - 1, down[1], down[0]),
            jnp.where(lane == LANES - 1, 0.0, down[1]),
        ]
    elif level.nz == LANES:
        low = [jnp.where(lane == 0, 0.0, up[0])]
        high = [jnp.where(lane == LANES - 1, 0.0, down[0])]
    else:
        low, high = up, down
    return [a + b for a, b in zip(low, high)]


def block(ref, half, x0, cx, r0, n):
    return ref[pl.ds(x0, cx), half, pl.ds(r0, n), :]


def couple(level, v_ref, c_ref, x0, cx, r0, n):
    halves = range(level.nh)
    v = [block(v_ref, h, x0, cx, r0, n) for h in halves]
    c = [block(c_ref, h, x0, cx, r0, n) for h in halves]
    vz = z_sum(level, v)
    uz = z_sum(level, [a * b for a, b in zip(c, v)])
    out = []
    for h in halves:
        sv, su = vz[h], uz[h]
        for dx, dr in ((-1, 0), (1, 0), (0, -1), (0, 1)):
            near = block(v_ref, h, x0 + dx, cx, r0 + dr, n)
            sv = sv + near
            su = su + near * block(c_ref, h, x0 + dx, cx, r0 + dr, n)
        out.append(c[h] * sv + su)
    return v, out


def tiles(r0, n):
    return tuple(range(r0, r0 + n, 8))


def loop(count, chunk, body):
    steps = count // chunk
    assert steps * chunk == count
    if steps == 1:
        body(0)
    else:
        lax.fori_loop(0, steps, lambda k, _: (body(k * chunk), 0)[1], 0)


def over(level, span, rows, body):
    lo, hi = span
    most = max(1, (PIECES // level.nh) // len(rows))
    chunk = max(c for c in range(1, hi - lo + 1) if (hi - lo) % c == 0 and c <= most)

    def several(k):
        for i in range(chunk):
            for r in rows:
                body(level.halo + lo + k + i, r)

    loop(hi - lo, chunk, several)


def sweep(level, src, dst, c, g, b, span, rows, put=None):
    def body(x0, r):
        v, t = couple(level, src, c, x0, 1, r, 8)
        for h in range(level.nh):
            new = (1.0 - RELAX) * v[h] + block(g, h, x0, 1, r, 8) * (
                t[h] + block(b, h, x0, 1, r, 8)
            )
            if put is None:
                dst[pl.ds(x0, 1), h, pl.ds(r, 8), :] = new
            else:
                put(x0, h, r, new)

    over(level, span, rows, body)


def first_sweep(level, dst, g, b, span, rows):
    def body(x0, r):
        for h in range(level.nh):
            dst[pl.ds(x0, 1), h, pl.ds(r, 8), :] = block(g, h, x0, 1, r, 8) * block(
                b, h, x0, 1, r, 8
            )

    over(level, span, rows, body)


def setup(level, c, g, d, span, rows, base_x, base_y):
    def body(x0, r):
        halves = range(level.nh)
        mid = [block(c, h, x0, 1, r, 8) for h in halves]
        cz = z_sum(level, mid)
        shape = mid[0].shape
        px = base_x + x0 - level.halo
        py = iota(shape, 1) + jnp.where((px >= 0) & (px < level.total_x), base_y + r - 8, -1000)
        mask = (py >= 0) & (py < level.total_y)
        if level.nz < LANES:
            mask = mask & (iota(shape, 2) < level.nz)
        for h in halves:
            total = 6.0 * mid[h] + cz[h]
            for dx, dr in ((-1, 0), (1, 0), (0, -1), (0, 1)):
                total = total + block(c, h, x0 + dx, 1, r + dr, 8)
            g[pl.ds(x0, 1), h, pl.ds(r, 8), :] = jnp.where(
                mask, RELAX / jnp.where(mask, total, 1.0), 0.0
            )
            d[pl.ds(x0, 1), h, pl.ds(r, 8), :] = total

    over(level, span, rows, body)


def residual_pairs(level, v_ref, c, b, d, s, keep):
    def body(k):
        for r in range(0, level.by, 8):
            parts = []
            for dx in range(2):
                x0 = level.halo + 2 * k + dx
                v, t = couple(level, v_ref, c, x0, 1, 8 + r, 8)
                for h in range(level.nh):
                    own = block(d, h, x0, 1, 8 + r, 8)
                    parts.append(block(b, h, x0, 1, 8 + r, 8) + t[h] - own * v[h])
                    if keep is not None:
                        keep[pl.ds(x0, 1), h, pl.ds(8 + r, 8), :] = v[h]
            for h in range(level.nh):
                total = parts[h] + parts[level.nh + h]
                s[pl.ds(k, 1), h, pl.ds(r, 8), :] = total

    loop(level.bx // 2, 1, body)


def field_pairs(level, ref, s):
    def body(k):
        x0 = level.halo + 2 * k
        for h in range(level.nh):
            r = block(ref, h, x0, 1, 8, level.by) + block(ref, h, x0 + 1, 1, 8, level.by)
            s[pl.ds(k, 1), h, pl.ds(0, level.by), :] = r

    loop(level.bx // 2, 1, body)


def dot(a, m):
    return jnp.dot(a, m, precision=lax.Precision.HIGHEST, preferred_element_type=F32)


def halve(level, s, weight):
    rows = level.by // 2
    count = level.bx // 2
    row, col = iota((LANES, LANES), 0), iota((LANES, LANES), 1)
    total = None
    for h in range(level.nh):
        pick = (lax.shift_right_logical(row, 1) + h * 64 == col) & (row < level.nz)
        m = jnp.where(pick, weight, 0.0).astype(F32)
        a = s[:, h, pl.ds(0, rows, stride=2), :] + s[:, h, pl.ds(1, rows, stride=2), :]
        part = dot(a.reshape(count * rows, LANES), m)
        total = part if total is None else total + part
    return total.reshape(count, rows, LANES)


def prolong(level, e, ex, er, count, ne, pe, base, dst, x0):
    row, col = iota((LANES, LANES), 0), iota((LANES, LANES), 1)
    coarse = e[pl.ds(ex, count), 0, pl.ds(er, ne), :].reshape(count * ne, LANES)
    for h in range(level.nh):
        m = jnp.where(row == lax.shift_right_logical(col, 1) + h * 64, 1.0, 0.0).astype(F32)
        pe[:, h, :, :] = dot(coarse, m).reshape(count, ne, LANES)


def add_prolonged(level, pe, base, dst, x0, r0, count, ne, er=0):
    def body(k):
        for h in range(level.nh):
            fine = pe[k, h, pl.ds(er, ne), :]
            for dx in range(2):
                for dr in range(2):
                    at = (x0 + 2 * k + dx, h, pl.ds(r0 + dr, ne, stride=2), slice(None))
                    dst[at] = base[at] + fine

    loop(count, 1, body)


class Packed:
    def __init__(self, count, pad, rows, width, groups):
        self.count, self.pad, self.rows, self.width, self.groups = count, pad, rows, width, groups

    def ext(self):
        return pltpu.VMEM((self.count + 2 * self.pad, 8, LANES), F32)

    def own(self, more=0):
        return pltpu.VMEM((self.count + more, 8, LANES), F32)


def packed_near(p, v):
    row = iota(v.shape, 1) & (p.rows - 1)
    after, before = pltpu.roll(v, 7, 1), pltpu.roll(v, 1, 1)
    return (
        jnp.where(row == p.rows - 1, pltpu.roll(after, LANES - p.width, 2), after),
        jnp.where(row == 0, pltpu.roll(before, p.width, 2), before),
        pltpu.roll(v, LANES - 1, 2),
        pltpu.roll(v, 1, 2),
    )


def packed_setup(p, c, w, wx, g, d, scale):
    def body(k):
        at = pl.ds(p.pad + k, 1)
        mid = c[at]
        lane, row = iota(mid.shape, 2), iota(mid.shape, 1) & (p.rows - 1)
        valid = lane < p.width * p.groups
        z = lane & (p.width - 1)
        inside = (
            (row < p.rows - 1) | (lane < p.width * (p.groups - 1)),
            (row > 0) | (lane >= p.width),
            z < p.width - 1,
            z > 0,
        )
        below = c[pl.ds(p.pad + k - 1, 1)]
        total = 6.0 * mid + below + c[pl.ds(p.pad + k + 1, 1)]
        wx[pl.ds(k, 1)] = mid + below
        for ref, near, ok in zip(w, packed_near(p, mid), inside):
            near = jnp.where(valid & ok, near, 0.0)
            ref[pl.ds(k, 1)] = jnp.where(valid & ok, mid + near, 0.0)
            total = total + near
        g[pl.ds(k, 1)] = jnp.where(valid, scale / jnp.where(valid, total, 1.0), 0.0)
        d[pl.ds(k, 1)] = total

    loop_pieces(p.count, 4, body)
    wx[pl.ds(p.count, 1)] = c[pl.ds(p.pad + p.count - 1, 1)]


def packed_couple(p, v_ref, w, wx, k):
    v = v_ref[pl.ds(p.pad + k, 1)]
    t = wx[pl.ds(k, 1)] * v_ref[pl.ds(p.pad + k - 1, 1)]
    t = t + wx[pl.ds(k + 1, 1)] * v_ref[pl.ds(p.pad + k + 1, 1)]
    parts = [ref[pl.ds(k, 1)] * near for ref, near in zip(w, packed_near(p, v))]
    return v, t + ((parts[0] + parts[1]) + (parts[2] + parts[3]))


def loop_pieces(count, chunk, body):
    def several(k):
        for i in range(chunk):
            body(k + i)

    loop(count, chunk, several)


def packed_sweep(p, src, dst, w, wx, g, b, b_pad):
    def body(k):
        v, t = packed_couple(p, src, w, wx, k)
        new = (1.0 - RELAX) * v + g[pl.ds(k, 1)] * (t + b[pl.ds(b_pad + k, 1)])
        dst[pl.ds(p.pad + k, 1)] = new

    loop_pieces(p.count, 16, body)


def packed_halve(s, weight):
    row, col = iota((LANES, LANES), 0), iota((LANES, LANES), 1)
    m = jnp.where(lax.shift_right_logical(row, 1) == col, weight, 0.0).astype(F32)
    a = s[:, pl.ds(0, 8, stride=2), :] + s[:, pl.ds(1, 8, stride=2), :]
    return dot(a.reshape(s.shape[0] * 8, LANES), m).reshape(s.shape[0], 8, LANES)


class Copy:
    def __init__(self, src, dst, target, sends, receives, sems):
        send_sem, recv_sem, index = sems
        self.copy = pltpu.make_async_remote_copy(
            src_ref=src,
            dst_ref=dst,
            send_sem=send_sem.at[index],
            recv_sem=recv_sem.at[index],
            device_id=target,
            device_id_type=MESH,
        )
        self.sends, self.receives = sends, receives

    def start(self):
        pl.when(self.sends)(lambda: self.copy.start())

    def arrive(self):
        pl.when(self.receives)(lambda: self.copy.wait_recv())

    def leave(self):
        pl.when(self.sends)(lambda: self.copy.wait_send())


def kernel(nx, ny, levels, guess, rhs, coef, out, *scratch):
    l0, l1, l2, l3, l4 = levels
    names = iter(scratch)
    take = lambda k: [next(names) for _ in range(k)]
    va0, vb0, vc0, c0, b0, g0, d0, ve0, vf0, s0, pe0 = take(11)
    va1, vb1, vc1, c1, b1, g1, d1, s1, pe1 = take(9)
    va2, vb2, vc2, c2, b2, g2, d2, s2, pe2 = take(9)
    va3, vb3, c3, b3, wx3, g3, d3, s3, t3 = take(9)
    w3 = take(4)
    va4, vb4, c4, wx4, q4, d4, res4, e4 = take(8)
    w4 = take(4)
    pc, pb = take(2)
    send_sem, recv_sem, gather_send, gather_recv, local_sem = take(5)

    gx, gy = lax.axis_index("gx"), lax.axis_index("gy")
    counter = iter(range(1000))

    def sems():
        return send_sem, recv_sem, next(counter)

    loads = []
    for i, (src, dst) in enumerate(((coef, c0), (guess, va0), (rhs, b0))):
        for h in range(2):
            loads.append(
                pltpu.make_async_copy(
                    src.at[:, :, h * LANES : (h + 1) * LANES],
                    dst.at[l0.halo : l0.halo + l0.bx, h, 8 : 8 + l0.by, :],
                    local_sem.at[2 * i + h],
                )
            )
    for copy in loads:
        copy.start()

    barrier = pltpu.get_barrier_semaphore()
    for k in range(1, nx):
        pl.semaphore_signal(
            barrier, inc=1, device_id=(lax.rem(gx + k, nx), gy), device_id_type=MESH
        )
    for k in range(1, ny):
        pl.semaphore_signal(
            barrier, inc=1, device_id=(gx, lax.rem(gy + k, ny)), device_id_type=MESH
        )

    for dx in (1, nx - 1):
        for dy in (1, ny - 1):
            diagonal = (lax.rem(gx + dx, nx), lax.rem(gy + dy, ny))
            pl.semaphore_signal(barrier, inc=1, device_id=diagonal, device_id_type=MESH)

    everything = []

    class Exchange:
        def __init__(self, level, ref, wide, reach=1, faces=True, direct=False):
            self.direct = direct
            lo, bx, by = level.halo, level.bx, level.by
            if reach == 1:
                up = ((lo + bx - wide, lo - wide), (lo, lo + bx))
            else:
                up = ((lo + 2 * bx - lo, 0), (lo, lo + 2 * bx))
            self.x, self.y, self.corners = [], [], []
            own = pl.ds(8, by)
            for sign, (src, dst) in zip((1, -1), up):
                there, back = gx + sign * reach, gx - sign * reach
                ok = lambda p: (p >= 0) & (p < nx)
                self.x.append(
                    Copy(
                        ref.at[pl.ds(src, wide), :, own, :],
                        ref.at[pl.ds(dst, wide), :, own, :],
                        (there, gy),
                        ok(there),
                        ok(back),
                        sems(),
                    )
                )
            rows = 4 if level.nh == 2 else 8
            sides = ((1, 8 + by - rows, 8 - rows), (-1, 8, 8 + by))
            inside_x, inside_y = (lambda p: (p >= 0) & (p < nx)), (lambda p: (p >= 0) & (p < ny))
            for sign, src, dst in sides:
                there, back = gy + sign, gy - sign
                sends, receives = inside_y(there), inside_y(back)

                def strip(start, count, row):
                    return ref.at[pl.ds(start, count), :, pl.ds(row, rows), :]

                if faces:
                    self.y.append(
                        Copy(
                            strip(lo, bx, src),
                            strip(lo, bx, dst),
                            (gx, there),
                            sends,
                            receives,
                            sems(),
                        )
                    )
                for sign_x, (src_x, dst_x) in zip((1, -1), up):
                    far, near = gx + sign_x * reach, gx - sign_x * reach
                    have = receives & inside_x(near)
                    self.corners.append(
                        Copy(
                            strip(src_x if direct else dst_x, wide, src),
                            strip(dst_x, wide, dst),
                            (far if direct else gx, there),
                            sends & inside_x(far if direct else near),
                            have,
                            sems(),
                        )
                    )
            everything.append(self)

        def send(self):
            for copy in self.x + self.y + (self.corners if self.direct else []):
                copy.start()

        def forward(self):
            for copy in self.x:
                copy.arrive()
            for copy in [] if self.direct else self.corners:
                copy.start()

        def finish(self):
            for copy in self.y + self.corners:
                copy.arrive()

        def leave(self):
            everything.remove(self)
            for copy in self.x + self.y + self.corners:
                copy.leave()

    class Gather:
        def __init__(self, rows, full, pad, index):
            self.rows, self.full, self.at = rows, full, pl.ds(pad + 2 * gx, 2)
            self.first = [
                self.copy(rows.at[gy], index, (gx, lax.rem(gy + k, ny))) for k in range(1, ny)
            ]
            mine = full.at[self.at]
            self.second = [
                self.copy(mine, index + 1, (lax.rem(gx + k, nx), gy)) for k in range(1, nx)
            ]
            self.first_all = self.copy(rows.at[pl.ds(0, ny - 1)], index, (gx, gy))
            self.second_all = self.copy(full.at[pl.ds(0, 2 * nx - 2)], index + 1, (gx, gy))

        def copy(self, ref, index, target):
            return pltpu.make_async_remote_copy(
                src_ref=ref,
                dst_ref=ref,
                send_sem=gather_send.at[index],
                recv_sem=gather_recv.at[index],
                device_id=target,
                device_id_type=MESH,
            )

        def send(self, tile):
            self.rows[gy] = tile
            for copy in self.first:
                copy.start()

        def forward(self):
            self.first_all.wait_recv()
            even, odd = self.rows[0], self.rows[1]
            for k in range(2, ny, 2):
                even, odd = even + self.rows[k], odd + self.rows[k + 1]
            low = iota(even.shape, 0) < 4
            layers = (
                jnp.where(low, even, pltpu.roll(odd, 4, 0)),
                jnp.where(low, pltpu.roll(even, 4, 0), odd),
            )
            for i in range(2):
                self.full[self.at.start + i] = layers[i]
            for copy in self.second:
                copy.start()

        def finish(self):
            self.second_all.wait_recv()

        def leave(self):
            self.first_all.wait_send()
            self.second_all.wait_send()

    x_v0, x_c0, x_b0 = Exchange(l0, va0, 4), Exchange(l0, c0, 4), Exchange(l0, b0, 3)
    x_k0 = Exchange(l0, vc0, 3)
    x_c1, x_b1, x_k1 = Exchange(l1, c1, 5), Exchange(l1, b1, 4, direct=True), Exchange(l1, vc1, 5)
    x_c2, x_k2 = Exchange(l2, c2, 4), Exchange(l2, vc2, 4)
    x_b2 = Exchange(l2, b2, 4, direct=True)
    f_c2, f_b2, f_k2 = (Exchange(l2, ref, 2, 2, False) for ref in (c2, b2, vc2))
    g_c3, g_b3 = Gather(pc, c3, l3.pad, 0), Gather(pb, b3, l3.pad, 2)

    for copy in loads:
        copy.wait()
    pl.semaphore_wait(barrier, nx + ny + 2)

    x_c0.send()
    x_v0.send()

    def double(k):
        for h in range(2):
            own = (pl.ds(l0.halo + k, 1), h, pl.ds(8, l0.by), slice(None))
            b0[own] = 2.0 * b0[own]

    loop(l0.bx, 1, double)
    x_b0.send()

    def clear(level, refs, far):
        lo, bx, by = level.halo, level.bx, level.by

        def layers(start, count):
            for ref in refs:
                ref[pl.ds(start, count)] = jnp.zeros((count,) + ref.shape[1:], F32)

        near = min(lo, bx)
        pl.when(gx == 0)(lambda: layers(lo - near, near))
        pl.when(gx == nx - 1)(lambda: layers(lo + bx, near))
        if far:
            pl.when(gx < 2)(lambda: layers(0, lo - bx))
            pl.when(gx >= nx - 2)(lambda: layers(lo + 2 * bx, lo - bx))

        def rows(start, count):
            for ref in refs:
                for h in range(level.nh):
                    ref[:, h, pl.ds(start, count), :] = jnp.zeros((level.width, count, LANES), F32)

        pl.when(gy == 0)(lambda: rows(0, 8))
        pl.when(gy == ny - 1)(lambda: rows(8 + by, 8))

    clear(l0, (va0, c0, b0, vc0), False)
    clear(l1, (c1, b1, vc1), False)
    clear(l2, (c2, b2, vc2), True)
    for ref in (va3, vb3, c3, va4, vb4, c4):
        pad = 1 if ref.shape[0] == nx + 2 else l3.pad
        for start in (0, ref.shape[0] - pad):
            ref[pl.ds(start, pad)] = jnp.zeros((pad, 8, LANES), F32)
    for ref in (va1, vb1, va2, vb2):
        for h in range(ref.shape[1]):
            for r in range(0, ref.shape[2], 8):
                ref[:, h, pl.ds(r, 8), :] = jnp.zeros((ref.shape[0], 8, LANES), F32)

    lane_base = 32 * lax.shift_right_logical(gy, 1)

    def tile_of(s, weight):
        row, col = iota((LANES, LANES), 0), iota((LANES, LANES), 1)
        pick = (lax.shift_right_logical(row, 1) + lane_base == col) & (row < l2.nz)
        m = jnp.where(pick, weight, 0.0).astype(F32)
        a = s[pl.ds(0, 8, stride=2), :] + s[pl.ds(1, 8, stride=2), :]
        return dot(a, m)

    field_pairs(l0, c0, s0)
    c1[l1.halo : l1.halo + l1.bx, 0, 8 : 8 + l1.by, :] = halve(l0, s0, 0.125)
    x_c1.send()
    field_pairs(l1, c1, s1)
    c2[l2.halo : l2.halo + l2.bx, 0, 8 : 8 + l2.by, :] = halve(l1, s1, 0.125)
    x_c2.send()
    f_c2.send()
    for k in range(2):
        s2[pl.ds(8 * k, 8), :] = (
            c2[l2.halo + 2 * k, 0, pl.ds(8, 8), :] + c2[l2.halo + 2 * k + 1, 0, pl.ds(8, 8), :]
        )
    g_c3.send(tile_of(s2, 0.125))

    bx0, by0 = gx * l0.bx, gy * l0.by
    chain = (va0, vb0, ve0, vf0)
    inner = tiles(12, 24)
    setup(l0, c0, g0, d0, (1, l0.bx - 1), inner, bx0, by0)
    for k in range(1, 4):
        sweep(l0, chain[k - 1], chain[k], c0, g0, b0, (k, l0.bx - k), inner)
    x_c0.forward()
    for span in ((-3, 1), (l0.bx - 1, l0.bx + 3)):
        setup(l0, c0, g0, d0, span, inner, bx0, by0)
    x_v0.forward()
    x_b0.forward()
    for k in range(1, 4):
        for span in ((k - 4, k), (l0.bx - k, l0.bx + 4 - k)):
            sweep(l0, chain[k - 1], chain[k], c0, g0, b0, span, inner)
    for exchange in (x_c0, x_v0, x_b0):
        exchange.finish()
    g_c3.forward()
    for exchange in (x_c1, x_c2, f_c2):
        exchange.forward()
    setup(l0, c0, g0, d0, (-3, l0.bx + 3), (4, 36), bx0, by0)
    for k in range(1, 4):
        span = (k - 4, l0.bx + 4 - k)
        sweep(l0, chain[k - 1], chain[k], c0, g0, b0, span, (3 + k, 37 - k))
    residual_pairs(l0, vf0, c0, b0, d0, s0, vc0)
    b1[l1.halo : l1.halo + l1.bx, 0, 8 : 8 + l1.by, :] = halve(l0, s0, 0.5)
    x_b1.send()
    x_k0.send()
    for exchange in (x_c1, x_c2, f_c2):
        exchange.finish()
    rows1, rows2 = tiles(4, 24), tiles(2, 24)
    setup(l1, c1, g1, d1, (-4, l1.bx + 4), rows1, gx * l1.bx, gy * l1.by)
    setup(l2, c2, g2, d2, (-5, l2.bx + 5), rows2, gx * l2.bx, gy * l2.by)
    x_b1.forward()
    x_b1.finish()
    first_sweep(l1, va1, g1, b1, (-3, l1.bx + 3), rows1)
    sweep(l1, va1, vb1, c1, g1, b1, (-2, l1.bx + 2), rows1)
    sweep(l1, vb1, va1, c1, g1, b1, (-1, l1.bx + 1), rows1)
    residual_pairs(l1, va1, c1, b1, d1, s1, vc1)
    b2[l2.halo : l2.halo + l2.bx, 0, 8 : 8 + l2.by, :] = halve(l1, s1, 0.5)
    x_b2.send()
    f_b2.send()
    x_k1.send()

    def pairs_of(ref):
        for k in range(nx):
            total = ref[l3.pad + 2 * k] + ref[l3.pad + 2 * k + 1]
            s3[k, pl.ds(0, 8), :] = total
            s3[k, pl.ds(8, 8), :] = total

    g_c3.finish()
    packed_setup(l3, c3, w3, wx3, g3, d3, RELAX)
    pairs_of(c3)
    c4[pl.ds(l4.pad, nx)] = packed_halve(s3, 0.125)
    packed_setup(l4, c4, w4, wx4, q4, d4, 1.0)

    x_b2.forward()
    x_b2.finish()
    first_sweep(l2, va2, g2, b2, (-3, l2.bx + 3), rows2)
    sweep(l2, va2, vb2, c2, g2, b2, (-2, l2.bx + 2), rows2)
    sweep(l2, vb2, va2, c2, g2, b2, (-1, l2.bx + 1), rows2)
    for k in range(2):
        total = None
        for x0 in (l2.halo + 2 * k, l2.halo + 2 * k + 1):
            v, t = couple(l2, va2, c2, x0, 1, 8, 8)
            r = block(b2, 0, x0, 1, 8, 8) + t[0] - block(d2, 0, x0, 1, 8, 8) * v[0]
            vc2[pl.ds(x0, 1), 0, pl.ds(8, 8), :] = v[0]
            total = r if total is None else total + r
        s2[pl.ds(8 * k, 8), :] = total[0]
    g_b3.send(tile_of(s2, 0.5))
    x_k2.send()
    f_k2.send()
    x_k0.forward()
    x_k1.forward()
    f_b2.forward()
    g_b3.forward()
    x_k2.forward()
    f_k2.forward()
    g_b3.finish()
    for k in range(l3.count):
        va3[l3.pad + k] = g3[k] * b3[l3.pad + k]
    packed_sweep(l3, va3, vb3, w3, wx3, g3, b3, l3.pad)
    packed_sweep(l3, vb3, va3, w3, wx3, g3, b3, l3.pad)

    def residual3(k):
        total = None
        for i in (2 * k, 2 * k + 1):
            v, t = packed_couple(l3, va3, w3, wx3, i)
            r = b3[pl.ds(l3.pad + i, 1)] + t - d3[pl.ds(i, 1)] * v
            total = r if total is None else total + r
        s3[pl.ds(k, 1), pl.ds(0, 8), :] = total
        s3[pl.ds(k, 1), pl.ds(8, 8), :] = total

    loop_pieces(nx, 2, residual3)
    res4[...] = packed_halve(s3, 0.5)

    sigma = THETA / DELTA
    rho = 1.0 / sigma
    for k in range(nx):
        direction = res4[k] * q4[k] * (1.0 / THETA)
        e4[k] = direction
        va4[l4.pad + k] = direction
    src, dst = va4, vb4
    for step in range(CHEB - 1):
        rho_new = 1.0 / (2.0 * sigma - rho)
        for k in range(nx):
            at = pl.ds(k, 1)
            v, t = packed_couple(l4, src, w4, wx4, k)
            r = res4[at] - (d4[at] * v - t)
            direction = (rho_new * rho) * v + (2.0 * rho_new / DELTA) * (r * q4[at])
            res4[at] = r
            e4[at] = e4[at] + direction
            dst[pl.ds(l4.pad + k, 1)] = direction
        rho = rho_new
        src, dst = dst, src

    row, col = iota((LANES, LANES), 0), iota((LANES, LANES), 1)
    spread = jnp.where(row == lax.shift_right_logical(col, 1), 1.0, 0.0).astype(F32)
    fine = dot(e4[...].reshape(nx * 8, LANES), spread).reshape(nx, 8, LANES)
    for dr in range(2):
        t3[:, pl.ds(dr, 4, stride=2), :] = fine[:, 0:4, :]
    for k in range(l3.count):
        vb3[l3.pad + k] = va3[l3.pad + k] + t3[k // 2]
    packed_sweep(l3, vb3, va3, w3, wx3, g3, b3, l3.pad)
    packed_sweep(l3, va3, vb3, w3, wx3, g3, b3, l3.pad)
    packed_sweep(l3, vb3, va3, w3, wx3, g3, b3, l3.pad)

    f_b2.finish()
    x_k2.finish()
    f_k2.finish()
    group = lax.shift_right_logical(gy, 1) - 1
    e3 = va3[pl.ds(l3.pad - 3 + 2 * gx, 8)].reshape(64, LANES)
    for q in range(3):
        pick = (row == lax.shift_right_logical(col, 1) + 32 * (group + q)) & (col < l2.nz)
        part = dot(e3, jnp.where(pick, 1.0, 0.0).astype(F32))
        pe2[:, 0, pl.ds(8 * q, 8), :] = part.reshape(8, 8, LANES)
    add_prolonged(l2, pe2, vc2, va2, 0, 0, 8, 16, 4 * (gy & 1) + 4)
    sweep(l2, va2, vb2, c2, g2, b2, (-5, l2.bx + 5), rows2)
    sweep(l2, vb2, va2, c2, g2, b2, (-4, l2.bx + 4), rows2)
    sweep(l2, va2, vb2, c2, g2, b2, (-3, l2.bx + 3), rows2)

    x_k1.finish()
    prolong(l1, vb2, 3, 4, 10, 16, pe1, None, None, 0)
    add_prolonged(l1, pe1, vc1, va1, 0, 0, 10, 16)
    sweep(l1, va1, vb1, c1, g1, b1, (-4, l1.bx + 4), rows1)
    sweep(l1, vb1, va1, c1, g1, b1, (-3, l1.bx + 3), rows1)
    sweep(l1, va1, vb1, c1, g1, b1, (-2, l1.bx + 2), rows1)

    x_k0.finish()
    prolong(l0, vb1, 4, 4, 12, 24, pe0, None, None, 0)
    x_v0.leave()
    add_prolonged(l0, pe0, vc0, va0, 0, 0, 12, 24)
    def put(x0, h, r, new):
        out[pl.ds(x0 - l0.halo, 1), pl.ds(r - 8, 8), h * LANES : (h + 1) * LANES] = new

    sweep(l0, va0, vb0, c0, g0, b0, (-2, l0.bx + 2), tiles(4, 40))
    sweep(l0, vb0, ve0, c0, g0, b0, (-1, l0.bx + 1), tiles(4, 40))
    sweep(l0, ve0, None, c0, g0, b0, (0, l0.bx), tiles(8, 32), put)
    for exchange in list(everything):
        exchange.leave()
    g_c3.leave()
    g_b3.leave()


def solution(mesh):
    nx, ny = mesh.shape["gx"], mesh.shape["gy"]
    l0 = Level(2, 256, 4, 16, 32, 48, 16 * nx, 32 * ny)
    l1 = Level(1, 128, 6, 8, 16, 32, 8 * nx, 16 * ny)
    l2 = Level(1, 64, 6, 4, 8, 32, 4 * nx, 8 * ny)
    l3 = Packed(2 * nx, 4, 8, 32, ny // 2)
    l4 = Packed(nx, 1, 4, 16, ny // 2)

    def vmem(*shape):
        return pltpu.VMEM(shape, F32)

    e, o = (lambda l: l.ext()), (lambda l: l.own())
    scratch = [e(l0)] * 9 + [vmem(8, 2, 32, LANES), vmem(12, 2, 24, LANES)]
    scratch += [e(l1)] * 7 + [vmem(4, 1, 16, LANES), vmem(10, 1, 16, LANES)]
    scratch += [e(l2)] * 7 + [vmem(16, LANES), vmem(8, 1, 24, LANES)]
    scratch += [e(l3)] * 4 + [l3.own(1), o(l3), o(l3), vmem(nx, 16, LANES), vmem(nx, 8, LANES)]
    scratch += [o(l3)] * 4
    scratch += [e(l4)] * 3 + [l4.own(1)] + [o(l4)] * 8
    scratch += [vmem(ny, 8, LANES)] * 2
    copies = 10 * 8 + 3 * 6
    scratch += [
        pltpu.SemaphoreType.DMA((copies,)),
        pltpu.SemaphoreType.DMA((copies,)),
        pltpu.SemaphoreType.DMA((4,)),
        pltpu.SemaphoreType.DMA((4,)),
        pltpu.SemaphoreType.DMA((8,)),
    ]

    def step(guess, right_side, coefficient):
        return pl.pallas_call(
            functools.partial(kernel, nx, ny, (l0, l1, l2, l3, l4)),
            out_shape=pltpu.VMEM(guess.shape, F32),
            in_specs=[pl.BlockSpec(memory_space=pl.ANY)] * 3,
            out_specs=pl.BlockSpec(memory_space=pltpu.VMEM),
            scratch_shapes=scratch,
            compiler_params=pltpu.CompilerParams(collective_id=0, has_side_effects=True),
        )(guess, right_side, coefficient)

    spec = P("gx", "gy", None)
    return jax.shard_map(
        step, mesh=mesh, in_specs=(spec, spec, spec), out_specs=spec, check_vma=False
    )
```

```python
import functools

import jax
import jax.numpy as jnp
from jax import lax
from jax.experimental import pallas as pl
from jax.experimental.pallas import tpu as pltpu
from jax.sharding import PartitionSpec as P

MESH = pl.DeviceIdType.MESH
F32 = jnp.float32
RELAX = 0.7
CHEB = 8
THETA = 1.04
DELTA = 0.96
LANES = 128
REGISTERS = 120


def iota(shape, dim):
    return lax.broadcasted_iota(jnp.int32, shape, dim)


class Level:
    def __init__(self, nh, nz, halo, bx, by, rows, total_x, total_y):
        self.nh, self.nz, self.halo, self.bx, self.by = nh, nz, halo, bx, by
        self.rows, self.total_x, self.total_y = rows, total_x, total_y
        self.width = bx + 2 * halo

    def ext(self):
        return pltpu.VMEM((self.width, self.nh, self.rows, LANES), F32)

    def own(self):
        return pltpu.VMEM((self.bx, self.nh, self.by, LANES), F32)


def z_sum(level, v):
    lane = iota(v.shape, 3)
    up, down = pltpu.roll(v, 1, 3), pltpu.roll(v, LANES - 1, 3)
    if level.nz >= LANES:
        none = jnp.zeros_like(v[:, :1])
        below = jnp.concatenate([none, up[:, :1]], 1) if level.nh == 2 else none
        above = jnp.concatenate([down[:, 1:], none], 1) if level.nh == 2 else none
        up = jnp.where(lane == 0, below, up)
        down = jnp.where(lane == LANES - 1, above, down)
    return up + down


def block(ref, x0, r0, n):
    return ref[pl.ds(x0, 1), :, pl.ds(r0, n), :]


def couple(level, v_ref, c_ref, x0, r0, n):
    v, c = block(v_ref, x0, r0, n), block(c_ref, x0, r0, n)
    sv, su = z_sum(level, v), z_sum(level, c * v)
    for dx, dr in ((-1, 0), (1, 0), (0, -1), (0, 1)):
        near = block(v_ref, x0 + dx, r0 + dr, n)
        sv = sv + near
        su = su + near * block(c_ref, x0 + dx, r0 + dr, n)
    return v, c * sv + su


def tiles(r0, n, most=16):
    return tuple((r, min(most, r0 + n - r)) for r in range(r0, r0 + n, most))


def loop(count, chunk, body):
    steps = count // chunk
    assert steps * chunk == count
    if steps == 1:
        body(0)
    else:
        lax.fori_loop(0, steps, lambda k, _: (body(k * chunk), 0)[1], 0)


def over(level, span, rows, body):
    lo, hi = span
    each = level.nh * sum(n for _, n in rows) // 8
    most = max(1, REGISTERS // each)
    chunk = max(c for c in range(1, hi - lo + 1) if (hi - lo) % c == 0 and c <= most)

    def several(k):
        for i in range(chunk):
            for r, n in rows:
                body(level.halo + lo + k + i, r, n)

    loop(hi - lo, chunk, several)


def sweep(level, src, dst, c, g, b, span, rows, put=None):
    def body(x0, r, n):
        v, t = couple(level, src, c, x0, r, n)
        new = (1.0 - RELAX) * v + block(g, x0, r, n) * (t + block(b, x0, r, n))
        if put is None:
            dst[pl.ds(x0, 1), :, pl.ds(r, n), :] = new
        else:
            put(x0, r, n, new)

    over(level, span, rows, body)


def first_sweep(level, dst, g, b, span, rows):
    def body(x0, r, n):
        dst[pl.ds(x0, 1), :, pl.ds(r, n), :] = block(g, x0, r, n) * block(b, x0, r, n)

    over(level, span, rows, body)


def setup(level, c, g, d, span, rows, base_x, base_y):
    def body(x0, r, n):
        mid = block(c, x0, r, n)
        px = base_x + x0 - level.halo
        py = iota(mid.shape, 2) + jnp.where(
            (px >= 0) & (px < level.total_x), base_y + r - 8, -1000
        )
        mask = (py >= 0) & (py < level.total_y)
        if level.nz < LANES:
            mask = mask & (iota(mid.shape, 3) < level.nz)
        total = 6.0 * mid + z_sum(level, mid)
        for dx, dr in ((-1, 0), (1, 0), (0, -1), (0, 1)):
            total = total + block(c, x0 + dx, r + dr, n)
        g[pl.ds(x0, 1), :, pl.ds(r, n), :] = jnp.where(
            mask, RELAX / jnp.where(mask, total, 1.0), 0.0
        )
        d[pl.ds(x0, 1), :, pl.ds(r, n), :] = total

    over(level, span, rows, body)


def residual_pairs(level, v_ref, c, b, d, s, keep):
    def body(k):
        for r, n in tiles(8, level.by):
            total = None
            for x0 in (level.halo + 2 * k, level.halo + 2 * k + 1):
                v, t = couple(level, v_ref, c, x0, r, n)
                part = block(b, x0, r, n) + t - block(d, x0, r, n) * v
                keep[pl.ds(x0, 1), :, pl.ds(r, n), :] = v
                total = part if total is None else total + part
            s[pl.ds(k, 1), :, pl.ds(r - 8, n), :] = total

    loop_pieces(level.bx // 2, 4, body)


def field_pairs(level, ref, s):
    def body(k):
        x0 = level.halo + 2 * k
        s[pl.ds(k, 1)] = block(ref, x0, 8, level.by) + block(ref, x0 + 1, 8, level.by)

    loop_pieces(level.bx // 2, 4, body)


def dot(a, m):
    return jnp.dot(a, m, precision=lax.Precision.HIGHEST, preferred_element_type=F32)


def halve(level, s, weight):
    rows = level.by // 2
    count = level.bx // 2
    row, col = iota((LANES, LANES), 0), iota((LANES, LANES), 1)
    total = None
    for h in range(level.nh):
        pick = (lax.shift_right_logical(row, 1) + h * 64 == col) & (row < level.nz)
        m = jnp.where(pick, weight, 0.0).astype(F32)
        a = s[:, h, pl.ds(0, rows, stride=2), :] + s[:, h, pl.ds(1, rows, stride=2), :]
        part = dot(a.reshape(count * rows, LANES), m)
        total = part if total is None else total + part
    return total.reshape(count, rows, LANES)


def prolong(level, e, ex, er, count, ne, pe, base, dst, x0):
    row, col = iota((LANES, LANES), 0), iota((LANES, LANES), 1)
    coarse = e[pl.ds(ex, count), 0, pl.ds(er, ne), :].reshape(count * ne, LANES)
    for h in range(level.nh):
        m = jnp.where(row == lax.shift_right_logical(col, 1) + h * 64, 1.0, 0.0).astype(F32)
        pe[:, h, :, :] = dot(coarse, m).reshape(count, ne, LANES)


def add_prolonged(level, pe, base, dst, x0, r0, count, ne, er=0):
    def body(k):
        for h in range(level.nh):
            fine = pe[k, h, pl.ds(er, ne), :]
            for dx in range(2):
                for dr in range(2):
                    at = (x0 + 2 * k + dx, h, pl.ds(r0 + dr, ne, stride=2), slice(None))
                    dst[at] = base[at] + fine

    loop(count, 1, body)


class Packed:
    def __init__(self, count, pad, rows, width, groups):
        self.count, self.pad, self.rows, self.width, self.groups = count, pad, rows, width, groups

    def ext(self):
        return pltpu.VMEM((self.count + 2 * self.pad, 8, LANES), F32)

    def own(self, more=0):
        return pltpu.VMEM((self.count + more, 8, LANES), F32)


def packed_near(p, v):
    row = iota(v.shape, 1) & (p.rows - 1)
    after, before = pltpu.roll(v, 7, 1), pltpu.roll(v, 1, 1)
    return (
        jnp.where(row == p.rows - 1, pltpu.roll(after, LANES - p.width, 2), after),
        jnp.where(row == 0, pltpu.roll(before, p.width, 2), before),
        pltpu.roll(v, LANES - 1, 2),
        pltpu.roll(v, 1, 2),
    )


def packed_setup(p, c, w, wx, g, d, scale):
    def body(k):
        at = pl.ds(p.pad + k, 1)
        mid = c[at]
        lane, row = iota(mid.shape, 2), iota(mid.shape, 1) & (p.rows - 1)
        valid = lane < p.width * p.groups
        z = lane & (p.width - 1)
        inside = (
            (row < p.rows - 1) | (lane < p.width * (p.groups - 1)),
            (row > 0) | (lane >= p.width),
            z < p.width - 1,
            z > 0,
        )
        below = c[pl.ds(p.pad + k - 1, 1)]
        total = 6.0 * mid + below + c[pl.ds(p.pad + k + 1, 1)]
        wx[pl.ds(k, 1)] = mid + below
        for ref, near, ok in zip(w, packed_near(p, mid), inside):
            near = jnp.where(valid & ok, near, 0.0)
            ref[pl.ds(k, 1)] = jnp.where(valid & ok, mid + near, 0.0)
            total = total + near
        g[pl.ds(k, 1)] = jnp.where(valid, scale / jnp.where(valid, total, 1.0), 0.0)
        d[pl.ds(k, 1)] = total

    loop_pieces(p.count, 4, body)
    wx[pl.ds(p.count, 1)] = c[pl.ds(p.pad + p.count - 1, 1)]


def packed_couple(p, v_ref, w, wx, k):
    v = v_ref[pl.ds(p.pad + k, 1)]
    t = wx[pl.ds(k, 1)] * v_ref[pl.ds(p.pad + k - 1, 1)]
    t = t + wx[pl.ds(k + 1, 1)] * v_ref[pl.ds(p.pad + k + 1, 1)]
    parts = [ref[pl.ds(k, 1)] * near for ref, near in zip(w, packed_near(p, v))]
    return v, t + ((parts[0] + parts[1]) + (parts[2] + parts[3]))


def loop_pieces(count, chunk, body):
    def several(k):
        for i in range(chunk):
            body(k + i)

    loop(count, chunk, several)


def packed_sweep(p, src, dst, w, wx, g, b, b_pad):
    def body(k):
        v, t = packed_couple(p, src, w, wx, k)
        new = (1.0 - RELAX) * v + g[pl.ds(k, 1)] * (t + b[pl.ds(b_pad + k, 1)])
        dst[pl.ds(p.pad + k, 1)] = new

    loop_pieces(p.count, 16, body)


def packed_halve(s, weight):
    row, col = iota((LANES, LANES), 0), iota((LANES, LANES), 1)
    m = jnp.where(lax.shift_right_logical(row, 1) == col, weight, 0.0).astype(F32)
    a = s[:, pl.ds(0, 8, stride=2), :] + s[:, pl.ds(1, 8, stride=2), :]
    return dot(a.reshape(s.shape[0] * 8, LANES), m).reshape(s.shape[0], 8, LANES)


class Copy:
    def __init__(self, src, dst, target, sends, receives, sems):
        send_sem, recv_sem, index = sems
        self.copy = pltpu.make_async_remote_copy(
            src_ref=src,
            dst_ref=dst,
            send_sem=send_sem.at[index],
            recv_sem=recv_sem.at[index],
            device_id=target,
            device_id_type=MESH,
        )
        self.sends, self.receives = sends, receives

    def start(self):
        pl.when(self.sends)(lambda: self.copy.start())

    def arrive(self):
        pl.when(self.receives)(lambda: self.copy.wait_recv())

    def leave(self):
        pl.when(self.sends)(lambda: self.copy.wait_send())


def kernel(nx, ny, levels, guess, rhs, coef, out, *scratch):
    l0, l1, l2, l3, l4 = levels
    names = iter(scratch)
    take = lambda k: [next(names) for _ in range(k)]
    va0, vb0, vc0, c0, b0, g0, d0, ve0, vf0, s0, pe0 = take(11)
    va1, vb1, vc1, c1, b1, g1, d1, s1, pe1 = take(9)
    va2, vb2, vc2, c2, b2, g2, d2, s2, pe2 = take(9)
    va3, vb3, c3, b3, wx3, g3, d3, s3, t3 = take(9)
    w3 = take(4)
    va4, vb4, c4, wx4, q4, d4, res4, e4 = take(8)
    w4 = take(4)
    pc, pb = take(2)
    send_sem, recv_sem, gather_send, gather_recv, local_sem = take(5)

    gx, gy = lax.axis_index("gx"), lax.axis_index("gy")
    counter = iter(range(1000))

    def sems():
        return send_sem, recv_sem, next(counter)

    loads = []
    for i, (src, dst) in enumerate(((coef, c0), (guess, va0), (rhs, b0))):
        for h in range(2):
            loads.append(
                pltpu.make_async_copy(
                    src.at[:, :, h * LANES : (h + 1) * LANES],
                    dst.at[l0.halo : l0.halo + l0.bx, h, 8 : 8 + l0.by, :],
                    local_sem.at[2 * i + h],
                )
            )
    for copy in loads:
        copy.start()

    barrier = pltpu.get_barrier_semaphore()
    for k in range(1, nx):
        pl.semaphore_signal(
            barrier, inc=1, device_id=(lax.rem(gx + k, nx), gy), device_id_type=MESH
        )
    for k in range(1, ny):
        pl.semaphore_signal(
            barrier, inc=1, device_id=(gx, lax.rem(gy + k, ny)), device_id_type=MESH
        )

    for dx in (1, nx - 1):
        for dy in (1, ny - 1):
            diagonal = (lax.rem(gx + dx, nx), lax.rem(gy + dy, ny))
            pl.semaphore_signal(barrier, inc=1, device_id=diagonal, device_id_type=MESH)

    everything = []

    class Exchange:
        def __init__(self, level, ref, wide, reach=1, faces=True, direct=False):
            self.direct = direct
            lo, bx, by = level.halo, level.bx, level.by
            if reach == 1:
                up = ((lo + bx - wide, lo - wide), (lo, lo + bx))
            else:
                up = ((lo + 2 * bx - lo, 0), (lo, lo + 2 * bx))
            self.x, self.y, self.corners = [], [], []
            own = pl.ds(8, by)
            for sign, (src, dst) in zip((1, -1), up):
                there, back = gx + sign * reach, gx - sign * reach
                ok = lambda p: (p >= 0) & (p < nx)
                self.x.append(
                    Copy(
                        ref.at[pl.ds(src, wide), :, own, :],
                        ref.at[pl.ds(dst, wide), :, own, :],
                        (there, gy),
                        ok(there),
                        ok(back),
                        sems(),
                    )
                )
            rows = 4 if level.nh == 2 else 8
            sides = ((1, 8 + by - rows, 8 - rows), (-1, 8, 8 + by))
            inside_x, inside_y = (lambda p: (p >= 0) & (p < nx)), (lambda p: (p >= 0) & (p < ny))
            for sign, src, dst in sides:
                there, back = gy + sign, gy - sign
                sends, receives = inside_y(there), inside_y(back)

                def strip(start, count, row):
                    return ref.at[pl.ds(start, count), :, pl.ds(row, rows), :]

                if faces:
                    self.y.append(
                        Copy(
                            strip(lo, bx, src),
                            strip(lo, bx, dst),
                            (gx, there),
                            sends,
                            receives,
                            sems(),
                        )
                    )
                for sign_x, (src_x, dst_x) in zip((1, -1), up):
                    far, near = gx + sign_x * reach, gx - sign_x * reach
                    have = receives & inside_x(near)
                    self.corners.append(
                        Copy(
                            strip(src_x if direct else dst_x, wide, src),
                            strip(dst_x, wide, dst),
                            (far if direct else gx, there),
                            sends & inside_x(far if direct else near),
                            have,
                            sems(),
                        )
                    )
            everything.append(self)

        def send(self):
            for copy in self.x + self.y + (self.corners if self.direct else []):
                copy.start()

        def forward(self):
            for copy in self.x:
                copy.arrive()
            for copy in [] if self.direct else self.corners:
                copy.start()

        def finish(self):
            for copy in self.y + self.corners:
                copy.arrive()

        def leave(self):
            everything.remove(self)
            for copy in self.x + self.y + self.corners:
                copy.leave()

    class Gather:
        def __init__(self, rows, full, pad, index):
            self.rows, self.full, self.at = rows, full, pl.ds(pad + 2 * gx, 2)
            self.first = [
                self.copy(rows.at[gy], index, (gx, lax.rem(gy + k, ny))) for k in range(1, ny)
            ]
            mine = full.at[self.at]
            self.second = [
                self.copy(mine, index + 1, (lax.rem(gx + k, nx), gy)) for k in range(1, nx)
            ]
            self.first_all = self.copy(rows.at[pl.ds(0, ny - 1)], index, (gx, gy))
            self.second_all = self.copy(full.at[pl.ds(0, 2 * nx - 2)], index + 1, (gx, gy))

        def copy(self, ref, index, target):
            return pltpu.make_async_remote_copy(
                src_ref=ref,
                dst_ref=ref,
                send_sem=gather_send.at[index],
                recv_sem=gather_recv.at[index],
                device_id=target,
                device_id_type=MESH,
            )

        def send(self, tile):
            self.rows[gy] = tile
            for copy in self.first:
                copy.start()

        def forward(self):
            self.first_all.wait_recv()
            even, odd = self.rows[0], self.rows[1]
            for k in range(2, ny, 2):
                even, odd = even + self.rows[k], odd + self.rows[k + 1]
            low = iota(even.shape, 0) < 4
            layers = (
                jnp.where(low, even, pltpu.roll(odd, 4, 0)),
                jnp.where(low, pltpu.roll(even, 4, 0), odd),
            )
            for i in range(2):
                self.full[self.at.start + i] = layers[i]
            for copy in self.second:
                copy.start()

        def finish(self):
            self.second_all.wait_recv()

        def leave(self):
            self.first_all.wait_send()
            self.second_all.wait_send()

    x_v0, x_c0, x_b0 = Exchange(l0, va0, 4), Exchange(l0, c0, 4), Exchange(l0, b0, 3)
    x_k0 = Exchange(l0, vc0, 3)
    x_c1, x_b1, x_k1 = Exchange(l1, c1, 5), Exchange(l1, b1, 4, direct=True), Exchange(l1, vc1, 5)
    x_c2, x_k2 = Exchange(l2, c2, 4), Exchange(l2, vc2, 4)
    x_b2 = Exchange(l2, b2, 4, direct=True)
    f_c2, f_b2, f_k2 = (Exchange(l2, ref, 2, 2, False) for ref in (c2, b2, vc2))
    g_c3, g_b3 = Gather(pc, c3, l3.pad, 0), Gather(pb, b3, l3.pad, 2)

    for copy in loads:
        copy.wait()
    pl.semaphore_wait(barrier, nx + ny + 2)

    x_c0.send()
    x_v0.send()

    def double(k):
        for h in range(2):
            own = (pl.ds(l0.halo + k, 1), h, pl.ds(8, l0.by), slice(None))
            b0[own] = 2.0 * b0[own]

    loop_pieces(l0.bx, 4, double)
    x_b0.send()

    def clear(level, refs, far):
        lo, bx, by = level.halo, level.bx, level.by

        def layers(start, count):
            for ref in refs:
                ref[pl.ds(start, count)] = jnp.zeros((count,) + ref.shape[1:], F32)

        near = min(lo, bx)
        pl.when(gx == 0)(lambda: layers(lo - near, near))
        pl.when(gx == nx - 1)(lambda: layers(lo + bx, near))
        if far:
            pl.when(gx < 2)(lambda: layers(0, lo - bx))
            pl.when(gx >= nx - 2)(lambda: layers(lo + 2 * bx, lo - bx))

        def rows(start, count):
            for ref in refs:
                for h in range(level.nh):
                    ref[:, h, pl.ds(start, count), :] = jnp.zeros((level.width, count, LANES), F32)

        pl.when(gy == 0)(lambda: rows(0, 8))
        pl.when(gy == ny - 1)(lambda: rows(8 + by, 8))

    clear(l0, (va0, c0, b0, vc0), False)
    clear(l1, (c1, b1, vc1), False)
    clear(l2, (c2, b2, vc2), True)
    for ref in (va3, vb3, c3, va4, vb4, c4):
        pad = 1 if ref.shape[0] == nx + 2 else l3.pad
        for start in (0, ref.shape[0] - pad):
            ref[pl.ds(start, pad)] = jnp.zeros((pad, 8, LANES), F32)
    for ref in (va1, vb1, va2, vb2):
        for h in range(ref.shape[1]):
            for r in range(0, ref.shape[2], 8):
                ref[:, h, pl.ds(r, 8), :] = jnp.zeros((ref.shape[0], 8, LANES), F32)

    lane_base = 32 * lax.shift_right_logical(gy, 1)

    def tile_of(s, weight):
        row, col = iota((LANES, LANES), 0), iota((LANES, LANES), 1)
        pick = (lax.shift_right_logical(row, 1) + lane_base == col) & (row < l2.nz)
        m = jnp.where(pick, weight, 0.0).astype(F32)
        a = s[pl.ds(0, 8, stride=2), :] + s[pl.ds(1, 8, stride=2), :]
        return dot(a, m)

    field_pairs(l0, c0, s0)
    c1[l1.halo : l1.halo + l1.bx, 0, 8 : 8 + l1.by, :] = halve(l0, s0, 0.125)
    x_c1.send()
    field_pairs(l1, c1, s1)
    c2[l2.halo : l2.halo + l2.bx, 0, 8 : 8 + l2.by, :] = halve(l1, s1, 0.125)
    x_c2.send()
    f_c2.send()
    for k in range(2):
        s2[pl.ds(8 * k, 8), :] = (
            c2[l2.halo + 2 * k, 0, pl.ds(8, 8), :] + c2[l2.halo + 2 * k + 1, 0, pl.ds(8, 8), :]
        )
    g_c3.send(tile_of(s2, 0.125))

    bx0, by0 = gx * l0.bx, gy * l0.by
    chain = (va0, vb0, ve0, vf0)
    inner = tiles(12, 24)
    setup(l0, c0, g0, d0, (1, l0.bx - 1), inner, bx0, by0)
    for k in range(1, 4):
        sweep(l0, chain[k - 1], chain[k], c0, g0, b0, (k, l0.bx - k), inner)
    x_c0.forward()
    for span in ((-3, 1), (l0.bx - 1, l0.bx + 3)):
        setup(l0, c0, g0, d0, span, inner, bx0, by0)
    x_v0.forward()
    x_b0.forward()
    for k in range(1, 4):
        for span in ((k - 4, k), (l0.bx - k, l0.bx + 4 - k)):
            sweep(l0, chain[k - 1], chain[k], c0, g0, b0, span, inner)
    for exchange in (x_c0, x_v0, x_b0):
        exchange.finish()
    g_c3.forward()
    for exchange in (x_c1, x_c2, f_c2):
        exchange.forward()
    setup(l0, c0, g0, d0, (-3, l0.bx + 3), ((4, 8), (36, 8)), bx0, by0)
    for k in range(1, 4):
        span = (k - 4, l0.bx + 4 - k)
        sweep(l0, chain[k - 1], chain[k], c0, g0, b0, span, ((3 + k, 8), (37 - k, 8)))
    residual_pairs(l0, vf0, c0, b0, d0, s0, vc0)
    b1[l1.halo : l1.halo + l1.bx, 0, 8 : 8 + l1.by, :] = halve(l0, s0, 0.5)
    x_b1.send()
    x_k0.send()
    for exchange in (x_c1, x_c2, f_c2):
        exchange.finish()
    rows1, rows2 = tiles(4, 24, 24), tiles(2, 24, 24)
    setup(l1, c1, g1, d1, (-4, l1.bx + 4), rows1, gx * l1.bx, gy * l1.by)
    setup(l2, c2, g2, d2, (-5, l2.bx + 5), rows2, gx * l2.bx, gy * l2.by)
    x_b1.forward()
    x_b1.finish()
    first_sweep(l1, va1, g1, b1, (-3, l1.bx + 3), rows1)
    sweep(l1, va1, vb1, c1, g1, b1, (-2, l1.bx + 2), rows1)
    sweep(l1, vb1, va1, c1, g1, b1, (-1, l1.bx + 1), rows1)
    residual_pairs(l1, va1, c1, b1, d1, s1, vc1)
    b2[l2.halo : l2.halo + l2.bx, 0, 8 : 8 + l2.by, :] = halve(l1, s1, 0.5)
    x_b2.send()
    f_b2.send()
    x_k1.send()

    def pairs_of(ref):
        for k in range(nx):
            total = ref[l3.pad + 2 * k] + ref[l3.pad + 2 * k + 1]
            s3[k, pl.ds(0, 8), :] = total
            s3[k, pl.ds(8, 8), :] = total

    g_c3.finish()
    packed_setup(l3, c3, w3, wx3, g3, d3, RELAX)
    pairs_of(c3)
    c4[pl.ds(l4.pad, nx)] = packed_halve(s3, 0.125)
    packed_setup(l4, c4, w4, wx4, q4, d4, 1.0)

    x_b2.forward()
    x_b2.finish()
    first_sweep(l2, va2, g2, b2, (-3, l2.bx + 3), rows2)
    sweep(l2, va2, vb2, c2, g2, b2, (-2, l2.bx + 2), rows2)
    sweep(l2, vb2, va2, c2, g2, b2, (-1, l2.bx + 1), rows2)
    for k in range(2):
        total = None
        for x0 in (l2.halo + 2 * k, l2.halo + 2 * k + 1):
            v, t = couple(l2, va2, c2, x0, 8, 8)
            part = block(b2, x0, 8, 8) + t - block(d2, x0, 8, 8) * v
            vc2[pl.ds(x0, 1), :, pl.ds(8, 8), :] = v
            total = part if total is None else total + part
        s2[pl.ds(8 * k, 8), :] = total[0, 0]
    g_b3.send(tile_of(s2, 0.5))
    x_k2.send()
    f_k2.send()
    x_k0.forward()
    x_k1.forward()
    f_b2.forward()
    g_b3.forward()
    x_k2.forward()
    f_k2.forward()
    g_b3.finish()
    for k in range(l3.count):
        va3[l3.pad + k] = g3[k] * b3[l3.pad + k]
    packed_sweep(l3, va3, vb3, w3, wx3, g3, b3, l3.pad)
    packed_sweep(l3, vb3, va3, w3, wx3, g3, b3, l3.pad)

    def residual3(k):
        total = None
        for i in (2 * k, 2 * k + 1):
            v, t = packed_couple(l3, va3, w3, wx3, i)
            r = b3[pl.ds(l3.pad + i, 1)] + t - d3[pl.ds(i, 1)] * v
            total = r if total is None else total + r
        s3[pl.ds(k, 1), pl.ds(0, 8), :] = total
        s3[pl.ds(k, 1), pl.ds(8, 8), :] = total

    loop_pieces(nx, 2, residual3)
    res4[...] = packed_halve(s3, 0.5)

    sigma = THETA / DELTA
    rho = 1.0 / sigma
    for k in range(nx):
        direction = res4[k] * q4[k] * (1.0 / THETA)
        e4[k] = direction
        va4[l4.pad + k] = direction
    src, dst = va4, vb4
    for step in range(CHEB - 1):
        rho_new = 1.0 / (2.0 * sigma - rho)
        for k in range(nx):
            at = pl.ds(k, 1)
            v, t = packed_couple(l4, src, w4, wx4, k)
            r = res4[at] - (d4[at] * v - t)
            direction = (rho_new * rho) * v + (2.0 * rho_new / DELTA) * (r * q4[at])
            res4[at] = r
            e4[at] = e4[at] + direction
            dst[pl.ds(l4.pad + k, 1)] = direction
        rho = rho_new
        src, dst = dst, src

    row, col = iota((LANES, LANES), 0), iota((LANES, LANES), 1)
    spread = jnp.where(row == lax.shift_right_logical(col, 1), 1.0, 0.0).astype(F32)
    fine = dot(e4[...].reshape(nx * 8, LANES), spread).reshape(nx, 8, LANES)
    for dr in range(2):
        t3[:, pl.ds(dr, 4, stride=2), :] = fine[:, 0:4, :]
    for k in range(l3.count):
        vb3[l3.pad + k] = va3[l3.pad + k] + t3[k // 2]
    packed_sweep(l3, vb3, va3, w3, wx3, g3, b3, l3.pad)
    packed_sweep(l3, va3, vb3, w3, wx3, g3, b3, l3.pad)
    packed_sweep(l3, vb3, va3, w3, wx3, g3, b3, l3.pad)

    f_b2.finish()
    x_k2.finish()
    f_k2.finish()
    group = lax.shift_right_logical(gy, 1) - 1
    e3 = va3[pl.ds(l3.pad - 3 + 2 * gx, 8)].reshape(64, LANES)
    for q in range(3):
        pick = (row == lax.shift_right_logical(col, 1) + 32 * (group + q)) & (col < l2.nz)
        part = dot(e3, jnp.where(pick, 1.0, 0.0).astype(F32))
        pe2[:, 0, pl.ds(8 * q, 8), :] = part.reshape(8, 8, LANES)
    add_prolonged(l2, pe2, vc2, va2, 0, 0, 8, 16, 4 * (gy & 1) + 4)
    sweep(l2, va2, vb2, c2, g2, b2, (-5, l2.bx + 5), rows2)
    sweep(l2, vb2, va2, c2, g2, b2, (-4, l2.bx + 4), rows2)
    sweep(l2, va2, vb2, c2, g2, b2, (-3, l2.bx + 3), rows2)

    x_k1.finish()
    prolong(l1, vb2, 3, 4, 10, 16, pe1, None, None, 0)
    add_prolonged(l1, pe1, vc1, va1, 0, 0, 10, 16)
    sweep(l1, va1, vb1, c1, g1, b1, (-4, l1.bx + 4), rows1)
    sweep(l1, vb1, va1, c1, g1, b1, (-3, l1.bx + 3), rows1)
    sweep(l1, va1, vb1, c1, g1, b1, (-2, l1.bx + 2), rows1)

    x_k0.finish()
    prolong(l0, vb1, 4, 4, 12, 24, pe0, None, None, 0)
    x_v0.leave()
    add_prolonged(l0, pe0, vc0, va0, 0, 0, 12, 24)
    def put(x0, r, n, new):
        for h in range(2):
            at = (pl.ds(x0 - l0.halo, 1), pl.ds(r - 8, n), slice(h * LANES, (h + 1) * LANES))
            out[at] = new[:, h]

    sweep(l0, va0, vb0, c0, g0, b0, (-2, l0.bx + 2), tiles(4, 40))
    sweep(l0, vb0, ve0, c0, g0, b0, (-1, l0.bx + 1), tiles(4, 40))
    sweep(l0, ve0, None, c0, g0, b0, (0, l0.bx), tiles(8, 32), put)
    for exchange in list(everything):
        exchange.leave()
    g_c3.leave()
    g_b3.leave()


def solution(mesh):
    nx, ny = mesh.shape["gx"], mesh.shape["gy"]
    l0 = Level(2, 256, 4, 16, 32, 48, 16 * nx, 32 * ny)
    l1 = Level(1, 128, 6, 8, 16, 32, 8 * nx, 16 * ny)
    l2 = Level(1, 64, 6, 4, 8, 32, 4 * nx, 8 * ny)
    l3 = Packed(2 * nx, 4, 8, 32, ny // 2)
    l4 = Packed(nx, 1, 4, 16, ny // 2)

    def vmem(*shape):
        return pltpu.VMEM(shape, F32)

    e, o = (lambda l: l.ext()), (lambda l: l.own())
    scratch = [e(l0)] * 9 + [vmem(8, 2, 32, LANES), vmem(12, 2, 24, LANES)]
    scratch += [e(l1)] * 7 + [vmem(4, 1, 16, LANES), vmem(10, 1, 16, LANES)]
    scratch += [e(l2)] * 7 + [vmem(16, LANES), vmem(8, 1, 24, LANES)]
    scratch += [e(l3)] * 4 + [l3.own(1), o(l3), o(l3), vmem(nx, 16, LANES), vmem(nx, 8, LANES)]
    scratch += [o(l3)] * 4
    scratch += [e(l4)] * 3 + [l4.own(1)] + [o(l4)] * 8
    scratch += [vmem(ny, 8, LANES)] * 2
    copies = 10 * 8 + 3 * 6
    scratch += [
        pltpu.SemaphoreType.DMA((copies,)),
        pltpu.SemaphoreType.DMA((copies,)),
        pltpu.SemaphoreType.DMA((4,)),
        pltpu.SemaphoreType.DMA((4,)),
        pltpu.SemaphoreType.DMA((8,)),
    ]

    def step(guess, right_side, coefficient):
        return pl.pallas_call(
            functools.partial(kernel, nx, ny, (l0, l1, l2, l3, l4)),
            out_shape=pltpu.VMEM(guess.shape, F32),
            in_specs=[pl.BlockSpec(memory_space=pl.ANY)] * 3,
            out_specs=pl.BlockSpec(memory_space=pltpu.VMEM),
            scratch_shapes=scratch,
            compiler_params=pltpu.CompilerParams(collective_id=0, has_side_effects=True),
        )(guess, right_side, coefficient)

    spec = P("gx", "gy", None)
    return jax.shard_map(
        step, mesh=mesh, in_specs=(spec, spec, spec), out_specs=spec, check_vma=False
    )
```

```python
import functools

import jax
import jax.numpy as jnp
from jax import lax
from jax.experimental import pallas as pl
from jax.experimental.pallas import tpu as pltpu
from jax.sharding import PartitionSpec as P

MESH = pl.DeviceIdType.MESH
F32 = jnp.float32
RELAX = 0.7
CHEB = 8
THETA = 1.04
DELTA = 0.96
LANES = 128
REGISTERS = 120


def iota(shape, dim):
    return lax.broadcasted_iota(jnp.int32, shape, dim)


class Level:
    def __init__(self, nh, nz, halo, bx, by, rows, total_x, total_y):
        self.nh, self.nz, self.halo, self.bx, self.by = nh, nz, halo, bx, by
        self.rows, self.total_x, self.total_y = rows, total_x, total_y
        self.width = bx + 2 * halo

    def ext(self):
        return pltpu.VMEM((self.width, self.nh, self.rows, LANES), F32)

    def own(self):
        return pltpu.VMEM((self.bx, self.nh, self.by, LANES), F32)


def z_sum(level, v):
    lane = iota(v.shape, 3)
    up, down = pltpu.roll(v, 1, 3), pltpu.roll(v, LANES - 1, 3)
    if level.nz >= LANES:
        none = jnp.zeros_like(v[:, :1])
        below = jnp.concatenate([none, up[:, :1]], 1) if level.nh == 2 else none
        above = jnp.concatenate([down[:, 1:], none], 1) if level.nh == 2 else none
        up = jnp.where(lane == 0, below, up)
        down = jnp.where(lane == LANES - 1, above, down)
    return up + down


def block(ref, x0, r0, n):
    return ref[pl.ds(x0, 1), :, pl.ds(r0, n), :]


def couple(level, v_ref, c_ref, x0, r0, n):
    v, c = block(v_ref, x0, r0, n), block(c_ref, x0, r0, n)
    sv, su = z_sum(level, v), z_sum(level, c * v)
    for dx, dr in ((-1, 0), (1, 0), (0, -1), (0, 1)):
        near = block(v_ref, x0 + dx, r0 + dr, n)
        sv = sv + near
        su = su + near * block(c_ref, x0 + dx, r0 + dr, n)
    return v, c * sv + su


def tiles(r0, n, most=16):
    return tuple((r, min(most, r0 + n - r)) for r in range(r0, r0 + n, most))


def loop(count, chunk, body):
    steps = count // chunk
    assert steps * chunk == count
    if steps == 1:
        body(0)
    else:
        lax.fori_loop(0, steps, lambda k, _: (body(k * chunk), 0)[1], 0)


def over(level, span, rows, body):
    lo, hi = span
    each = level.nh * sum(n for _, n in rows) // 8
    most = max(1, REGISTERS // each)
    chunk = max(c for c in range(1, hi - lo + 1) if (hi - lo) % c == 0 and c <= most)

    def several(k):
        for i in range(chunk):
            for r, n in rows:
                body(level.halo + lo + k + i, r, n)

    loop(hi - lo, chunk, several)


def sweep(level, src, dst, c, g, b, span, rows, put=None):
    def body(x0, r, n):
        v, t = couple(level, src, c, x0, r, n)
        new = (1.0 - RELAX) * v + block(g, x0, r, n) * (t + block(b, x0, r, n))
        if put is None:
            dst[pl.ds(x0, 1), :, pl.ds(r, n), :] = new
        else:
            put(x0, r, n, new)

    over(level, span, rows, body)


def first_sweep(level, dst, g, b, span, rows):
    def body(x0, r, n):
        dst[pl.ds(x0, 1), :, pl.ds(r, n), :] = block(g, x0, r, n) * block(b, x0, r, n)

    over(level, span, rows, body)


def setup(level, c, g, d, span, rows, base_x, base_y):
    def body(x0, r, n):
        mid = block(c, x0, r, n)
        px = base_x + x0 - level.halo
        py = iota(mid.shape, 2) + jnp.where(
            (px >= 0) & (px < level.total_x), base_y + r - 8, -1000
        )
        mask = (py >= 0) & (py < level.total_y)
        if level.nz < LANES:
            mask = mask & (iota(mid.shape, 3) < level.nz)
        total = 6.0 * mid + z_sum(level, mid)
        for dx, dr in ((-1, 0), (1, 0), (0, -1), (0, 1)):
            total = total + block(c, x0 + dx, r + dr, n)
        g[pl.ds(x0, 1), :, pl.ds(r, n), :] = jnp.where(
            mask, RELAX / jnp.where(mask, total, 1.0), 0.0
        )
        d[pl.ds(x0, 1), :, pl.ds(r, n), :] = total

    over(level, span, rows, body)


def residual_pairs(level, v_ref, c, b, d, s, keep, span=None):
    lo, hi = span or (0, level.bx // 2)

    def body(i):
        k = lo + i
        for r, n in tiles(8, level.by):
            total = None
            for x0 in (level.halo + 2 * k, level.halo + 2 * k + 1):
                v, t = couple(level, v_ref, c, x0, r, n)
                part = block(b, x0, r, n) + t - block(d, x0, r, n) * v
                keep[pl.ds(x0, 1), :, pl.ds(r, n), :] = v
                total = part if total is None else total + part
            s[pl.ds(k, 1), :, pl.ds(r - 8, n), :] = total

    count = hi - lo
    loop_pieces(count, max(i for i in (1, 2, 3, 4) if count % i == 0), body)


def field_pairs(level, ref, s):
    def body(k):
        x0 = level.halo + 2 * k
        s[pl.ds(k, 1)] = block(ref, x0, 8, level.by) + block(ref, x0 + 1, 8, level.by)

    loop_pieces(level.bx // 2, 4, body)


def dot(a, m):
    return jnp.dot(a, m, precision=lax.Precision.HIGHEST, preferred_element_type=F32)


def halve(level, s, weight):
    rows = level.by // 2
    count = level.bx // 2
    row, col = iota((LANES, LANES), 0), iota((LANES, LANES), 1)
    total = None
    for h in range(level.nh):
        pick = (lax.shift_right_logical(row, 1) + h * 64 == col) & (row < level.nz)
        m = jnp.where(pick, weight, 0.0).astype(F32)
        a = s[:, h, pl.ds(0, rows, stride=2), :] + s[:, h, pl.ds(1, rows, stride=2), :]
        part = dot(a.reshape(count * rows, LANES), m)
        total = part if total is None else total + part
    return total.reshape(count, rows, LANES)


def prolong(level, e, ex, er, count, ne, pe, base, dst, x0):
    row, col = iota((LANES, LANES), 0), iota((LANES, LANES), 1)
    coarse = e[pl.ds(ex, count), 0, pl.ds(er, ne), :].reshape(count * ne, LANES)
    for h in range(level.nh):
        m = jnp.where(row == lax.shift_right_logical(col, 1) + h * 64, 1.0, 0.0).astype(F32)
        pe[:, h, :, :] = dot(coarse, m).reshape(count, ne, LANES)


def add_prolonged(level, pe, base, dst, x0, r0, count, ne, er=0):
    def body(k):
        for h in range(level.nh):
            fine = pe[k, h, pl.ds(er, ne), :]
            for dx in range(2):
                for dr in range(2):
                    at = (x0 + 2 * k + dx, h, pl.ds(r0 + dr, ne, stride=2), slice(None))
                    dst[at] = base[at] + fine

    loop(count, 1, body)


class Packed:
    def __init__(self, count, pad, rows, width, groups):
        self.count, self.pad, self.rows, self.width, self.groups = count, pad, rows, width, groups

    def ext(self):
        return pltpu.VMEM((self.count + 2 * self.pad, 8, LANES), F32)

    def own(self, more=0):
        return pltpu.VMEM((self.count + more, 8, LANES), F32)


def packed_near(p, v):
    row = iota(v.shape, 1) & (p.rows - 1)
    after, before = pltpu.roll(v, 7, 1), pltpu.roll(v, 1, 1)
    return (
        jnp.where(row == p.rows - 1, pltpu.roll(after, LANES - p.width, 2), after),
        jnp.where(row == 0, pltpu.roll(before, p.width, 2), before),
        pltpu.roll(v, LANES - 1, 2),
        pltpu.roll(v, 1, 2),
    )


def packed_setup(p, c, w, wx, g, d, scale):
    def body(k):
        at = pl.ds(p.pad + k, 1)
        mid = c[at]
        lane, row = iota(mid.shape, 2), iota(mid.shape, 1) & (p.rows - 1)
        valid = lane < p.width * p.groups
        z = lane & (p.width - 1)
        inside = (
            (row < p.rows - 1) | (lane < p.width * (p.groups - 1)),
            (row > 0) | (lane >= p.width),
            z < p.width - 1,
            z > 0,
        )
        below = c[pl.ds(p.pad + k - 1, 1)]
        total = 6.0 * mid + below + c[pl.ds(p.pad + k + 1, 1)]
        wx[pl.ds(k, 1)] = mid + below
        for ref, near, ok in zip(w, packed_near(p, mid), inside):
            near = jnp.where(valid & ok, near, 0.0)
            ref[pl.ds(k, 1)] = jnp.where(valid & ok, mid + near, 0.0)
            total = total + near
        g[pl.ds(k, 1)] = jnp.where(valid, scale / jnp.where(valid, total, 1.0), 0.0)
        d[pl.ds(k, 1)] = total

    loop_pieces(p.count, 4, body)
    wx[pl.ds(p.count, 1)] = c[pl.ds(p.pad + p.count - 1, 1)]


def packed_couple(p, v_ref, w, wx, k):
    v = v_ref[pl.ds(p.pad + k, 1)]
    t = wx[pl.ds(k, 1)] * v_ref[pl.ds(p.pad + k - 1, 1)]
    t = t + wx[pl.ds(k + 1, 1)] * v_ref[pl.ds(p.pad + k + 1, 1)]
    parts = [ref[pl.ds(k, 1)] * near for ref, near in zip(w, packed_near(p, v))]
    return v, t + ((parts[0] + parts[1]) + (parts[2] + parts[3]))


def loop_pieces(count, chunk, body):
    def several(k):
        for i in range(chunk):
            body(k + i)

    loop(count, chunk, several)


def packed_sweep(p, src, dst, w, wx, g, b, b_pad):
    def body(k):
        v, t = packed_couple(p, src, w, wx, k)
        new = (1.0 - RELAX) * v + g[pl.ds(k, 1)] * (t + b[pl.ds(b_pad + k, 1)])
        dst[pl.ds(p.pad + k, 1)] = new

    loop_pieces(p.count, 16, body)


def packed_halve(s, weight):
    row, col = iota((LANES, LANES), 0), iota((LANES, LANES), 1)
    m = jnp.where(lax.shift_right_logical(row, 1) == col, weight, 0.0).astype(F32)
    a = s[:, pl.ds(0, 8, stride=2), :] + s[:, pl.ds(1, 8, stride=2), :]
    return dot(a.reshape(s.shape[0] * 8, LANES), m).reshape(s.shape[0], 8, LANES)


class Bundle:
    def __init__(self, pairs, target, sends, receives, tiles, unit, sems):
        send_sem, recv_sem, index = sems

        def copy(src, dst):
            return pltpu.make_async_remote_copy(
                src_ref=src,
                dst_ref=dst,
                send_sem=send_sem.at[index],
                recv_sem=recv_sem.at[index],
                device_id=target,
                device_id_type=MESH,
            )

        self.copies = [copy(src, dst) for src, dst in pairs]
        whole = unit.at[pl.ds(0, tiles)]
        self.whole = self.copies[0] if len(pairs) == 1 else copy(whole, whole)
        self.sends, self.receives = sends, receives

    def start(self):
        def go():
            for copy in self.copies:
                copy.start()

        pl.when(self.sends)(go)

    def arrive(self):
        pl.when(self.receives)(lambda: self.whole.wait_recv())

    def leave(self):
        pl.when(self.sends)(lambda: self.whole.wait_send())


def kernel(nx, ny, levels, guess, rhs, coef, out, *scratch):
    l0, l1, l2, l3, l4 = levels
    names = iter(scratch)
    take = lambda k: [next(names) for _ in range(k)]
    va0, vb0, vc0, c0, b0, g0, d0, ve0, vf0, s0, pe0 = take(11)
    va1, vb1, vc1, c1, b1, g1, d1, s1, pe1 = take(9)
    va2, vb2, vc2, c2, b2, g2, d2, s2, pe2 = take(9)
    va3, vb3, c3, b3, wx3, g3, d3, s3, t3 = take(9)
    w3 = take(4)
    va4, vb4, c4, wx4, q4, d4, res4, e4 = take(8)
    w4 = take(4)
    pc, pb, unit = take(3)
    send_sem, recv_sem, gather_send, gather_recv, local_sem = take(5)

    gx, gy = lax.axis_index("gx"), lax.axis_index("gy")
    counter = iter(range(1000))

    def sems():
        return send_sem, recv_sem, next(counter)

    loads = []
    for i, (src, dst) in enumerate(((coef, c0), (guess, va0), (rhs, b0))):
        for h in range(2):
            loads.append(
                pltpu.make_async_copy(
                    src.at[:, :, h * LANES : (h + 1) * LANES],
                    dst.at[l0.halo : l0.halo + l0.bx, h, 8 : 8 + l0.by, :],
                    local_sem.at[2 * i + h],
                )
            )
    for copy in loads:
        copy.start()

    barrier = pltpu.get_barrier_semaphore()
    for k in range(1, nx):
        pl.semaphore_signal(
            barrier, inc=1, device_id=(lax.rem(gx + k, nx), gy), device_id_type=MESH
        )
    for k in range(1, ny):
        pl.semaphore_signal(
            barrier, inc=1, device_id=(gx, lax.rem(gy + k, ny)), device_id_type=MESH
        )

    for dx in (1, nx - 1):
        for dy in (1, ny - 1):
            diagonal = (lax.rem(gx + dx, nx), lax.rem(gy + dy, ny))
            pl.semaphore_signal(barrier, inc=1, device_id=diagonal, device_id_type=MESH)

    everything = []

    class Exchange:
        def __init__(self, *parts, reach=1, direct=False):
            self.direct = direct
            on_x, on_y = (lambda p: (p >= 0) & (p < nx)), (lambda p: (p >= 0) & (p < ny))

            def layers(level, sign, a, b):
                lo, bx = level.halo, level.bx
                if sign > 0:
                    return lo + reach * bx - b, lo - b, b - a + 1
                return lo + a - 1 - (reach - 1) * bx, lo + bx + a - 1, b - a + 1

            def bundle(pairs, target, sends, receives):
                total = sum(
                    src.shape[0] * src.shape[1] * src.shape[2] for src, _ in pairs
                )
                return Bundle(pairs, target, sends, receives, total // 8, unit, sems())

            self.x, self.y, self.corners = [], [], []
            for sign in (1, -1):
                there, back = gx + sign * reach, gx - sign * reach
                pairs = []
                for level, src, dst, a, b, faces, corner in parts:
                    at, to, count = layers(level, sign, a, b)
                    own = pl.ds(8, level.by)
                    pairs.append(
                        (src.at[pl.ds(at, count), :, own, :], dst.at[pl.ds(to, count), :, own, :])
                    )
                self.x.append(bundle(pairs, (there, gy), on_x(there), on_x(back)))
            for sign in (1, -1):
                there, back = gy + sign, gy - sign
                pairs, corner_pairs = [], ([], [])
                for level, src, dst, a, b, faces, corner in parts:
                    deep = 4 if level.nh == 2 else 8
                    row = 8 + level.by - deep if sign > 0 else 8
                    to_row = 8 - deep if sign > 0 else 8 + level.by

                    def strips(ref, at, to, count):
                        return (
                            ref.at[pl.ds(at, count), :, pl.ds(row, deep), :],
                            dst.at[pl.ds(to, count), :, pl.ds(to_row, deep), :],
                        )

                    if faces:
                        pairs.append(strips(src, level.halo, level.halo, level.bx))
                    if corner:
                        for i, sign_x in enumerate((1, -1)):
                            at, to, count = layers(level, sign_x, *corner)
                            corner_pairs[i].append(strips(src if direct else dst, at if direct else to, to, count))
                if pairs:
                    self.y.append(bundle(pairs, (gx, there), on_y(there), on_y(back)))
                for i, sign_x in enumerate((1, -1)):
                    if corner_pairs[i]:
                        far, near = gx + sign_x * reach, gx - sign_x * reach
                        self.corners.append(
                            bundle(
                                corner_pairs[i],
                                (far if direct else gx, there),
                                on_y(there) & on_x(far if direct else near),
                                on_y(back) & on_x(near),
                            )
                        )
            everything.append(self)

        def send(self):
            for copies in self.x + self.y + (self.corners if self.direct else []):
                copies.start()

        def rows(self):
            for copies in self.y:
                copies.arrive()

        def forward(self):
            for copies in self.x:
                copies.arrive()
            for copies in self.corners:
                copies.arrive() if self.direct else copies.start()

        def finish(self):
            self.rows()
            self.last()

        def last(self):
            for copies in [] if self.direct else self.corners:
                copies.arrive()

        def leave(self):
            everything.remove(self)
            for copies in self.x + self.y + self.corners:
                copies.leave()

    class Gather:
        def __init__(self, rows, full, pad, index):
            self.rows, self.full, self.at = rows, full, pl.ds(pad + 2 * gx, 2)
            self.first = [
                self.copy(rows.at[gy], index, (gx, lax.rem(gy + k, ny))) for k in range(1, ny)
            ]
            mine = full.at[self.at]
            self.second = [
                self.copy(mine, index + 1, (lax.rem(gx + k, nx), gy)) for k in range(1, nx)
            ]
            self.first_all = self.copy(rows.at[pl.ds(0, ny - 1)], index, (gx, gy))
            self.second_all = self.copy(full.at[pl.ds(0, 2 * nx - 2)], index + 1, (gx, gy))

        def copy(self, ref, index, target):
            return pltpu.make_async_remote_copy(
                src_ref=ref,
                dst_ref=ref,
                send_sem=gather_send.at[index],
                recv_sem=gather_recv.at[index],
                device_id=target,
                device_id_type=MESH,
            )

        def send(self, tile):
            self.rows[gy] = tile
            for copy in self.first:
                copy.start()

        def forward(self):
            self.first_all.wait_recv()
            even, odd = self.rows[0], self.rows[1]
            for k in range(2, ny, 2):
                even, odd = even + self.rows[k], odd + self.rows[k + 1]
            low = iota(even.shape, 0) < 4
            layers = (
                jnp.where(low, even, pltpu.roll(odd, 4, 0)),
                jnp.where(low, pltpu.roll(even, 4, 0), odd),
            )
            for i in range(2):
                self.full[self.at.start + i] = layers[i]
            for copy in self.second:
                copy.start()

        def finish(self):
            self.second_all.wait_recv()

        def leave(self):
            self.first_all.wait_send()
            self.second_all.wait_send()

    x_0 = Exchange(
        (l0, c0, c0, 1, 2, True, (1, 1)),
        (l0, va0, va0, 1, 2, True, (1, 1)),
        (l0, b0, b0, 1, 1, True, None),
        direct=True,
    )
    x_v = Exchange((l0, ve0, ve0, 1, 2, True, (1, 1)), direct=True)
    x_late = Exchange((l0, c0, c0, 3, 3, False, (2, 3)), (l0, b0, b0, 2, 2, False, (1, 2)))
    x_k0 = Exchange((l0, vf0, vc0, 1, 3, True, (1, 3)))
    x_c = Exchange((l1, c1, c1, 1, 5, True, (1, 5)), (l2, c2, c2, 1, 4, True, (1, 4)))
    f_c = Exchange((l2, c2, c2, 5, 6, False, (5, 6)), reach=2)
    x_b1 = Exchange((l1, b1, b1, 1, 4, True, (1, 4)), direct=True)
    x_b2 = Exchange((l2, b2, b2, 1, 4, True, (1, 4)), direct=True)
    x_k = Exchange((l1, vc1, vc1, 1, 5, True, (1, 5)), (l2, vc2, vc2, 1, 4, True, (1, 4)))
    f_k = Exchange(
        (l2, b2, b2, 5, 6, False, (5, 6)), (l2, vc2, vc2, 5, 6, False, (5, 6)), reach=2
    )
    g_c3, g_b3 = Gather(pc, c3, l3.pad, 0), Gather(pb, b3, l3.pad, 2)

    for copy in loads:
        copy.wait()
    pl.semaphore_wait(barrier, nx + ny + 2)


    def double(k):
        for h in range(2):
            own = (pl.ds(l0.halo + k, 1), h, pl.ds(8, l0.by), slice(None))
            b0[own] = 2.0 * b0[own]

    loop_pieces(l0.bx, 4, double)
    x_0.send()

    def clear(level, refs, far):
        lo, bx, by = level.halo, level.bx, level.by

        def layers(start, count):
            for ref in refs:
                ref[pl.ds(start, count)] = jnp.zeros((count,) + ref.shape[1:], F32)

        near = min(lo, bx)
        pl.when(gx == 0)(lambda: layers(lo - near, near))
        pl.when(gx == nx - 1)(lambda: layers(lo + bx, near))
        if far:
            pl.when(gx < 2)(lambda: layers(0, lo - bx))
            pl.when(gx >= nx - 2)(lambda: layers(lo + 2 * bx, lo - bx))

        def rows(start, count):
            for ref in refs:
                for h in range(level.nh):
                    ref[:, h, pl.ds(start, count), :] = jnp.zeros((level.width, count, LANES), F32)

        pl.when(gy == 0)(lambda: rows(0, 8))
        pl.when(gy == ny - 1)(lambda: rows(8 + by, 8))

    clear(l0, (va0, c0, b0, vc0, ve0), False)
    clear(l1, (c1, b1, vc1), False)
    clear(l2, (c2, b2, vc2), True)
    for ref in (va3, vb3, c3, va4, vb4, c4):
        pad = 1 if ref.shape[0] == nx + 2 else l3.pad
        for start in (0, ref.shape[0] - pad):
            ref[pl.ds(start, pad)] = jnp.zeros((pad, 8, LANES), F32)
    for ref in (va1, vb1, va2, vb2):
        for h in range(ref.shape[1]):
            for r in range(0, ref.shape[2], 8):
                ref[:, h, pl.ds(r, 8), :] = jnp.zeros((ref.shape[0], 8, LANES), F32)

    lane_base = 32 * lax.shift_right_logical(gy, 1)

    def tile_of(s, weight):
        row, col = iota((LANES, LANES), 0), iota((LANES, LANES), 1)
        pick = (lax.shift_right_logical(row, 1) + lane_base == col) & (row < l2.nz)
        m = jnp.where(pick, weight, 0.0).astype(F32)
        a = s[pl.ds(0, 8, stride=2), :] + s[pl.ds(1, 8, stride=2), :]
        return dot(a, m)

    field_pairs(l0, c0, s0)
    c1[l1.halo : l1.halo + l1.bx, 0, 8 : 8 + l1.by, :] = halve(l0, s0, 0.125)
    field_pairs(l1, c1, s1)
    c2[l2.halo : l2.halo + l2.bx, 0, 8 : 8 + l2.by, :] = halve(l1, s1, 0.125)
    x_c.send()
    f_c.send()
    for k in range(2):
        s2[pl.ds(8 * k, 8), :] = (
            c2[l2.halo + 2 * k, 0, pl.ds(8, 8), :] + c2[l2.halo + 2 * k + 1, 0, pl.ds(8, 8), :]
        )
    g_c3.send(tile_of(s2, 0.125))

    bx0, by0 = gx * l0.bx, gy * l0.by
    chain, bx = (va0, vb0, ve0, vf0), l0.bx
    inner, outer, own, whole = tiles(12, 24), ((4, 8), (36, 8)), tiles(8, 32), tiles(4, 40)

    def prepare(span, rows):
        setup(l0, c0, g0, d0, span, rows, bx0, by0)

    def relax(k, span, rows):
        sweep(l0, chain[k - 1], chain[k], c0, g0, b0, span, rows)

    def rest(span):
        residual_pairs(l0, vf0, c0, b0, d0, s0, vc0, span)

    edges = (((-1, 0), own), ((0, 1), whole), ((bx - 1, bx), whole), ((bx, bx + 1), own))
    prepare((1, bx - 1), inner)
    relax(1, (1, bx - 1), inner)
    relax(2, (2, bx - 2), inner)
    x_0.rows()
    prepare((1, bx - 1), outer)
    relax(1, (1, bx - 1), outer)
    relax(2, (2, bx - 2), ((8, 8), (32, 8)))
    x_0.forward()
    for span, rows in edges:
        prepare(span, rows)
        relax(1, span, rows)
    for span in ((0, 2), (bx - 2, bx)):
        relax(2, span, own)
    x_v.send()
    x_late.send()
    relax(3, (1, bx - 1), inner)
    g_c3.forward()
    x_c.forward()
    f_c.forward()
    x_v.rows()
    relax(3, (1, bx - 1), outer)
    rest((1, bx // 2 - 1))
    x_v.forward()
    for span, rows in edges:
        relax(3, span, rows)
    for span in ((0, 1), (bx // 2 - 1, bx // 2)):
        rest(span)
    b1[l1.halo : l1.halo + l1.bx, 0, 8 : 8 + l1.by, :] = halve(l0, s0, 0.5)
    x_b1.send()
    x_late.forward()
    x_c.finish()
    f_c.finish()
    rows1, rows2 = tiles(4, 24, 24), tiles(2, 24, 24)
    setup(l1, c1, g1, d1, (-4, l1.bx + 4), rows1, gx * l1.bx, gy * l1.by)
    setup(l2, c2, g2, d2, (-5, l2.bx + 5), rows2, gx * l2.bx, gy * l2.by)
    x_b1.forward()
    x_b1.finish()
    first_sweep(l1, va1, g1, b1, (-3, l1.bx + 3), rows1)
    sweep(l1, va1, vb1, c1, g1, b1, (-2, l1.bx + 2), rows1)
    sweep(l1, vb1, va1, c1, g1, b1, (-1, l1.bx + 1), rows1)
    residual_pairs(l1, va1, c1, b1, d1, s1, vc1)
    b2[l2.halo : l2.halo + l2.bx, 0, 8 : 8 + l2.by, :] = halve(l1, s1, 0.5)
    x_b2.send()

    def pairs_of(ref):
        for k in range(nx):
            total = ref[l3.pad + 2 * k] + ref[l3.pad + 2 * k + 1]
            s3[k, pl.ds(0, 8), :] = total
            s3[k, pl.ds(8, 8), :] = total

    g_c3.finish()
    packed_setup(l3, c3, w3, wx3, g3, d3, RELAX)
    pairs_of(c3)
    c4[pl.ds(l4.pad, nx)] = packed_halve(s3, 0.125)
    packed_setup(l4, c4, w4, wx4, q4, d4, 1.0)

    x_b2.forward()
    x_b2.finish()
    x_k0.send()
    first_sweep(l2, va2, g2, b2, (-3, l2.bx + 3), rows2)
    sweep(l2, va2, vb2, c2, g2, b2, (-2, l2.bx + 2), rows2)
    sweep(l2, vb2, va2, c2, g2, b2, (-1, l2.bx + 1), rows2)
    for k in range(2):
        total = None
        for x0 in (l2.halo + 2 * k, l2.halo + 2 * k + 1):
            v, t = couple(l2, va2, c2, x0, 8, 8)
            part = block(b2, x0, 8, 8) + t - block(d2, x0, 8, 8) * v
            vc2[pl.ds(x0, 1), :, pl.ds(8, 8), :] = v
            total = part if total is None else total + part
        s2[pl.ds(8 * k, 8), :] = total[0, 0]
    g_b3.send(tile_of(s2, 0.5))
    x_k.send()
    f_k.send()
    g_b3.forward()
    x_late.finish()
    for span in ((-2, 0), (bx, bx + 2)):
        prepare(span, whole)
    x_k0.forward()
    x_k.forward()
    f_k.forward()
    g_b3.finish()
    for k in range(l3.count):
        va3[l3.pad + k] = g3[k] * b3[l3.pad + k]
    packed_sweep(l3, va3, vb3, w3, wx3, g3, b3, l3.pad)
    packed_sweep(l3, vb3, va3, w3, wx3, g3, b3, l3.pad)

    def residual3(k):
        total = None
        for i in (2 * k, 2 * k + 1):
            v, t = packed_couple(l3, va3, w3, wx3, i)
            r = b3[pl.ds(l3.pad + i, 1)] + t - d3[pl.ds(i, 1)] * v
            total = r if total is None else total + r
        s3[pl.ds(k, 1), pl.ds(0, 8), :] = total
        s3[pl.ds(k, 1), pl.ds(8, 8), :] = total

    loop_pieces(nx, 2, residual3)
    res4[...] = packed_halve(s3, 0.5)

    sigma = THETA / DELTA
    rho = 1.0 / sigma
    for k in range(nx):
        direction = res4[k] * q4[k] * (1.0 / THETA)
        e4[k] = direction
        va4[l4.pad + k] = direction
    src, dst = va4, vb4
    for step in range(CHEB - 1):
        rho_new = 1.0 / (2.0 * sigma - rho)
        for k in range(nx):
            at = pl.ds(k, 1)
            v, t = packed_couple(l4, src, w4, wx4, k)
            r = res4[at] - (d4[at] * v - t)
            direction = (rho_new * rho) * v + (2.0 * rho_new / DELTA) * (r * q4[at])
            res4[at] = r
            e4[at] = e4[at] + direction
            dst[pl.ds(l4.pad + k, 1)] = direction
        rho = rho_new
        src, dst = dst, src

    row, col = iota((LANES, LANES), 0), iota((LANES, LANES), 1)
    spread = jnp.where(row == lax.shift_right_logical(col, 1), 1.0, 0.0).astype(F32)
    fine = dot(e4[...].reshape(nx * 8, LANES), spread).reshape(nx, 8, LANES)
    for dr in range(2):
        t3[:, pl.ds(dr, 4, stride=2), :] = fine[:, 0:4, :]
    for k in range(l3.count):
        vb3[l3.pad + k] = va3[l3.pad + k] + t3[k // 2]
    packed_sweep(l3, vb3, va3, w3, wx3, g3, b3, l3.pad)
    packed_sweep(l3, va3, vb3, w3, wx3, g3, b3, l3.pad)
    packed_sweep(l3, vb3, va3, w3, wx3, g3, b3, l3.pad)

    f_k.finish()
    x_k.finish()
    group = lax.shift_right_logical(gy, 1) - 1
    e3 = va3[pl.ds(l3.pad - 3 + 2 * gx, 8)].reshape(64, LANES)
    for q in range(3):
        pick = (row == lax.shift_right_logical(col, 1) + 32 * (group + q)) & (col < l2.nz)
        part = dot(e3, jnp.where(pick, 1.0, 0.0).astype(F32))
        pe2[:, 0, pl.ds(8 * q, 8), :] = part.reshape(8, 8, LANES)
    add_prolonged(l2, pe2, vc2, va2, 0, 0, 8, 16, 4 * (gy & 1) + 4)
    sweep(l2, va2, vb2, c2, g2, b2, (-5, l2.bx + 5), rows2)
    sweep(l2, vb2, va2, c2, g2, b2, (-4, l2.bx + 4), rows2)
    sweep(l2, va2, vb2, c2, g2, b2, (-3, l2.bx + 3), rows2)

    prolong(l1, vb2, 3, 4, 10, 16, pe1, None, None, 0)
    add_prolonged(l1, pe1, vc1, va1, 0, 0, 10, 16)
    sweep(l1, va1, vb1, c1, g1, b1, (-4, l1.bx + 4), rows1)
    sweep(l1, vb1, va1, c1, g1, b1, (-3, l1.bx + 3), rows1)
    sweep(l1, va1, vb1, c1, g1, b1, (-2, l1.bx + 2), rows1)

    x_k0.finish()
    prolong(l0, vb1, 4, 4, 12, 24, pe0, None, None, 0)
    x_0.leave()
    x_v.leave()
    add_prolonged(l0, pe0, vc0, va0, 0, 0, 12, 24)
    def put(x0, r, n, new):
        for h in range(2):
            at = (pl.ds(x0 - l0.halo, 1), pl.ds(r - 8, n), slice(h * LANES, (h + 1) * LANES))
            out[at] = new[:, h]

    sweep(l0, va0, vb0, c0, g0, b0, (-2, l0.bx + 2), tiles(4, 40))
    sweep(l0, vb0, ve0, c0, g0, b0, (-1, l0.bx + 1), tiles(4, 40))
    sweep(l0, ve0, None, c0, g0, b0, (0, l0.bx), tiles(8, 32), put)
    for exchange in list(everything):
        exchange.leave()
    g_c3.leave()
    g_b3.leave()


def solution(mesh):
    nx, ny = mesh.shape["gx"], mesh.shape["gy"]
    l0 = Level(2, 256, 4, 16, 32, 48, 16 * nx, 32 * ny)
    l1 = Level(1, 128, 6, 8, 16, 32, 8 * nx, 16 * ny)
    l2 = Level(1, 64, 6, 4, 8, 32, 4 * nx, 8 * ny)
    l3 = Packed(2 * nx, 4, 8, 32, ny // 2)
    l4 = Packed(nx, 1, 4, 16, ny // 2)

    def vmem(*shape):
        return pltpu.VMEM(shape, F32)

    e, o = (lambda l: l.ext()), (lambda l: l.own())
    scratch = [e(l0)] * 9 + [vmem(8, 2, 32, LANES), vmem(12, 2, 24, LANES)]
    scratch += [e(l1)] * 7 + [vmem(4, 1, 16, LANES), vmem(10, 1, 16, LANES)]
    scratch += [e(l2)] * 7 + [vmem(16, LANES), vmem(8, 1, 24, LANES)]
    scratch += [e(l3)] * 4 + [l3.own(1), o(l3), o(l3), vmem(nx, 16, LANES), vmem(nx, 8, LANES)]
    scratch += [o(l3)] * 4
    scratch += [e(l4)] * 3 + [l4.own(1)] + [o(l4)] * 8
    scratch += [vmem(ny, 8, LANES)] * 2 + [vmem(64, 8, LANES)]
    copies = 7 * 8 + 3 * 6
    scratch += [
        pltpu.SemaphoreType.DMA((copies,)),
        pltpu.SemaphoreType.DMA((copies,)),
        pltpu.SemaphoreType.DMA((4,)),
        pltpu.SemaphoreType.DMA((4,)),
        pltpu.SemaphoreType.DMA((8,)),
    ]

    def step(guess, right_side, coefficient):
        return pl.pallas_call(
            functools.partial(kernel, nx, ny, (l0, l1, l2, l3, l4)),
            out_shape=pltpu.VMEM(guess.shape, F32),
            in_specs=[pl.BlockSpec(memory_space=pl.ANY)] * 3,
            out_specs=pl.BlockSpec(memory_space=pltpu.VMEM),
            scratch_shapes=scratch,
            compiler_params=pltpu.CompilerParams(collective_id=0, has_side_effects=True),
        )(guess, right_side, coefficient)

    spec = P("gx", "gy", None)
    return jax.shard_map(
        step, mesh=mesh, in_specs=(spec, spec, spec), out_specs=spec, check_vma=False
    )
```

```python
import functools
import math

import jax
import jax.numpy as jnp
from jax import lax
from jax.experimental import pallas as pl
from jax.experimental.pallas import tpu as pltpu
from jax.sharding import PartitionSpec as P

MESH = pl.DeviceIdType.MESH
F32 = jnp.float32
RELAX = 0.7
CHEB = 8
THETA = 1.04
DELTA = 0.96
LANES = 128
REGISTERS = 120


def iota(shape, dim):
    return lax.broadcasted_iota(jnp.int32, shape, dim)


class Level:
    def __init__(self, nh, nz, halo, bx, by, rows, total_x, total_y):
        self.nh, self.nz, self.halo, self.bx, self.by = nh, nz, halo, bx, by
        self.rows, self.total_x, self.total_y = rows, total_x, total_y
        self.width = bx + 2 * halo

    def ext(self):
        return pltpu.VMEM((self.width, self.nh, self.rows, LANES), F32)

    def own(self):
        return pltpu.VMEM((self.bx, self.nh, self.by, LANES), F32)


def z_sum(level, v):
    lane = iota(v.shape, 3)
    up, down = pltpu.roll(v, 1, 3), pltpu.roll(v, LANES - 1, 3)
    if level.nz >= LANES:
        none = jnp.zeros_like(v[:, :1])
        below = jnp.concatenate([none, up[:, :1]], 1) if level.nh == 2 else none
        above = jnp.concatenate([down[:, 1:], none], 1) if level.nh == 2 else none
        up = jnp.where(lane == 0, below, up)
        down = jnp.where(lane == LANES - 1, above, down)
    return up + down


def block(ref, x0, r0, n):
    return ref[pl.ds(x0, 1), :, pl.ds(r0, n), :]


def couple(level, v_ref, c_ref, x0, r0, n):
    v, c = block(v_ref, x0, r0, n), block(c_ref, x0, r0, n)
    sv, su = z_sum(level, v), z_sum(level, c * v)
    for dx, dr in ((-1, 0), (1, 0), (0, -1), (0, 1)):
        near = block(v_ref, x0 + dx, r0 + dr, n)
        sv = sv + near
        su = su + near * block(c_ref, x0 + dx, r0 + dr, n)
    return v, c * sv + su


def tiles(r0, n, most=16):
    return tuple((r, min(most, r0 + n - r)) for r in range(r0, r0 + n, most))


def loop(count, chunk, body):
    steps = count // chunk
    assert steps * chunk == count
    if steps == 1:
        body(0)
    else:
        lax.fori_loop(0, steps, lambda k, _: (body(k * chunk), 0)[1], 0)


def over(level, span, rows, body):
    lo, hi = span
    each = level.nh * sum(n for _, n in rows) // 8
    most = max(1, REGISTERS // each)
    chunk = max(c for c in range(1, hi - lo + 1) if (hi - lo) % c == 0 and c <= most)

    def several(k):
        for i in range(chunk):
            for r, n in rows:
                body(level.halo + lo + k + i, r, n)

    loop(hi - lo, chunk, several)


def sweep(level, src, dst, c, g, b, span, rows, put=None):
    def body(x0, r, n):
        v, t = couple(level, src, c, x0, r, n)
        new = (1.0 - RELAX) * v + block(g, x0, r, n) * (t + block(b, x0, r, n))
        if put is None:
            dst[pl.ds(x0, 1), :, pl.ds(r, n), :] = new
        else:
            put(x0, r, n, new)

    over(level, span, rows, body)


def first_sweep(level, dst, g, b, span, rows):
    def body(x0, r, n):
        dst[pl.ds(x0, 1), :, pl.ds(r, n), :] = block(g, x0, r, n) * block(b, x0, r, n)

    over(level, span, rows, body)


def setup(level, c, g, d, span, rows, base_x, base_y):
    def body(x0, r, n):
        mid = block(c, x0, r, n)
        px = base_x + x0 - level.halo
        py = iota(mid.shape, 2) + jnp.where(
            (px >= 0) & (px < level.total_x), base_y + r - 8, -1000
        )
        mask = (py >= 0) & (py < level.total_y)
        if level.nz < LANES:
            mask = mask & (iota(mid.shape, 3) < level.nz)
        total = 6.0 * mid + z_sum(level, mid)
        for dx, dr in ((-1, 0), (1, 0), (0, -1), (0, 1)):
            total = total + block(c, x0 + dx, r + dr, n)
        g[pl.ds(x0, 1), :, pl.ds(r, n), :] = jnp.where(
            mask, RELAX / jnp.where(mask, total, 1.0), 0.0
        )
        d[pl.ds(x0, 1), :, pl.ds(r, n), :] = total

    over(level, span, rows, body)


def residual_pairs(level, v_ref, c, b, d, s, keep, span=None):
    lo, hi = span or (0, level.bx // 2)

    def body(i):
        k = lo + i
        for r, n in tiles(8, level.by):
            total = None
            for x0 in (level.halo + 2 * k, level.halo + 2 * k + 1):
                v, t = couple(level, v_ref, c, x0, r, n)
                part = block(b, x0, r, n) + t - block(d, x0, r, n) * v
                keep[pl.ds(x0, 1), :, pl.ds(r, n), :] = v
                total = part if total is None else total + part
            s[pl.ds(k, 1), :, pl.ds(r - 8, n), :] = total

    count = hi - lo
    loop_pieces(count, max(i for i in (1, 2, 3, 4) if count % i == 0), body)


def field_pairs(level, ref, s):
    def body(k):
        x0 = level.halo + 2 * k
        s[pl.ds(k, 1)] = block(ref, x0, 8, level.by) + block(ref, x0 + 1, 8, level.by)

    loop_pieces(level.bx // 2, 4, body)


def dot(a, m):
    half = jnp.bfloat16
    high = a.astype(half)
    rest = a - high.astype(F32)
    middle = rest.astype(half)
    low = (rest - middle.astype(F32)).astype(half)
    m = m.astype(half)
    parts = [jnp.dot(p, m, preferred_element_type=F32) for p in (low, middle, high)]
    return (parts[0] + parts[1]) + parts[2]


def halve(level, s, weight):
    rows = level.by // 2
    count = level.bx // 2
    row, col = iota((LANES, LANES), 0), iota((LANES, LANES), 1)
    total = None
    for h in range(level.nh):
        pick = (lax.shift_right_logical(row, 1) + h * 64 == col) & (row < level.nz)
        m = jnp.where(pick, weight, 0.0).astype(F32)
        a = s[:, h, pl.ds(0, rows, stride=2), :] + s[:, h, pl.ds(1, rows, stride=2), :]
        part = dot(a.reshape(count * rows, LANES), m)
        total = part if total is None else total + part
    return total.reshape(count, rows, LANES)


def prolong(level, e, ex, er, count, ne, pe, base, dst, x0):
    row, col = iota((LANES, LANES), 0), iota((LANES, LANES), 1)
    coarse = e[pl.ds(ex, count), 0, pl.ds(er, ne), :].reshape(count * ne, LANES)
    for h in range(level.nh):
        m = jnp.where(row == lax.shift_right_logical(col, 1) + h * 64, 1.0, 0.0).astype(F32)
        pe[:, h, :, :] = dot(coarse, m).reshape(count, ne, LANES)


def add_prolonged(level, pe, base, dst, x0, r0, count, ne, er=0):
    def body(k):
        for h in range(level.nh):
            fine = pe[k, h, pl.ds(er, ne), :]
            for dx in range(2):
                for dr in range(2):
                    at = (x0 + 2 * k + dx, h, pl.ds(r0 + dr, ne, stride=2), slice(None))
                    dst[at] = base[at] + fine

    loop(count, 1, body)


class Packed:
    def __init__(self, count, pad, rows, width, groups):
        self.count, self.pad, self.rows, self.width, self.groups = count, pad, rows, width, groups

    def ext(self):
        return pltpu.VMEM((self.count + 2 * self.pad, 8, LANES), F32)

    def own(self, more=0):
        return pltpu.VMEM((self.count + more, 8, LANES), F32)


def packed_near(p, v):
    row = iota(v.shape, 1) & (p.rows - 1)
    after, before = pltpu.roll(v, 7, 1), pltpu.roll(v, 1, 1)
    return (
        jnp.where(row == p.rows - 1, pltpu.roll(after, LANES - p.width, 2), after),
        jnp.where(row == 0, pltpu.roll(before, p.width, 2), before),
        pltpu.roll(v, LANES - 1, 2),
        pltpu.roll(v, 1, 2),
    )


def packed_setup(p, c, w, wx, g, d, scale):
    def body(k):
        at = pl.ds(p.pad + k, 1)
        mid = c[at]
        lane, row = iota(mid.shape, 2), iota(mid.shape, 1) & (p.rows - 1)
        valid = lane < p.width * p.groups
        z = lane & (p.width - 1)
        inside = (
            (row < p.rows - 1) | (lane < p.width * (p.groups - 1)),
            (row > 0) | (lane >= p.width),
            z < p.width - 1,
            z > 0,
        )
        below = c[pl.ds(p.pad + k - 1, 1)]
        total = 6.0 * mid + below + c[pl.ds(p.pad + k + 1, 1)]
        wx[pl.ds(k, 1)] = mid + below
        for ref, near, ok in zip(w, packed_near(p, mid), inside):
            near = jnp.where(valid & ok, near, 0.0)
            ref[pl.ds(k, 1)] = jnp.where(valid & ok, mid + near, 0.0)
            total = total + near
        g[pl.ds(k, 1)] = jnp.where(valid, scale / jnp.where(valid, total, 1.0), 0.0)
        d[pl.ds(k, 1)] = total

    loop_pieces(p.count, 4, body)
    wx[pl.ds(p.count, 1)] = c[pl.ds(p.pad + p.count - 1, 1)]


def packed_couple(p, v_ref, w, wx, k):
    v = v_ref[pl.ds(p.pad + k, 1)]
    t = wx[pl.ds(k, 1)] * v_ref[pl.ds(p.pad + k - 1, 1)]
    t = t + wx[pl.ds(k + 1, 1)] * v_ref[pl.ds(p.pad + k + 1, 1)]
    parts = [ref[pl.ds(k, 1)] * near for ref, near in zip(w, packed_near(p, v))]
    return v, t + ((parts[0] + parts[1]) + (parts[2] + parts[3]))


def loop_pieces(count, chunk, body):
    def several(k):
        for i in range(chunk):
            body(k + i)

    loop(count, chunk, several)


def packed_sweep(p, src, dst, w, wx, g, b, b_pad):
    def body(k):
        v, t = packed_couple(p, src, w, wx, k)
        new = (1.0 - RELAX) * v + g[pl.ds(k, 1)] * (t + b[pl.ds(b_pad + k, 1)])
        dst[pl.ds(p.pad + k, 1)] = new

    loop_pieces(p.count, p.count, body)


def packed_halve(s, weight):
    row, col = iota((LANES, LANES), 0), iota((LANES, LANES), 1)
    m = jnp.where(lax.shift_right_logical(row, 1) == col, weight, 0.0).astype(F32)
    a = s[:, pl.ds(0, 8, stride=2), :] + s[:, pl.ds(1, 8, stride=2), :]
    return dot(a.reshape(s.shape[0] * 8, LANES), m).reshape(s.shape[0], 8, LANES)


class Bundle:
    def __init__(self, pairs, target, sends, receives, tiles, unit, sems):
        send_sem, recv_sem, index = sems

        def copy(src, dst):
            return pltpu.make_async_remote_copy(
                src_ref=src,
                dst_ref=dst,
                send_sem=send_sem.at[index],
                recv_sem=recv_sem.at[index],
                device_id=target,
                device_id_type=MESH,
            )

        self.copies = [copy(src, dst) for src, dst in pairs]
        whole = unit.at[pl.ds(0, tiles)]
        self.whole = self.copies[0] if len(pairs) == 1 else copy(whole, whole)
        self.sends, self.receives = sends, receives

    def start(self):
        def go():
            for copy in self.copies:
                copy.start()

        pl.when(self.sends)(go)

    def arrive(self):
        pl.when(self.receives)(lambda: self.whole.wait_recv())

    def leave(self):
        pl.when(self.sends)(lambda: self.whole.wait_send())


def kernel(nx, ny, levels, guess, rhs, coef, out, *scratch):
    l0, l1, l2, l3, l4 = levels
    names = iter(scratch)
    take = lambda k: [next(names) for _ in range(k)]
    va0, vb0, vc0, c0, b0, g0, d0, ve0, vf0, s0, pe0 = take(11)
    va1, vb1, vc1, c1, b1, g1, d1, s1, pe1 = take(9)
    va2, vb2, vc2, c2, b2, g2, d2, s2, pe2 = take(9)
    va3, vb3, c3, b3, wx3, g3, d3, s3, t3 = take(9)
    w3 = take(4)
    va4, vb4, c4, wx4, q4, d4, res4, e4 = take(8)
    w4 = take(4)
    pc, pb, unit = take(3)
    send_sem, recv_sem, gather_send, gather_recv, local_sem = take(5)

    gx, gy = lax.axis_index("gx"), lax.axis_index("gy")
    counter = iter(range(1000))

    def sems(again=None):
        return send_sem, recv_sem, next(counter if again is None else again)

    loads = []
    for i, (src, dst) in enumerate(((coef, c0), (guess, va0), (rhs, b0))):
        for h in range(2):
            loads.append(
                pltpu.make_async_copy(
                    src.at[:, :, h * LANES : (h + 1) * LANES],
                    dst.at[l0.halo : l0.halo + l0.bx, h, 8 : 8 + l0.by, :],
                    local_sem.at[2 * i + h],
                )
            )
    for copy in loads:
        copy.start()

    barrier = pltpu.get_barrier_semaphore()
    for k in range(1, nx):
        pl.semaphore_signal(
            barrier, inc=1, device_id=(lax.rem(gx + k, nx), gy), device_id_type=MESH
        )
    for k in range(1, ny):
        pl.semaphore_signal(
            barrier, inc=1, device_id=(gx, lax.rem(gy + k, ny)), device_id_type=MESH
        )

    for dx in (1, nx - 1):
        for dy in (1, ny - 1):
            diagonal = (lax.rem(gx + dx, nx), lax.rem(gy + dy, ny))
            pl.semaphore_signal(barrier, inc=1, device_id=diagonal, device_id_type=MESH)

    everything = []

    class Exchange:
        def __init__(self, *parts, reach=1, direct=False, after=None):
            self.direct = direct
            again = None if after is None else iter(after.indices)
            self.indices = []
            on_x, on_y = (lambda p: (p >= 0) & (p < nx)), (lambda p: (p >= 0) & (p < ny))

            def layers(level, sign, a, b):
                lo, bx = level.halo, level.bx
                if sign > 0:
                    return lo + reach * bx - b, lo - b, b - a + 1
                return lo + a - 1 - (reach - 1) * bx, lo + bx + a - 1, b - a + 1

            def bundle(pairs, target, sends, receives):
                total = sum(math.prod(dst.shape) for _, dst in pairs) // (8 * LANES)
                chosen = sems(again)
                self.indices.append(chosen[2])
                return Bundle(pairs, target, sends, receives, total, unit, chosen)

            self.x, self.y, self.corners = [], [], []
            for sign in (1, -1):
                there, back = gx + sign * reach, gx - sign * reach
                pairs = []
                for level, src, dst, a, b, faces, corner in parts:
                    at, to, count = layers(level, sign, a, b)
                    own = pl.ds(8, level.by)
                    pairs.append(
                        (src.at[pl.ds(at, count), :, own, :], dst.at[pl.ds(to, count), :, own, :])
                    )
                self.x.append(bundle(pairs, (there, gy), on_x(there), on_x(back)))
            for sign in (1, -1):
                there, back = gy + sign, gy - sign
                pairs, corner_pairs = [], ([], [])
                for level, src, dst, a, b, faces, corner in parts:
                    deep = 4 if level.nh == 2 else 8
                    row = 8 + level.by - deep if sign > 0 else 8
                    to_row = 8 - deep if sign > 0 else 8 + level.by

                    def strips(ref, at, to, count):
                        return (
                            ref.at[pl.ds(at, count), :, pl.ds(row, deep), :],
                            dst.at[pl.ds(to, count), :, pl.ds(to_row, deep), :],
                        )

                    if faces:
                        pairs.append(strips(src, level.halo, level.halo, level.bx))
                    if corner:
                        for i, sign_x in enumerate((1, -1)):
                            at, to, count = layers(level, sign_x, *corner)
                            corner_pairs[i].append(strips(src if direct else dst, at if direct else to, to, count))
                if pairs:
                    self.y.append(bundle(pairs, (gx, there), on_y(there), on_y(back)))
                for i, sign_x in enumerate((1, -1)):
                    if corner_pairs[i]:
                        far, near = gx + sign_x * reach, gx - sign_x * reach
                        self.corners.append(
                            bundle(
                                corner_pairs[i],
                                (far if direct else gx, there),
                                on_y(there) & on_x(far if direct else near),
                                on_y(back) & on_x(near),
                            )
                        )
            everything.append(self)

        def send(self):
            for copies in self.x + self.y + (self.corners if self.direct else []):
                copies.start()

        def rows(self):
            for copies in self.y:
                copies.arrive()

        def forward(self):
            for copies in self.x:
                copies.arrive()
            for copies in self.corners:
                copies.arrive() if self.direct else copies.start()

        def finish(self):
            self.rows()
            self.last()

        def last(self):
            for copies in [] if self.direct else self.corners:
                copies.arrive()

        def leave(self):
            everything.remove(self)
            for copies in self.x + self.y + self.corners:
                copies.leave()

    class Gather:
        def __init__(self, rows, full, pad, index):
            self.rows, self.full, self.at = rows, full, pl.ds(pad + 2 * gx, 2)
            self.first = [
                self.copy(rows.at[gy], index, (gx, lax.rem(gy + k, ny))) for k in range(1, ny)
            ]
            mine = full.at[self.at]
            self.second = [
                self.copy(mine, index + 1, (lax.rem(gx + k, nx), gy)) for k in range(1, nx)
            ]
            self.first_all = self.copy(rows.at[pl.ds(0, ny - 1)], index, (gx, gy))
            self.second_all = self.copy(full.at[pl.ds(0, 2 * nx - 2)], index + 1, (gx, gy))

        def copy(self, ref, index, target):
            return pltpu.make_async_remote_copy(
                src_ref=ref,
                dst_ref=ref,
                send_sem=gather_send.at[index],
                recv_sem=gather_recv.at[index],
                device_id=target,
                device_id_type=MESH,
            )

        def send(self, tile):
            self.rows[gy] = tile
            for copy in self.first:
                copy.start()

        def forward(self):
            self.first_all.wait_recv()
            even, odd = self.rows[0], self.rows[1]
            for k in range(2, ny, 2):
                even, odd = even + self.rows[k], odd + self.rows[k + 1]
            low = iota(even.shape, 0) < 4
            layers = (
                jnp.where(low, even, pltpu.roll(odd, 4, 0)),
                jnp.where(low, pltpu.roll(even, 4, 0), odd),
            )
            for i in range(2):
                self.full[self.at.start + i] = layers[i]
            for copy in self.second:
                copy.start()

        def finish(self):
            self.second_all.wait_recv()

        def leave(self):
            self.first_all.wait_send()
            self.second_all.wait_send()

    x_0 = Exchange(
        (l0, c0, c0, 1, 2, True, (1, 1)),
        (l0, va0, va0, 1, 2, True, (1, 1)),
        (l0, b0, b0, 1, 1, True, None),
        direct=True,
    )
    x_v = Exchange((l0, ve0, ve0, 1, 2, True, (1, 1)), direct=True)
    x_late = Exchange((l0, c0, c0, 3, 3, False, (2, 3)), (l0, b0, b0, 2, 2, False, (1, 2)))
    x_k0 = Exchange((l0, vf0, vc0, 1, 3, True, (1, 3)))
    x_c = Exchange((l1, c1, c1, 1, 5, True, (1, 5)), (l2, c2, c2, 1, 4, True, (1, 4)))
    f_c = Exchange((l2, c2, c2, 5, 6, False, (5, 6)), reach=2)
    x_b1 = Exchange((l1, b1, b1, 1, 4, True, (1, 4)), direct=True, after=x_0)
    x_b2 = Exchange((l2, b2, b2, 1, 4, True, (1, 4)), direct=True, after=x_v)
    x_k = Exchange((l1, vc1, vc1, 1, 5, True, (1, 5)), (l2, vc2, vc2, 1, 4, True, (1, 4)),
        after=x_c,
    )
    f_k = Exchange(
        (l2, b2, b2, 5, 6, False, (5, 6)), (l2, vc2, vc2, 5, 6, False, (5, 6)), reach=2, after=f_c
    )
    g_c3, g_b3 = Gather(pc, c3, l3.pad, 0), Gather(pb, b3, l3.pad, 2)

    for copy in loads:
        copy.wait()
    pl.semaphore_wait(barrier, nx + ny + 2)


    def double(k):
        for h in range(2):
            own = (pl.ds(l0.halo + k, 1), h, pl.ds(8, l0.by), slice(None))
            b0[own] = 2.0 * b0[own]

    loop_pieces(l0.bx, 4, double)
    x_0.send()

    def clear(level, refs, far):
        lo, bx, by = level.halo, level.bx, level.by

        def layers(start, count):
            for ref in refs:
                ref[pl.ds(start, count)] = jnp.zeros((count,) + ref.shape[1:], F32)

        near = min(lo, bx)
        pl.when(gx == 0)(lambda: layers(lo - near, near))
        pl.when(gx == nx - 1)(lambda: layers(lo + bx, near))
        if far:
            pl.when(gx < 2)(lambda: layers(0, lo - bx))
            pl.when(gx >= nx - 2)(lambda: layers(lo + 2 * bx, lo - bx))

        def rows(start, count):
            for ref in refs:
                for h in range(level.nh):
                    ref[:, h, pl.ds(start, count), :] = jnp.zeros((level.width, count, LANES), F32)

        pl.when(gy == 0)(lambda: rows(0, 8))
        pl.when(gy == ny - 1)(lambda: rows(8 + by, 8))

    clear(l0, (va0, c0, b0, vc0, ve0), False)
    clear(l1, (c1, b1, vc1), False)
    clear(l2, (c2, b2, vc2), True)
    for ref in (va3, vb3, c3, va4, vb4, c4):
        pad = 1 if ref.shape[0] == nx + 2 else l3.pad
        for start in (0, ref.shape[0] - pad):
            ref[pl.ds(start, pad)] = jnp.zeros((pad, 8, LANES), F32)
    for ref in (va1, vb1, va2, vb2):
        for h in range(ref.shape[1]):
            for r in range(0, ref.shape[2], 8):
                ref[:, h, pl.ds(r, 8), :] = jnp.zeros((ref.shape[0], 8, LANES), F32)

    lane_base = 32 * lax.shift_right_logical(gy, 1)

    def tile_of(s, weight):
        row, col = iota((LANES, LANES), 0), iota((LANES, LANES), 1)
        pick = (lax.shift_right_logical(row, 1) + lane_base == col) & (row < l2.nz)
        m = jnp.where(pick, weight, 0.0).astype(F32)
        a = s[pl.ds(0, 8, stride=2), :] + s[pl.ds(1, 8, stride=2), :]
        return dot(a, m)

    field_pairs(l0, c0, s0)
    c1[l1.halo : l1.halo + l1.bx, 0, 8 : 8 + l1.by, :] = halve(l0, s0, 0.125)
    field_pairs(l1, c1, s1)
    c2[l2.halo : l2.halo + l2.bx, 0, 8 : 8 + l2.by, :] = halve(l1, s1, 0.125)
    x_c.send()
    f_c.send()
    for k in range(2):
        s2[pl.ds(8 * k, 8), :] = (
            c2[l2.halo + 2 * k, 0, pl.ds(8, 8), :] + c2[l2.halo + 2 * k + 1, 0, pl.ds(8, 8), :]
        )
    g_c3.send(tile_of(s2, 0.125))

    bx0, by0 = gx * l0.bx, gy * l0.by
    chain, bx = (va0, vb0, ve0, vf0), l0.bx
    inner, outer, own, whole = tiles(12, 24), ((4, 8), (36, 8)), tiles(8, 32), tiles(4, 40)

    def prepare(span, rows):
        setup(l0, c0, g0, d0, span, rows, bx0, by0)

    def relax(k, span, rows):
        sweep(l0, chain[k - 1], chain[k], c0, g0, b0, span, rows)

    def rest(span):
        residual_pairs(l0, vf0, c0, b0, d0, s0, vc0, span)

    edges = (((-1, 0), own), ((0, 1), whole), ((bx - 1, bx), whole), ((bx, bx + 1), own))
    prepare((1, bx - 1), inner)
    relax(1, (1, bx - 1), inner)
    relax(2, (2, bx - 2), inner)
    x_0.rows()
    prepare((1, bx - 1), outer)
    relax(1, (1, bx - 1), outer)
    relax(2, (2, bx - 2), ((8, 8), (32, 8)))
    x_0.forward()
    for span, rows in edges:
        prepare(span, rows)
        relax(1, span, rows)
    for span in ((0, 2), (bx - 2, bx)):
        relax(2, span, own)
    x_v.send()
    x_late.send()
    relax(3, (1, bx - 1), inner)
    g_c3.forward()
    x_c.forward()
    f_c.forward()
    x_v.rows()
    relax(3, (1, bx - 1), outer)
    rest((1, bx // 2 - 1))
    x_v.forward()
    for span, rows in edges:
        relax(3, span, rows)
    for span in ((0, 1), (bx // 2 - 1, bx // 2)):
        rest(span)
    b1[l1.halo : l1.halo + l1.bx, 0, 8 : 8 + l1.by, :] = halve(l0, s0, 0.5)
    x_0.leave()
    x_b1.send()
    x_late.forward()
    x_c.finish()
    f_c.finish()
    rows1, rows2 = tiles(4, 24, 24), tiles(2, 24, 24)
    setup(l1, c1, g1, d1, (-4, l1.bx + 4), rows1, gx * l1.bx, gy * l1.by)
    setup(l2, c2, g2, d2, (-5, l2.bx + 5), rows2, gx * l2.bx, gy * l2.by)
    x_b1.forward()
    x_b1.finish()
    first_sweep(l1, va1, g1, b1, (-3, l1.bx + 3), rows1)
    sweep(l1, va1, vb1, c1, g1, b1, (-2, l1.bx + 2), rows1)
    sweep(l1, vb1, va1, c1, g1, b1, (-1, l1.bx + 1), rows1)
    residual_pairs(l1, va1, c1, b1, d1, s1, vc1)
    b2[l2.halo : l2.halo + l2.bx, 0, 8 : 8 + l2.by, :] = halve(l1, s1, 0.5)
    x_v.leave()
    x_b2.send()

    def pairs_of(ref):
        for k in range(nx):
            total = ref[l3.pad + 2 * k] + ref[l3.pad + 2 * k + 1]
            s3[k, pl.ds(0, 8), :] = total
            s3[k, pl.ds(8, 8), :] = total

    g_c3.finish()
    packed_setup(l3, c3, w3, wx3, g3, d3, RELAX)
    pairs_of(c3)
    c4[pl.ds(l4.pad, nx)] = packed_halve(s3, 0.125)
    packed_setup(l4, c4, w4, wx4, q4, d4, 1.0)

    x_b2.forward()
    x_b2.finish()
    x_k0.send()
    first_sweep(l2, va2, g2, b2, (-3, l2.bx + 3), rows2)
    sweep(l2, va2, vb2, c2, g2, b2, (-2, l2.bx + 2), rows2)
    sweep(l2, vb2, va2, c2, g2, b2, (-1, l2.bx + 1), rows2)
    for k in range(2):
        total = None
        for x0 in (l2.halo + 2 * k, l2.halo + 2 * k + 1):
            v, t = couple(l2, va2, c2, x0, 8, 8)
            part = block(b2, x0, 8, 8) + t - block(d2, x0, 8, 8) * v
            vc2[pl.ds(x0, 1), :, pl.ds(8, 8), :] = v
            total = part if total is None else total + part
        s2[pl.ds(8 * k, 8), :] = total[0, 0]
    g_b3.send(tile_of(s2, 0.5))
    x_c.leave()
    f_c.leave()
    x_k.send()
    f_k.send()
    g_b3.forward()
    x_late.finish()
    for span in ((-2, 0), (bx, bx + 2)):
        prepare(span, whole)
    x_k.forward()
    f_k.forward()
    g_b3.finish()
    for k in range(l3.count):
        va3[l3.pad + k] = g3[k] * b3[l3.pad + k]
    packed_sweep(l3, va3, vb3, w3, wx3, g3, b3, l3.pad)
    packed_sweep(l3, vb3, va3, w3, wx3, g3, b3, l3.pad)

    def residual3(k):
        total = None
        for i in (2 * k, 2 * k + 1):
            v, t = packed_couple(l3, va3, w3, wx3, i)
            r = b3[pl.ds(l3.pad + i, 1)] + t - d3[pl.ds(i, 1)] * v
            total = r if total is None else total + r
        s3[pl.ds(k, 1), pl.ds(0, 8), :] = total
        s3[pl.ds(k, 1), pl.ds(8, 8), :] = total

    loop_pieces(nx, 2, residual3)
    res4[...] = packed_halve(s3, 0.5)

    x_k0.forward()
    sigma = THETA / DELTA
    rho = 1.0 / sigma
    for k in range(nx):
        direction = res4[k] * q4[k] * (1.0 / THETA)
        e4[k] = direction
        va4[l4.pad + k] = direction
    src, dst = va4, vb4
    for step in range(CHEB - 1):
        rho_new = 1.0 / (2.0 * sigma - rho)
        for k in range(nx):
            at = pl.ds(k, 1)
            v, t = packed_couple(l4, src, w4, wx4, k)
            r = res4[at] - (d4[at] * v - t)
            direction = (rho_new * rho) * v + (2.0 * rho_new / DELTA) * (r * q4[at])
            res4[at] = r
            e4[at] = e4[at] + direction
            dst[pl.ds(l4.pad + k, 1)] = direction
        rho = rho_new
        src, dst = dst, src

    row, col = iota((LANES, LANES), 0), iota((LANES, LANES), 1)
    spread = jnp.where(row == lax.shift_right_logical(col, 1), 1.0, 0.0).astype(F32)
    fine = dot(e4[...].reshape(nx * 8, LANES), spread).reshape(nx, 8, LANES)
    for dr in range(2):
        t3[:, pl.ds(dr, 4, stride=2), :] = fine[:, 0:4, :]
    for k in range(l3.count):
        vb3[l3.pad + k] = va3[l3.pad + k] + t3[k // 2]
    packed_sweep(l3, vb3, va3, w3, wx3, g3, b3, l3.pad)
    packed_sweep(l3, va3, vb3, w3, wx3, g3, b3, l3.pad)
    packed_sweep(l3, vb3, va3, w3, wx3, g3, b3, l3.pad)

    f_k.finish()
    x_k.finish()
    group = lax.shift_right_logical(gy, 1) - 1
    e3 = va3[pl.ds(l3.pad - 3 + 2 * gx, 8)].reshape(64, LANES)
    for q in range(3):
        pick = (row == lax.shift_right_logical(col, 1) + 32 * (group + q)) & (col < l2.nz)
        part = dot(e3, jnp.where(pick, 1.0, 0.0).astype(F32))
        pe2[:, 0, pl.ds(8 * q, 8), :] = part.reshape(8, 8, LANES)
    add_prolonged(l2, pe2, vc2, va2, 0, 0, 8, 16, 4 * (gy & 1) + 4)
    sweep(l2, va2, vb2, c2, g2, b2, (-5, l2.bx + 5), rows2)
    sweep(l2, vb2, va2, c2, g2, b2, (-4, l2.bx + 4), rows2)
    sweep(l2, va2, vb2, c2, g2, b2, (-3, l2.bx + 3), rows2)

    prolong(l1, vb2, 3, 4, 10, 16, pe1, None, None, 0)
    add_prolonged(l1, pe1, vc1, va1, 0, 0, 10, 16)
    sweep(l1, va1, vb1, c1, g1, b1, (-4, l1.bx + 4), rows1)
    sweep(l1, vb1, va1, c1, g1, b1, (-3, l1.bx + 3), rows1)
    sweep(l1, va1, vb1, c1, g1, b1, (-2, l1.bx + 2), rows1)

    x_k0.finish()
    prolong(l0, vb1, 4, 4, 12, 24, pe0, None, None, 0)
    add_prolonged(l0, pe0, vc0, va0, 0, 0, 12, 24)
    def put(x0, r, n, new):
        for h in range(2):
            at = (pl.ds(x0 - l0.halo, 1), pl.ds(r - 8, n), slice(h * LANES, (h + 1) * LANES))
            out[at] = new[:, h]

    sweep(l0, va0, vb0, c0, g0, b0, (-2, l0.bx + 2), tiles(4, 40))
    sweep(l0, vb0, ve0, c0, g0, b0, (-1, l0.bx + 1), tiles(4, 40))
    sweep(l0, ve0, None, c0, g0, b0, (0, l0.bx), tiles(8, 32), put)
    for exchange in list(everything):
        exchange.leave()
    g_c3.leave()
    g_b3.leave()


def solution(mesh):
    nx, ny = mesh.shape["gx"], mesh.shape["gy"]
    l0 = Level(2, 256, 4, 16, 32, 48, 16 * nx, 32 * ny)
    l1 = Level(1, 128, 6, 8, 16, 32, 8 * nx, 16 * ny)
    l2 = Level(1, 64, 6, 4, 8, 32, 4 * nx, 8 * ny)
    l3 = Packed(2 * nx, 4, 8, 32, ny // 2)
    l4 = Packed(nx, 1, 4, 16, ny // 2)

    def vmem(*shape):
        return pltpu.VMEM(shape, F32)

    e, o = (lambda l: l.ext()), (lambda l: l.own())
    scratch = [e(l0)] * 9 + [vmem(8, 2, 32, LANES), vmem(12, 2, 24, LANES)]
    scratch += [e(l1)] * 7 + [vmem(4, 1, 16, LANES), vmem(10, 1, 16, LANES)]
    scratch += [e(l2)] * 7 + [vmem(16, LANES), vmem(8, 1, 24, LANES)]
    scratch += [e(l3)] * 4 + [l3.own(1), o(l3), o(l3), vmem(nx, 16, LANES), vmem(nx, 8, LANES)]
    scratch += [o(l3)] * 4
    scratch += [e(l4)] * 3 + [l4.own(1)] + [o(l4)] * 8
    scratch += [vmem(ny, 8, LANES)] * 2 + [vmem(64, 8, LANES)]
    copies = 4 * 8 + 2 * 6
    scratch += [
        pltpu.SemaphoreType.DMA((copies,)),
        pltpu.SemaphoreType.DMA((copies,)),
        pltpu.SemaphoreType.DMA((4,)),
        pltpu.SemaphoreType.DMA((4,)),
        pltpu.SemaphoreType.DMA((8,)),
    ]

    def step(guess, right_side, coefficient):
        return pl.pallas_call(
            functools.partial(kernel, nx, ny, (l0, l1, l2, l3, l4)),
            out_shape=pltpu.VMEM(guess.shape, F32),
            in_specs=[pl.BlockSpec(memory_space=pl.ANY)] * 3,
            out_specs=pl.BlockSpec(memory_space=pltpu.VMEM),
            scratch_shapes=scratch,
            compiler_params=pltpu.CompilerParams(collective_id=0, has_side_effects=True),
        )(guess, right_side, coefficient)

    spec = P("gx", "gy", None)
    return jax.shard_map(
        step, mesh=mesh, in_specs=(spec, spec, spec), out_specs=spec, check_vma=False
    )
```

```python
import functools
import math

import jax
import jax.numpy as jnp
from jax import lax
from jax.experimental import pallas as pl
from jax.experimental.pallas import tpu as pltpu
from jax.sharding import PartitionSpec as P

MESH = pl.DeviceIdType.MESH
F32 = jnp.float32
RELAX = 0.7
CHEB = 8
THETA = 1.04
DELTA = 0.96
LANES = 128
REGISTERS = 260


def iota(shape, dim):
    return lax.broadcasted_iota(jnp.int32, shape, dim)


class Level:
    def __init__(self, nh, nz, halo, bx, by, rows, total_x, total_y):
        self.nh, self.nz, self.halo, self.bx, self.by = nh, nz, halo, bx, by
        self.rows, self.total_x, self.total_y = rows, total_x, total_y
        self.width = bx + 2 * halo

    def ext(self):
        return pltpu.VMEM((self.width, self.nh, self.rows, LANES), F32)

    def own(self):
        return pltpu.VMEM((self.bx, self.nh, self.by, LANES), F32)


def z_sum(level, v):
    lane = iota(v.shape, 3)
    up, down = pltpu.roll(v, 1, 3), pltpu.roll(v, LANES - 1, 3)
    if level.nz >= LANES:
        none = jnp.zeros_like(v[:, :1])
        below = jnp.concatenate([none, up[:, :1]], 1) if level.nh == 2 else none
        above = jnp.concatenate([down[:, 1:], none], 1) if level.nh == 2 else none
        up = jnp.where(lane == 0, below, up)
        down = jnp.where(lane == LANES - 1, above, down)
    return up + down


def block(ref, x0, r0, n):
    return ref[pl.ds(x0, 1), :, pl.ds(r0, n), :]


def couple(level, v_ref, c_ref, x0, r0, n):
    v, c = block(v_ref, x0, r0, n), block(c_ref, x0, r0, n)
    sv, su = z_sum(level, v), z_sum(level, c * v)
    for dx, dr in ((-1, 0), (1, 0), (0, -1), (0, 1)):
        near = block(v_ref, x0 + dx, r0 + dr, n)
        sv = sv + near
        su = su + near * block(c_ref, x0 + dx, r0 + dr, n)
    return v, c * sv + su


def tiles(r0, n, most=16):
    return tuple((r, min(most, r0 + n - r)) for r in range(r0, r0 + n, most))


def loop(count, chunk, body):
    steps = count // chunk
    assert steps * chunk == count
    if steps == 1:
        body(0)
    else:
        lax.fori_loop(0, steps, lambda k, _: (body(k * chunk), 0)[1], 0)


def over(level, span, rows, body):
    lo, hi = span
    each = level.nh * sum(n for _, n in rows) // 8
    most = max(1, REGISTERS // each)
    chunk = max(c for c in range(1, hi - lo + 1) if (hi - lo) % c == 0 and c <= most)

    def several(k):
        for i in range(chunk):
            for r, n in rows:
                body(level.halo + lo + k + i, r, n)

    loop(hi - lo, chunk, several)


def sweep(level, src, dst, c, g, b, span, rows, put=None):
    def body(x0, r, n):
        v, t = couple(level, src, c, x0, r, n)
        new = (1.0 - RELAX) * v + block(g, x0, r, n) * (t + block(b, x0, r, n))
        if put is None:
            dst[pl.ds(x0, 1), :, pl.ds(r, n), :] = new
        else:
            put(x0, r, n, new)

    over(level, span, rows, body)


def first_sweep(level, dst, g, b, span, rows):
    def body(x0, r, n):
        dst[pl.ds(x0, 1), :, pl.ds(r, n), :] = block(g, x0, r, n) * block(b, x0, r, n)

    over(level, span, rows, body)


def setup(level, c, g, d, span, rows, base_x, base_y):
    def body(x0, r, n):
        mid = block(c, x0, r, n)
        px = base_x + x0 - level.halo
        py = iota(mid.shape, 2) + jnp.where(
            (px >= 0) & (px < level.total_x), base_y + r - 8, -1000
        )
        mask = (py >= 0) & (py < level.total_y)
        if level.nz < LANES:
            mask = mask & (iota(mid.shape, 3) < level.nz)
        total = 6.0 * mid + z_sum(level, mid)
        for dx, dr in ((-1, 0), (1, 0), (0, -1), (0, 1)):
            total = total + block(c, x0 + dx, r + dr, n)
        g[pl.ds(x0, 1), :, pl.ds(r, n), :] = jnp.where(
            mask, RELAX / jnp.where(mask, total, 1.0), 0.0
        )
        d[pl.ds(x0, 1), :, pl.ds(r, n), :] = total

    over(level, span, rows, body)


def residual_pairs(level, v_ref, c, b, d, s, keep, span=None):
    lo, hi = span or (0, level.bx // 2)

    def body(i):
        k = lo + i
        for r, n in tiles(8, level.by):
            total = None
            for x0 in (level.halo + 2 * k, level.halo + 2 * k + 1):
                v, t = couple(level, v_ref, c, x0, r, n)
                part = block(b, x0, r, n) + t - block(d, x0, r, n) * v
                keep[pl.ds(x0, 1), :, pl.ds(r, n), :] = v
                total = part if total is None else total + part
            s[pl.ds(k, 1), :, pl.ds(r - 8, n), :] = total

    count = hi - lo
    loop_pieces(count, max(i for i in (1, 2, 3, 4) if count % i == 0), body)


def field_pairs(level, ref, s):
    def body(k):
        x0 = level.halo + 2 * k
        s[pl.ds(k, 1)] = block(ref, x0, 8, level.by) + block(ref, x0 + 1, 8, level.by)

    loop_pieces(level.bx // 2, 4, body)


def dot(a, m):
    half = jnp.bfloat16
    high = a.astype(half)
    rest = a - high.astype(F32)
    middle = rest.astype(half)
    low = (rest - middle.astype(F32)).astype(half)
    m = m.astype(half)
    parts = [jnp.dot(p, m, preferred_element_type=F32) for p in (low, middle, high)]
    return (parts[0] + parts[1]) + parts[2]


def halve(level, s, weight):
    rows = level.by // 2
    count = level.bx // 2
    row, col = iota((LANES, LANES), 0), iota((LANES, LANES), 1)
    total = None
    for h in range(level.nh):
        pick = (lax.shift_right_logical(row, 1) + h * 64 == col) & (row < level.nz)
        m = jnp.where(pick, weight, 0.0).astype(F32)
        a = s[:, h, pl.ds(0, rows, stride=2), :] + s[:, h, pl.ds(1, rows, stride=2), :]
        part = dot(a.reshape(count * rows, LANES), m)
        total = part if total is None else total + part
    return total.reshape(count, rows, LANES)


def prolong(level, e, ex, er, count, ne, pe, base, dst, x0):
    row, col = iota((LANES, LANES), 0), iota((LANES, LANES), 1)
    coarse = e[pl.ds(ex, count), 0, pl.ds(er, ne), :].reshape(count * ne, LANES)
    for h in range(level.nh):
        m = jnp.where(row == lax.shift_right_logical(col, 1) + h * 64, 1.0, 0.0).astype(F32)
        pe[:, h, :, :] = dot(coarse, m).reshape(count, ne, LANES)


def add_prolonged(level, pe, base, dst, x0, r0, count, ne, er=0):
    def body(k):
        for h in range(level.nh):
            fine = pe[k, h, pl.ds(er, ne), :]
            for dx in range(2):
                for dr in range(2):
                    at = (x0 + 2 * k + dx, h, pl.ds(r0 + dr, ne, stride=2), slice(None))
                    dst[at] = base[at] + fine

    loop(count, 1, body)


class Packed:
    def __init__(self, count, pad, rows, width, groups):
        self.count, self.pad, self.rows, self.width, self.groups = count, pad, rows, width, groups

    def ext(self):
        return pltpu.VMEM((self.count + 2 * self.pad, 8, LANES), F32)

    def own(self, more=0):
        return pltpu.VMEM((self.count + more, 8, LANES), F32)


def packed_near(p, v):
    row = iota(v.shape, 1) & (p.rows - 1)
    after, before = pltpu.roll(v, 7, 1), pltpu.roll(v, 1, 1)
    return (
        jnp.where(row == p.rows - 1, pltpu.roll(after, LANES - p.width, 2), after),
        jnp.where(row == 0, pltpu.roll(before, p.width, 2), before),
        pltpu.roll(v, LANES - 1, 2),
        pltpu.roll(v, 1, 2),
    )


def packed_setup(p, c, w, wx, g, d, scale):
    def body(k):
        at = pl.ds(p.pad + k, 1)
        mid = c[at]
        lane, row = iota(mid.shape, 2), iota(mid.shape, 1) & (p.rows - 1)
        valid = lane < p.width * p.groups
        z = lane & (p.width - 1)
        inside = (
            (row < p.rows - 1) | (lane < p.width * (p.groups - 1)),
            (row > 0) | (lane >= p.width),
            z < p.width - 1,
            z > 0,
        )
        below = c[pl.ds(p.pad + k - 1, 1)]
        total = 6.0 * mid + below + c[pl.ds(p.pad + k + 1, 1)]
        wx[pl.ds(k, 1)] = mid + below
        for ref, near, ok in zip(w, packed_near(p, mid), inside):
            near = jnp.where(valid & ok, near, 0.0)
            ref[pl.ds(k, 1)] = jnp.where(valid & ok, mid + near, 0.0)
            total = total + near
        g[pl.ds(k, 1)] = jnp.where(valid, scale / jnp.where(valid, total, 1.0), 0.0)
        d[pl.ds(k, 1)] = total

    loop_pieces(p.count, 4, body)
    wx[pl.ds(p.count, 1)] = c[pl.ds(p.pad + p.count - 1, 1)]


def packed_couple(p, v_ref, w, wx, k):
    v = v_ref[pl.ds(p.pad + k, 1)]
    t = wx[pl.ds(k, 1)] * v_ref[pl.ds(p.pad + k - 1, 1)]
    t = t + wx[pl.ds(k + 1, 1)] * v_ref[pl.ds(p.pad + k + 1, 1)]
    parts = [ref[pl.ds(k, 1)] * near for ref, near in zip(w, packed_near(p, v))]
    return v, t + ((parts[0] + parts[1]) + (parts[2] + parts[3]))


def loop_pieces(count, chunk, body):
    def several(k):
        for i in range(chunk):
            body(k + i)

    loop(count, chunk, several)


def packed_sweep(p, src, dst, w, wx, g, b, b_pad):
    def body(k):
        v, t = packed_couple(p, src, w, wx, k)
        new = (1.0 - RELAX) * v + g[pl.ds(k, 1)] * (t + b[pl.ds(b_pad + k, 1)])
        dst[pl.ds(p.pad + k, 1)] = new

    loop_pieces(p.count, p.count, body)


def packed_halve(s, weight):
    row, col = iota((LANES, LANES), 0), iota((LANES, LANES), 1)
    m = jnp.where(lax.shift_right_logical(row, 1) == col, weight, 0.0).astype(F32)
    a = s[:, pl.ds(0, 8, stride=2), :] + s[:, pl.ds(1, 8, stride=2), :]
    return dot(a.reshape(s.shape[0] * 8, LANES), m).reshape(s.shape[0], 8, LANES)


class Bundle:
    def __init__(self, pairs, target, sends, receives, tiles, unit, sems):
        send_sem, recv_sem, index = sems

        def copy(src, dst):
            return pltpu.make_async_remote_copy(
                src_ref=src,
                dst_ref=dst,
                send_sem=send_sem.at[index],
                recv_sem=recv_sem.at[index],
                device_id=target,
                device_id_type=MESH,
            )

        self.copies = [copy(src, dst) for src, dst in pairs]
        whole = unit.at[pl.ds(0, tiles)]
        self.whole = self.copies[0] if len(pairs) == 1 else copy(whole, whole)
        self.sends, self.receives = sends, receives

    def start(self):
        def go():
            for copy in self.copies:
                copy.start()

        pl.when(self.sends)(go)

    def arrive(self):
        pl.when(self.receives)(lambda: self.whole.wait_recv())

    def leave(self):
        pl.when(self.sends)(lambda: self.whole.wait_send())


def kernel(nx, ny, levels, guess, rhs, coef, out, *scratch):
    l0, l1, l2, l3, l4 = levels
    names = iter(scratch)
    take = lambda k: [next(names) for _ in range(k)]
    va0, vb0, vc0, c0, b0, g0, d0, ve0, vf0, s0, pe0 = take(11)
    va1, vb1, vc1, c1, b1, g1, d1, s1, pe1 = take(9)
    va2, vb2, vc2, c2, b2, g2, d2, s2, pe2 = take(9)
    va3, vb3, c3, b3, wx3, g3, d3, s3, t3 = take(9)
    w3 = take(4)
    va4, vb4, c4, wx4, q4, d4, res4, e4 = take(8)
    w4 = take(4)
    pc, pb, unit = take(3)
    send_sem, recv_sem, gather_send, gather_recv, local_sem = take(5)

    gx, gy = lax.axis_index("gx"), lax.axis_index("gy")
    counter = iter(range(1000))

    def sems(again=None):
        return send_sem, recv_sem, next(counter if again is None else again)

    loads = []
    for i, (src, dst) in enumerate(((coef, c0), (guess, va0), (rhs, b0))):
        for h in range(2):
            loads.append(
                pltpu.make_async_copy(
                    src.at[:, :, h * LANES : (h + 1) * LANES],
                    dst.at[l0.halo : l0.halo + l0.bx, h, 8 : 8 + l0.by, :],
                    local_sem.at[2 * i + h],
                )
            )
    for copy in loads:
        copy.start()

    barrier = pltpu.get_barrier_semaphore()
    for k in range(1, nx):
        pl.semaphore_signal(
            barrier, inc=1, device_id=(lax.rem(gx + k, nx), gy), device_id_type=MESH
        )
    for k in range(1, ny):
        pl.semaphore_signal(
            barrier, inc=1, device_id=(gx, lax.rem(gy + k, ny)), device_id_type=MESH
        )

    for dx in (1, nx - 1):
        for dy in (1, ny - 1):
            diagonal = (lax.rem(gx + dx, nx), lax.rem(gy + dy, ny))
            pl.semaphore_signal(barrier, inc=1, device_id=diagonal, device_id_type=MESH)

    everything = []

    class Exchange:
        def __init__(self, *parts, reach=1, direct=False, after=None):
            self.direct = direct
            again = None if after is None else iter(after.indices)
            self.indices = []
            on_x, on_y = (lambda p: (p >= 0) & (p < nx)), (lambda p: (p >= 0) & (p < ny))

            def layers(level, sign, a, b):
                lo, bx = level.halo, level.bx
                if sign > 0:
                    return lo + reach * bx - b, lo - b, b - a + 1
                return lo + a - 1 - (reach - 1) * bx, lo + bx + a - 1, b - a + 1

            def bundle(pairs, target, sends, receives):
                total = sum(math.prod(dst.shape) for _, dst in pairs) // (8 * LANES)
                chosen = sems(again)
                self.indices.append(chosen[2])
                return Bundle(pairs, target, sends, receives, total, unit, chosen)

            self.x, self.y, self.corners = [], [], []
            for sign in (1, -1):
                there, back = gx + sign * reach, gx - sign * reach
                pairs = []
                for level, src, dst, a, b, faces, corner in parts:
                    at, to, count = layers(level, sign, a, b)
                    own = pl.ds(8, level.by)
                    pairs.append(
                        (src.at[pl.ds(at, count), :, own, :], dst.at[pl.ds(to, count), :, own, :])
                    )
                self.x.append(bundle(pairs, (there, gy), on_x(there), on_x(back)))
            for sign in (1, -1):
                there, back = gy + sign, gy - sign
                pairs, corner_pairs = [], ([], [])
                for level, src, dst, a, b, faces, corner in parts:
                    deep = 4 if level.nh == 2 else 8
                    row = 8 + level.by - deep if sign > 0 else 8
                    to_row = 8 - deep if sign > 0 else 8 + level.by

                    def strips(ref, at, to, count):
                        return (
                            ref.at[pl.ds(at, count), :, pl.ds(row, deep), :],
                            dst.at[pl.ds(to, count), :, pl.ds(to_row, deep), :],
                        )

                    if faces:
                        pairs.append(strips(src, level.halo, level.halo, level.bx))
                    if corner:
                        for i, sign_x in enumerate((1, -1)):
                            at, to, count = layers(level, sign_x, *corner)
                            corner_pairs[i].append(strips(src if direct else dst, at if direct else to, to, count))
                if pairs:
                    self.y.append(bundle(pairs, (gx, there), on_y(there), on_y(back)))
                for i, sign_x in enumerate((1, -1)):
                    if corner_pairs[i]:
                        far, near = gx + sign_x * reach, gx - sign_x * reach
                        self.corners.append(
                            bundle(
                                corner_pairs[i],
                                (far if direct else gx, there),
                                on_y(there) & on_x(far if direct else near),
                                on_y(back) & on_x(near),
                            )
                        )
            everything.append(self)

        def send(self):
            for copies in self.x + self.y + (self.corners if self.direct else []):
                copies.start()

        def rows(self):
            for copies in self.y:
                copies.arrive()

        def forward(self):
            for copies in self.x:
                copies.arrive()
            for copies in self.corners:
                copies.arrive() if self.direct else copies.start()

        def finish(self):
            self.rows()
            self.last()

        def last(self):
            for copies in [] if self.direct else self.corners:
                copies.arrive()

        def leave(self):
            everything.remove(self)
            for copies in self.x + self.y + self.corners:
                copies.leave()

    class Gather:
        def __init__(self, rows, full, pad, index):
            self.rows, self.full, self.at = rows, full, pl.ds(pad + 2 * gx, 2)
            self.first = [
                self.copy(rows.at[gy], index, (gx, lax.rem(gy + k, ny))) for k in range(1, ny)
            ]
            mine = full.at[self.at]
            self.second = [
                self.copy(mine, index + 1, (lax.rem(gx + k, nx), gy)) for k in range(1, nx)
            ]
            self.first_all = self.copy(rows.at[pl.ds(0, ny - 1)], index, (gx, gy))
            self.second_all = self.copy(full.at[pl.ds(0, 2 * nx - 2)], index + 1, (gx, gy))

        def copy(self, ref, index, target):
            return pltpu.make_async_remote_copy(
                src_ref=ref,
                dst_ref=ref,
                send_sem=gather_send.at[index],
                recv_sem=gather_recv.at[index],
                device_id=target,
                device_id_type=MESH,
            )

        def send(self, tile):
            self.rows[gy] = tile
            for copy in self.first:
                copy.start()

        def forward(self):
            self.first_all.wait_recv()
            even, odd = self.rows[0], self.rows[1]
            for k in range(2, ny, 2):
                even, odd = even + self.rows[k], odd + self.rows[k + 1]
            low = iota(even.shape, 0) < 4
            layers = (
                jnp.where(low, even, pltpu.roll(odd, 4, 0)),
                jnp.where(low, pltpu.roll(even, 4, 0), odd),
            )
            for i in range(2):
                self.full[self.at.start + i] = layers[i]
            for copy in self.second:
                copy.start()

        def finish(self):
            self.second_all.wait_recv()

        def leave(self):
            self.first_all.wait_send()
            self.second_all.wait_send()

    x_0 = Exchange(
        (l0, c0, c0, 1, 2, True, (1, 1)),
        (l0, va0, va0, 1, 2, True, (1, 1)),
        (l0, b0, b0, 1, 1, True, None),
        direct=True,
    )
    x_v = Exchange((l0, ve0, ve0, 1, 2, True, (1, 1)), direct=True)
    x_late = Exchange((l0, c0, c0, 3, 3, False, (2, 3)), (l0, b0, b0, 2, 2, False, (1, 2)))
    x_k0 = Exchange((l0, vf0, vc0, 1, 3, True, (1, 3)))
    x_c = Exchange((l1, c1, c1, 1, 5, True, (1, 5)), (l2, c2, c2, 1, 4, True, (1, 4)))
    f_c = Exchange((l2, c2, c2, 5, 6, False, (5, 6)), reach=2)
    x_b1 = Exchange((l1, b1, b1, 1, 4, True, (1, 4)), direct=True, after=x_0)
    x_b2 = Exchange((l2, b2, b2, 1, 4, True, (1, 4)), direct=True, after=x_v)
    x_k = Exchange((l1, vc1, vc1, 1, 5, True, (1, 5)), (l2, vc2, vc2, 1, 4, True, (1, 4)),
        after=x_c,
    )
    f_k = Exchange(
        (l2, b2, b2, 5, 6, False, (5, 6)), (l2, vc2, vc2, 5, 6, False, (5, 6)), reach=2, after=f_c
    )
    g_c3, g_b3 = Gather(pc, c3, l3.pad, 0), Gather(pb, b3, l3.pad, 2)

    for copy in loads:
        copy.wait()
    pl.semaphore_wait(barrier, nx + ny + 2)


    def double(k):
        for h in range(2):
            own = (pl.ds(l0.halo + k, 1), h, pl.ds(8, l0.by), slice(None))
            b0[own] = 2.0 * b0[own]

    loop_pieces(l0.bx, 4, double)
    x_0.send()

    def clear(level, refs, far):
        lo, bx, by = level.halo, level.bx, level.by

        def layers(start, count):
            for ref in refs:
                ref[pl.ds(start, count)] = jnp.zeros((count,) + ref.shape[1:], F32)

        near = min(lo, bx)
        pl.when(gx == 0)(lambda: layers(lo - near, near))
        pl.when(gx == nx - 1)(lambda: layers(lo + bx, near))
        if far:
            pl.when(gx < 2)(lambda: layers(0, lo - bx))
            pl.when(gx >= nx - 2)(lambda: layers(lo + 2 * bx, lo - bx))

        def rows(start, count):
            for ref in refs:
                for h in range(level.nh):
                    ref[:, h, pl.ds(start, count), :] = jnp.zeros((level.width, count, LANES), F32)

        pl.when(gy == 0)(lambda: rows(0, 8))
        pl.when(gy == ny - 1)(lambda: rows(8 + by, 8))

    clear(l0, (va0, c0, b0, vc0, ve0), False)
    clear(l1, (c1, b1, vc1), False)
    clear(l2, (c2, b2, vc2), True)
    for ref in (va3, vb3, c3, va4, vb4, c4):
        pad = 1 if ref.shape[0] == nx + 2 else l3.pad
        for start in (0, ref.shape[0] - pad):
            ref[pl.ds(start, pad)] = jnp.zeros((pad, 8, LANES), F32)
    for ref in (va1, vb1, va2, vb2):
        for h in range(ref.shape[1]):
            for r in range(0, ref.shape[2], 8):
                ref[:, h, pl.ds(r, 8), :] = jnp.zeros((ref.shape[0], 8, LANES), F32)

    lane_base = 32 * lax.shift_right_logical(gy, 1)

    def tile_of(s, weight):
        row, col = iota((LANES, LANES), 0), iota((LANES, LANES), 1)
        pick = (lax.shift_right_logical(row, 1) + lane_base == col) & (row < l2.nz)
        m = jnp.where(pick, weight, 0.0).astype(F32)
        a = s[pl.ds(0, 8, stride=2), :] + s[pl.ds(1, 8, stride=2), :]
        return dot(a, m)

    field_pairs(l0, c0, s0)
    c1[l1.halo : l1.halo + l1.bx, 0, 8 : 8 + l1.by, :] = halve(l0, s0, 0.125)
    field_pairs(l1, c1, s1)
    c2[l2.halo : l2.halo + l2.bx, 0, 8 : 8 + l2.by, :] = halve(l1, s1, 0.125)
    x_c.send()
    f_c.send()
    for k in range(2):
        s2[pl.ds(8 * k, 8), :] = (
            c2[l2.halo + 2 * k, 0, pl.ds(8, 8), :] + c2[l2.halo + 2 * k + 1, 0, pl.ds(8, 8), :]
        )
    g_c3.send(tile_of(s2, 0.125))

    bx0, by0 = gx * l0.bx, gy * l0.by
    chain, bx = (va0, vb0, ve0, vf0), l0.bx
    inner, outer, own, whole = tiles(12, 24), ((4, 8), (36, 8)), tiles(8, 32), tiles(4, 40)

    def prepare(span, rows):
        setup(l0, c0, g0, d0, span, rows, bx0, by0)

    def relax(k, span, rows):
        sweep(l0, chain[k - 1], chain[k], c0, g0, b0, span, rows)

    def rest(span):
        residual_pairs(l0, vf0, c0, b0, d0, s0, vc0, span)

    edges = (((-1, 0), own), ((0, 1), whole), ((bx - 1, bx), whole), ((bx, bx + 1), own))
    prepare((1, bx - 1), inner)
    relax(1, (1, bx - 1), inner)
    relax(2, (2, bx - 2), inner)
    x_0.rows()
    prepare((1, bx - 1), outer)
    relax(1, (1, bx - 1), outer)
    relax(2, (2, bx - 2), ((8, 8), (32, 8)))
    x_0.forward()
    for span, rows in edges:
        prepare(span, rows)
        relax(1, span, rows)
    for span in ((0, 2), (bx - 2, bx)):
        relax(2, span, own)
    x_v.send()
    x_late.send()
    relax(3, (1, bx - 1), inner)
    g_c3.forward()
    x_c.forward()
    f_c.forward()
    x_v.rows()
    relax(3, (1, bx - 1), outer)
    rest((1, bx // 2 - 1))
    x_v.forward()
    for span, rows in edges:
        relax(3, span, rows)
    for span in ((0, 1), (bx // 2 - 1, bx // 2)):
        rest(span)
    b1[l1.halo : l1.halo + l1.bx, 0, 8 : 8 + l1.by, :] = halve(l0, s0, 0.5)
    x_0.leave()
    x_b1.send()
    x_late.forward()
    x_c.finish()
    f_c.finish()
    rows1, rows2 = tiles(4, 24, 24), tiles(2, 24, 24)
    setup(l1, c1, g1, d1, (-4, l1.bx + 4), rows1, gx * l1.bx, gy * l1.by)
    setup(l2, c2, g2, d2, (-5, l2.bx + 5), rows2, gx * l2.bx, gy * l2.by)
    x_b1.forward()
    x_b1.finish()
    first_sweep(l1, va1, g1, b1, (-3, l1.bx + 3), rows1)
    sweep(l1, va1, vb1, c1, g1, b1, (-2, l1.bx + 2), rows1)
    sweep(l1, vb1, va1, c1, g1, b1, (-1, l1.bx + 1), rows1)
    residual_pairs(l1, va1, c1, b1, d1, s1, vc1)
    b2[l2.halo : l2.halo + l2.bx, 0, 8 : 8 + l2.by, :] = halve(l1, s1, 0.5)
    x_v.leave()
    x_b2.send()

    def pairs_of(ref):
        for k in range(nx):
            total = ref[l3.pad + 2 * k] + ref[l3.pad + 2 * k + 1]
            s3[k, pl.ds(0, 8), :] = total
            s3[k, pl.ds(8, 8), :] = total

    g_c3.finish()
    packed_setup(l3, c3, w3, wx3, g3, d3, RELAX)
    pairs_of(c3)
    c4[pl.ds(l4.pad, nx)] = packed_halve(s3, 0.125)
    packed_setup(l4, c4, w4, wx4, q4, d4, 1.0)

    x_b2.forward()
    x_b2.finish()
    x_k0.send()
    first_sweep(l2, va2, g2, b2, (-3, l2.bx + 3), rows2)
    sweep(l2, va2, vb2, c2, g2, b2, (-2, l2.bx + 2), rows2)
    sweep(l2, vb2, va2, c2, g2, b2, (-1, l2.bx + 1), rows2)
    for k in range(2):
        total = None
        for x0 in (l2.halo + 2 * k, l2.halo + 2 * k + 1):
            v, t = couple(l2, va2, c2, x0, 8, 8)
            part = block(b2, x0, 8, 8) + t - block(d2, x0, 8, 8) * v
            vc2[pl.ds(x0, 1), :, pl.ds(8, 8), :] = v
            total = part if total is None else total + part
        s2[pl.ds(8 * k, 8), :] = total[0, 0]
    g_b3.send(tile_of(s2, 0.5))
    x_c.leave()
    f_c.leave()
    x_k.send()
    f_k.send()
    g_b3.forward()
    x_late.finish()
    for span in ((-2, 0), (bx, bx + 2)):
        prepare(span, whole)
    x_k.forward()
    f_k.forward()
    g_b3.finish()
    for k in range(l3.count):
        va3[l3.pad + k] = g3[k] * b3[l3.pad + k]
    packed_sweep(l3, va3, vb3, w3, wx3, g3, b3, l3.pad)
    packed_sweep(l3, vb3, va3, w3, wx3, g3, b3, l3.pad)

    def residual3(k):
        total = None
        for i in (2 * k, 2 * k + 1):
            v, t = packed_couple(l3, va3, w3, wx3, i)
            r = b3[pl.ds(l3.pad + i, 1)] + t - d3[pl.ds(i, 1)] * v
            total = r if total is None else total + r
        s3[pl.ds(k, 1), pl.ds(0, 8), :] = total
        s3[pl.ds(k, 1), pl.ds(8, 8), :] = total

    loop_pieces(nx, 2, residual3)
    res4[...] = packed_halve(s3, 0.5)

    x_k0.forward()
    sigma = THETA / DELTA
    rho = 1.0 / sigma
    for k in range(nx):
        direction = res4[k] * q4[k] * (1.0 / THETA)
        e4[k] = direction
        va4[l4.pad + k] = direction
    src, dst = va4, vb4
    for step in range(CHEB - 1):
        rho_new = 1.0 / (2.0 * sigma - rho)
        for k in range(nx):
            at = pl.ds(k, 1)
            v, t = packed_couple(l4, src, w4, wx4, k)
            r = res4[at] - (d4[at] * v - t)
            direction = (rho_new * rho) * v + (2.0 * rho_new / DELTA) * (r * q4[at])
            res4[at] = r
            e4[at] = e4[at] + direction
            dst[pl.ds(l4.pad + k, 1)] = direction
        rho = rho_new
        src, dst = dst, src

    row, col = iota((LANES, LANES), 0), iota((LANES, LANES), 1)
    spread = jnp.where(row == lax.shift_right_logical(col, 1), 1.0, 0.0).astype(F32)
    fine = dot(e4[...].reshape(nx * 8, LANES), spread).reshape(nx, 8, LANES)
    for dr in range(2):
        t3[:, pl.ds(dr, 4, stride=2), :] = fine[:, 0:4, :]
    for k in range(l3.count):
        vb3[l3.pad + k] = va3[l3.pad + k] + t3[k // 2]
    packed_sweep(l3, vb3, va3, w3, wx3, g3, b3, l3.pad)
    packed_sweep(l3, va3, vb3, w3, wx3, g3, b3, l3.pad)
    packed_sweep(l3, vb3, va3, w3, wx3, g3, b3, l3.pad)

    f_k.finish()
    x_k.finish()
    group = lax.shift_right_logical(gy, 1) - 1
    e3 = va3[pl.ds(l3.pad - 3 + 2 * gx, 8)].reshape(64, LANES)
    for q in range(3):
        pick = (row == lax.shift_right_logical(col, 1) + 32 * (group + q)) & (col < l2.nz)
        part = dot(e3, jnp.where(pick, 1.0, 0.0).astype(F32))
        pe2[:, 0, pl.ds(8 * q, 8), :] = part.reshape(8, 8, LANES)
    add_prolonged(l2, pe2, vc2, va2, 0, 0, 8, 16, 4 * (gy & 1) + 4)
    sweep(l2, va2, vb2, c2, g2, b2, (-5, l2.bx + 5), rows2)
    sweep(l2, vb2, va2, c2, g2, b2, (-4, l2.bx + 4), rows2)
    sweep(l2, va2, vb2, c2, g2, b2, (-3, l2.bx + 3), rows2)

    prolong(l1, vb2, 3, 4, 10, 16, pe1, None, None, 0)
    add_prolonged(l1, pe1, vc1, va1, 0, 0, 10, 16)
    sweep(l1, va1, vb1, c1, g1, b1, (-4, l1.bx + 4), rows1)
    sweep(l1, vb1, va1, c1, g1, b1, (-3, l1.bx + 3), rows1)
    sweep(l1, va1, vb1, c1, g1, b1, (-2, l1.bx + 2), rows1)

    x_k0.finish()
    prolong(l0, vb1, 4, 4, 12, 24, pe0, None, None, 0)
    add_prolonged(l0, pe0, vc0, va0, 0, 0, 12, 24)
    def put(x0, r, n, new):
        for h in range(2):
            at = (pl.ds(x0 - l0.halo, 1), pl.ds(r - 8, n), slice(h * LANES, (h + 1) * LANES))
            out[at] = new[:, h]

    sweep(l0, va0, vb0, c0, g0, b0, (-2, l0.bx + 2), tiles(4, 40))
    sweep(l0, vb0, ve0, c0, g0, b0, (-1, l0.bx + 1), tiles(4, 40))
    sweep(l0, ve0, None, c0, g0, b0, (0, l0.bx), tiles(8, 32), put)
    for exchange in list(everything):
        exchange.leave()
    g_c3.leave()
    g_b3.leave()


def solution(mesh):
    nx, ny = mesh.shape["gx"], mesh.shape["gy"]
    l0 = Level(2, 256, 4, 16, 32, 48, 16 * nx, 32 * ny)
    l1 = Level(1, 128, 6, 8, 16, 32, 8 * nx, 16 * ny)
    l2 = Level(1, 64, 6, 4, 8, 32, 4 * nx, 8 * ny)
    l3 = Packed(2 * nx, 4, 8, 32, ny // 2)
    l4 = Packed(nx, 1, 4, 16, ny // 2)

    def vmem(*shape):
        return pltpu.VMEM(shape, F32)

    e, o = (lambda l: l.ext()), (lambda l: l.own())
    scratch = [e(l0)] * 9 + [vmem(8, 2, 32, LANES), vmem(12, 2, 24, LANES)]
    scratch += [e(l1)] * 7 + [vmem(4, 1, 16, LANES), vmem(10, 1, 16, LANES)]
    scratch += [e(l2)] * 7 + [vmem(16, LANES), vmem(8, 1, 24, LANES)]
    scratch += [e(l3)] * 4 + [l3.own(1), o(l3), o(l3), vmem(nx, 16, LANES), vmem(nx, 8, LANES)]
    scratch += [o(l3)] * 4
    scratch += [e(l4)] * 3 + [l4.own(1)] + [o(l4)] * 8
    scratch += [vmem(ny, 8, LANES)] * 2 + [vmem(64, 8, LANES)]
    copies = 4 * 8 + 2 * 6
    scratch += [
        pltpu.SemaphoreType.DMA((copies,)),
        pltpu.SemaphoreType.DMA((copies,)),
        pltpu.SemaphoreType.DMA((4,)),
        pltpu.SemaphoreType.DMA((4,)),
        pltpu.SemaphoreType.DMA((8,)),
    ]

    def step(guess, right_side, coefficient):
        return pl.pallas_call(
            functools.partial(kernel, nx, ny, (l0, l1, l2, l3, l4)),
            out_shape=pltpu.VMEM(guess.shape, F32),
            in_specs=[pl.BlockSpec(memory_space=pl.ANY)] * 3,
            out_specs=pl.BlockSpec(memory_space=pltpu.VMEM),
            scratch_shapes=scratch,
            compiler_params=pltpu.CompilerParams(collective_id=0, has_side_effects=True),
        )(guess, right_side, coefficient)

    spec = P("gx", "gy", None)
    return jax.shard_map(
        step, mesh=mesh, in_specs=(spec, spec, spec), out_specs=spec, check_vma=False
    )
```
